128 devices in a mesh: space: 16 (over y, z_hi, core), band: 8 (over x, z_lo).
Axes of the slice: x: 4, y: 4, z: 4 (z_hi: 2, z_lo: 2; z = z_hi * 2 + z_lo), core: 2. Of those that a mesh axis runs over, the one named last changes fastest.
Arguments:
- states: bfloat16 [165888, 1024], P('space', 'band'), may hold values from -12 to 12, as said below
- potential: float32 [165888], P('space'), may hold values from 0 to 2, as said below
- cell_matrix: bfloat16 [512, 512], replicated, may hold values from -1 to 1, as said below
- cell_scale: float32 [400], P('space'), may hold values from 0.5 to 1.5
- connectivity: int32 [400, 512], P('space'), may hold values from 0 to 10367, as said below
- lower_bound: float32 [1], replicated, may hold values from 0.4 to 0.8
- upper_bound: float32 [1], replicated, may hold values from 16 to 20
Outputs:
- filtered: bfloat16 [165888, 1024], P('space', 'band')
- projected: float32 [1024, 1024], P('band', 'space')
The draws below stay inside these ranges and needn't reach their ends.
Inputs may be any that keep to these rules, and one draw needn't show every extreme that they name: `connectivity`: each slab is a block of 5 x 5 x 1 hexahedral cells with 8 nodes along each edge, slabs stacked along the third dimension. Cell c of a slab is the cell at position (c % 5, (c // 5) % 5, c // 25), and its entry j is its node at corner offset (j % 8, (j // 8) % 8, j // 64). Nodes shared by cells get the same row. The nodes of node plane k along the third dimension have rows k * 1296 to (k + 1) * 1296 - 1 of the slab, in an order of their own. `states`: the copies of a node on a face shared by two slabs carry equal values. `potential`: the copies of a node on a face shared by two slabs carry equal values. `cell_matrix`: symmetric positive definite.
All inputs are finite; a program needn't handle non-finite values.
Results may differ from the reference program's by a relative error of at most 0.012.
The reference program's roundings to bfloat16 on the way count: a program that leaves them out, or rounds other values in their place, can miss the bound.
Values may be sent and summed in bfloat16 or wider, within the bound.
No kernel may reach another device: no remote copies, remote signals or barrier semaphores. Data moves between devices by JAX's collectives and lax.ppermute only.
A program may use at most 128 MiB of HBM per device.

```python
import math
import jax
import jax.numpy as jnp
from jax import lax

EDGE = 8
STATES = 1024
SLAB_XY = 5
STEPS = 4
CELL_NODES = 512
FACE = 1296
LAYERS = 8
NODES_DEV = 10368
CELLS_DEV = 25
NODES = 165888
CELLS = 400
GLOBAL_NODES = 146448
N_SPACE = 16


def node_numbers(key):
    slab_count = NODES // NODES_DEV
    subkeys = jax.random.split(jax.random.fold_in(key, 4242), slab_count * LAYERS)
    within = jax.vmap(lambda subkey: jax.random.permutation(subkey, FACE))(subkeys).astype(jnp.int32)
    within = within.reshape(slab_count, LAYERS, FACE)
    planes = jnp.arange(LAYERS, dtype=jnp.int32)[None, :, None] * FACE
    return (planes + within).reshape(slab_count, NODES_DEV).astype(jnp.int32)


def face_lists(numbers):
    across = jnp.arange(FACE, dtype=jnp.int32)
    lower_ids = numbers[:, across]
    upper_ids = numbers[:, (LAYERS - 1) * FACE + across]
    return (lower_ids, upper_ids)


def pick_rows_drawn(slab_rows, face_ids):
    return slab_rows[face_ids]


def put_rows(slab_rows, face_ids, fresh_rows):
    return slab_rows.at[face_ids].set(fresh_rows)


def share_faces(values, numbers):
    lower_ids, upper_ids = face_lists(numbers)
    upper_rows = jax.vmap(pick_rows_drawn)(values, upper_ids)
    first_rows = jax.vmap(pick_rows_drawn)(values[:1], lower_ids[:1])
    source = jnp.concatenate([first_rows, upper_rows[:-1]], axis=0)
    return jax.vmap(put_rows)(values, lower_ids, source)


def draw_connectivity(key, part):
    numbers = node_numbers(key)
    side_nodes = (EDGE - 1) * SLAB_XY + 1
    corner = jnp.arange(EDGE, dtype=jnp.int32)
    cell_ids = jnp.arange(CELLS_DEV, dtype=jnp.int32)
    cell_x = cell_ids % SLAB_XY
    cell_y = cell_ids // SLAB_XY % SLAB_XY
    cell_z = cell_ids // (SLAB_XY * SLAB_XY)
    index_x = cell_x[:, None, None, None] * (EDGE - 1) + corner[None, None, None, :]
    index_y = cell_y[:, None, None, None] * (EDGE - 1) + corner[None, None, :, None]
    index_z = cell_z[:, None, None, None] * (EDGE - 1) + corner[None, :, None, None]
    drawn_rows = ((index_z * side_nodes + index_y) * side_nodes + index_x).reshape(CELLS_DEV, CELL_NODES)
    return numbers[:, drawn_rows].reshape(CELLS, CELL_NODES).astype(jnp.int32)


def draw_states(key, part):
    numbers = node_numbers(key)
    slab_count = NODES // NODES_DEV
    shape = (slab_count, NODES_DEV, STATES)
    plane = (jnp.arange(NODES_DEV, dtype=jnp.int32) // FACE).astype(jnp.float32) / (LAYERS - 1)
    rising = 0.4 * jnp.exp(jnp.log(6.0) * plane)
    values = jnp.clip(rising[None, :, None] * jax.random.normal(jax.random.fold_in(key, 11), shape, jnp.float32), -12.0, 12.0)
    values = share_faces(values, numbers)
    return values.reshape(NODES, STATES).astype(jnp.bfloat16)


def draw_potential(key, part):
    numbers = node_numbers(key)
    slab_count = NODES // NODES_DEV
    uniform_part = jax.random.uniform(jax.random.fold_in(key, 21), (slab_count, NODES_DEV, 1), jnp.float32, 0.0, 1.0)
    values = 2.0 * uniform_part
    values = share_faces(values, numbers)
    return values.reshape(NODES).astype(jnp.float32)


def draw_cell_matrix(key, part):
    factor = jax.random.normal(jax.random.fold_in(key, 32), (CELL_NODES, CELL_NODES), jnp.float32)
    gram = jnp.dot(factor, factor.T, precision=lax.Precision.HIGHEST) / (4.0 * CELL_NODES)
    return (gram + 0.1 * jnp.eye(CELL_NODES, dtype=jnp.float32)).astype(jnp.bfloat16)


def block_levels(rng, shape, shards, smallest, largest):
    factor_of = 1.0
    for position, parts in shards:
        heights = jax.random.uniform(jax.random.fold_in(jax.random.fold_in(rng, 6), position), (parts,), jnp.float32, smallest / len(shards), largest / len(shards))
        factor_of = factor_of * jnp.repeat(jnp.exp(heights), shape[position] // parts).reshape((-1,) + (1,) * (len(shape) - 1 - position))
    return factor_of


def setup_inputs(seed: int = 0) -> dict:
    seeds = jax.random.split(jax.random.key(seed), 8)
    return {
        "states": draw_states(jax.random.fold_in(seeds[7], 71), 0),
        "potential": draw_potential(jax.random.fold_in(seeds[7], 71), 0),
        "cell_matrix": draw_cell_matrix(jax.random.fold_in(seeds[7], 71), 0),
        "cell_scale": jnp.clip(jnp.exp(math.log(1.5) - 1.0986123 * jax.random.uniform(seeds[3], (CELLS,), jnp.float32) ** block_levels(seeds[3], (CELLS,), ((0, 16),), -0.2, 0.2)), 0.5, 1.5),
        "connectivity": draw_connectivity(jax.random.fold_in(seeds[7], 71), 0),
        "lower_bound": jnp.clip(jax.random.uniform(seeds[5], (1,), jnp.float32, 0.4, 0.8), 0.4, 0.8),
        "upper_bound": jnp.clip(jax.random.uniform(seeds[6], (1,), jnp.float32, 16.0, 20.0), 16.0, 20.0),
    }


def settle(values):
    return lax.optimization_barrier(values.astype(jnp.bfloat16))


def plain_index():
    side_nodes = (EDGE - 1) * SLAB_XY + 1
    corner = jnp.arange(EDGE, dtype=jnp.int32)
    cell_ids = jnp.arange(CELLS_DEV, dtype=jnp.int32)
    cell_x = cell_ids % SLAB_XY
    cell_y = (cell_ids // SLAB_XY) % SLAB_XY
    cell_z = cell_ids // (SLAB_XY * SLAB_XY)
    index_x = cell_x[:, None, None, None] * (EDGE - 1) + corner[None, None, None, :]
    index_y = cell_y[:, None, None, None] * (EDGE - 1) + corner[None, None, :, None]
    index_z = cell_z[:, None, None, None] * (EDGE - 1) + corner[None, :, None, None]
    return ((index_z * side_nodes + index_y) * side_nodes + index_x).reshape(CELLS_DEV, CELL_NODES).astype(jnp.int32)


def plane_rows(connect_slab):
    plain = plain_index()
    return jnp.zeros((NODES_DEV,), jnp.int32).at[plain.reshape(-1)].set(connect_slab.reshape(-1).astype(jnp.int32))


def slab_terms(values, connect_rows, scale_rows, matrix):
    gathered = values.astype(jnp.float32)[connect_rows]
    products = jnp.einsum("ij,cjs->cis", matrix, gathered, precision=lax.Precision.HIGHEST)
    products = products * scale_rows[:, None, None]
    return jax.ops.segment_sum(products.reshape(-1, STATES), connect_rows.reshape(-1), num_segments=NODES_DEV)


def pick_rows(slab_rows, face_ids):
    return slab_rows[face_ids]


def add_faces(slab_rows, low_ids, up_ids, add_low, add_up):
    return slab_rows.at[low_ids].add(add_low).at[up_ids].add(add_up)


def operator(stack, potential_rows, connect_all, scale_all, matrix, lower_ids, upper_ids):
    local = lax.map(lambda packed: slab_terms(packed[0], packed[1], packed[2], matrix), (stack, connect_all, scale_all))
    from_lower_faces = jax.vmap(pick_rows)(local, lower_ids)
    from_upper_faces = jax.vmap(pick_rows)(local, upper_ids)
    zero_face = jnp.zeros_like(from_upper_faces[:1])
    from_below = jnp.concatenate([zero_face, from_upper_faces[:-1]], axis=0)
    from_above = jnp.concatenate([from_lower_faces[1:], zero_face], axis=0)
    local = jax.vmap(add_faces)(local, lower_ids, upper_ids, from_below, from_above)
    return local + potential_rows[:, :, None] * stack.astype(jnp.float32)


def set_weights(weight_row, low_ids, up_ids, low_w, up_w):
    return weight_row.at[low_ids].set(low_w).at[up_ids].set(up_w)


def reference(states, potential, cell_matrix, cell_scale, connectivity, lower_bound, upper_bound):
    matrix = cell_matrix.astype(jnp.float32)
    stack = states.reshape(N_SPACE, NODES_DEV, STATES)
    potential_rows = potential.reshape(N_SPACE, NODES_DEV)
    connect_all = connectivity.reshape(N_SPACE, CELLS_DEV, CELL_NODES)
    scale_all = cell_scale.reshape(N_SPACE, CELLS_DEV)
    ordered = jax.vmap(plane_rows)(connect_all)
    lower_ids = ordered[:, :FACE]
    upper_ids = ordered[:, NODES_DEV - FACE:]
    center = (lower_bound[0] + upper_bound[0]) * 0.5
    half_width = (upper_bound[0] - lower_bound[0]) * 0.5

    def apply_h(values):
        return operator(values, potential_rows, connect_all, scale_all, matrix, lower_ids, upper_ids)

    previous = stack
    current = settle((apply_h(previous) - center * previous.astype(jnp.float32)) / half_width)
    for repeat in range(STEPS - 1):
        following = settle(2.0 * ((apply_h(current) - center * current.astype(jnp.float32)) / half_width) - previous.astype(jnp.float32))
        previous, current = current, following
    image = settle(apply_h(current))
    slab_index = jnp.arange(N_SPACE)
    lower_weight = jnp.where(slab_index > 0, 0.5, 1.0).astype(jnp.float32)
    upper_weight = jnp.where(slab_index < N_SPACE - 1, 0.5, 1.0).astype(jnp.float32)
    weights = jnp.ones((N_SPACE, NODES_DEV), jnp.float32)
    weights = jax.vmap(set_weights)(weights, lower_ids, upper_ids, lower_weight, upper_weight)
    weighted = settle(image.astype(jnp.float32) * weights[:, :, None])
    flat_states = current.reshape(-1, STATES).astype(jnp.float32)
    flat_images = weighted.reshape(-1, STATES).astype(jnp.float32)
    totals = lax.dot_general(flat_states, flat_images, (((0,), (0,)), ((), ())), precision=lax.Precision.HIGHEST)
    return current.reshape(NODES, STATES), totals / GLOBAL_NODES
```

```python
import functools

import jax
import jax.numpy as jnp
from jax import lax
from jax.experimental import pallas as pl
from jax.experimental.pallas import tpu as pltpu
from jax.sharding import PartitionSpec as P

EDGE = 8
SLAB_XY = 5
STEPS = 4
CELLS = SLAB_XY * SLAB_XY
PAIRS = (CELLS + 1) // 2
CELL_NODES = EDGE**3
SIDE = (EDGE - 1) * SLAB_XY + 1
FACE = SIDE * SIDE
NODES = FACE * EDGE
COLS = 128
QUAD = EDGE * EDGE
THIRDS = 3
THIRD = FACE // THIRDS
F32 = jnp.float32
BF16 = jnp.bfloat16
VMEM = pl.BlockSpec(memory_space=pltpu.VMEM)
SMEM = pl.BlockSpec(memory_space=pltpu.SMEM)
BIG = pltpu.CompilerParams(vmem_limit_bytes=24 * 1024 * 1024)


def first_row(cell_y, cell_x, j):
    return (((EDGE - 1) * cell_y + j) * SIDE + (EDGE - 1) * cell_x) * EDGE


def gather_kernel(states_ref, pot_ref, index_ref, matrix_ref, field_ref, pot_out_ref, mat_ref, face_mat_ref,
                  rhs_ref, hot_ref, column_ref):
    for cell_y in range(SLAB_XY):
        five = index_ref[cell_y * SLAB_XY : (cell_y + 1) * SLAB_XY, :].astype(F32)
        five = jnp.concatenate([five, jnp.zeros((EDGE - SLAB_XY, CELL_NODES), F32)], axis=0)
        column_ref[cell_y * CELL_NODES : (cell_y + 1) * CELL_NODES, :EDGE] = jnp.transpose(five)
    pot = jnp.transpose(pot_ref[...])
    high = pot.astype(BF16)
    rest = pot - high.astype(F32)
    mid = rest.astype(BF16)
    low = (rest - mid.astype(F32)).astype(BF16)
    rhs_ref[:, COLS:] = jnp.concatenate(
        [high, mid, low, jnp.zeros((FACE, COLS - 3 * EDGE), BF16)], axis=1)

    new = lax.broadcasted_iota(jnp.int32, (CELL_NODES, CELL_NODES), 0)
    old = lax.broadcasted_iota(jnp.int32, (CELL_NODES, CELL_NODES), 1)
    order = jnp.where(old == (new % EDGE) * QUAD + new // EDGE, 1.0, 0.0).astype(BF16)
    across = (((1,), (1,)), ((), ()))
    turned = lax.dot_general(matrix_ref[...], order, across, preferred_element_type=F32).astype(BF16)
    face_mat_ref[:QUAD, :] = turned[:QUAD, :]
    face_mat_ref[QUAD:, :] = turned[CELL_NODES - QUAD :, :]
    mat_ref[...] = jnp.dot(order, turned, preferred_element_type=F32).astype(BF16)

    def step(i, _):
        plane = i // SLAB_XY
        cell_y = i % SLAB_XY

        @pl.when(cell_y == 0)
        def _():
            rhs_ref[:, :COLS] = states_ref[pl.ds(pl.multiple_of(plane * FACE, 16), FACE), :]

        lanes = lax.broadcasted_iota(jnp.int32, (QUAD, FACE), 1).astype(F32)
        shift = (plane * FACE).astype(F32)
        for cell_x in range(SLAB_XY):
            want = column_ref[pl.ds(pl.multiple_of(cell_y * CELL_NODES + plane * QUAD, 8), QUAD), cell_x : cell_x + 1] - shift
            hot_ref[cell_x * QUAD : (cell_x + 1) * QUAD, :] = jnp.where(want == lanes, 1.0, 0.0).astype(BF16)
        got = jnp.dot(hot_ref[...], rhs_ref[...], preferred_element_type=F32)
        lane = lax.broadcasted_iota(jnp.int32, (EDGE, COLS), 1)
        mine = (lane % EDGE == plane) & (lane < 3 * EDGE)
        for cell_x in range(SLAB_XY):
            for j in range(EDGE):
                at = cell_x * QUAD + j * EDGE
                rows = pl.ds(first_row(cell_y, cell_x, j) + plane, EDGE, stride=EDGE)
                field_ref[rows, :] = got[at : at + EDGE, :COLS]
                value = jnp.sum(jnp.where(mine, got[at : at + EDGE, COLS:], 0.0), axis=1, keepdims=True)
                pot_out_ref[rows, :] = jnp.broadcast_to(value, (EDGE, COLS))
        return 0

    lax.fori_loop(0, EDGE * SLAB_XY, step, 0)


def gather(states, potential, connectivity, matrix):
    return pl.pallas_call(
        gather_kernel,
        name="gather_states",
        out_shape=(
            pltpu.VMEM((NODES, COLS), F32),
            pltpu.VMEM((NODES, COLS), F32),
            pltpu.VMEM((CELL_NODES, CELL_NODES), BF16),
            pltpu.VMEM((2 * QUAD, CELL_NODES), BF16),
        ),
        in_specs=[VMEM] * 4,
        out_specs=(VMEM,) * 4,
        scratch_shapes=[
            pltpu.VMEM((FACE, 2 * COLS), BF16),
            pltpu.VMEM((SLAB_XY * QUAD, FACE), BF16),
            pltpu.VMEM((SLAB_XY * CELL_NODES, COLS), F32),
        ],
        compiler_params=BIG,
    )(states, potential.reshape(EDGE, FACE), connectivity, matrix)


def half_width_of(bounds):
    low, high = bounds
    return jnp.full((1, COLS), (high[0] - low[0]) * 0.5, F32)


def factors(bounds, stage):
    if stage > STEPS:
        return jnp.ones((1, COLS), F32), None
    low, high = bounds
    center = (high[0] + low[0]) * 0.5
    lead = (1.0 if stage == 1 else 2.0) / half_width_of(bounds)
    return lead, lead * center


def pair_cells(pair, scale_ref):
    for half in range(2):
        index = 2 * pair + half
        cell = jnp.minimum(index, CELLS - 1)
        yield half, cell // SLAB_XY, cell % SLAB_XY, jnp.where(index < CELLS, scale_ref[cell], 0.0)


def faces_kernel(stage, settle, emit, spread, *refs):
    refs = list(refs)
    field_ref = refs.pop(0)
    if settle:
        low_in, high_in = refs.pop(0), refs.pop(0)
    bounds = (refs.pop(0), refs.pop(0))
    weight_ref = refs.pop(0)
    if spread:
        face_mat_ref, scale_ref = refs.pop(0), refs.pop(0)
    if settle:
        out_ref = refs.pop(0)
    if emit:
        plain_ref = refs.pop(0)
    if spread:
        low_out, high_out, blocks_ref, sums_ref = refs
    if settle:
        lead, _ = factors(bounds, stage)

        def settle_rows(i, _):
            for side, (face_in, plane) in enumerate(((low_in, 0), (high_in, EDGE - 1))):
                got = face_in[pl.ds(pl.multiple_of(i * 16, 16), 16), :].astype(F32)
                for part in range(2):
                    rows = pl.ds((i * 2 + part) * QUAD + plane, EDGE, stride=EDGE)
                    value = field_ref[rows, :] + lead * got[part * EDGE : (part + 1) * EDGE, :]
                    value = value.astype(BF16).astype(F32)
                    if stage > STEPS:
                        value = value * weight_ref[side]
                    out_ref[rows, :] = value
            return 0

        lax.fori_loop(0, FACE // 16, settle_rows, 0)
        field_ref = out_ref
    if emit:

        def emit_rows(i, _):
            rows = pl.ds(pl.multiple_of(i * 128, 128), 128)
            plain_ref[rows, :] = field_ref[rows, :].astype(BF16)
            return 0

        lax.fori_loop(0, NODES // 128, emit_rows, 0)
    if spread:
        sums_ref[...] = jnp.zeros_like(sums_ref)

        def step(pair, _):
            for half, cell_y, cell_x, scale in pair_cells(pair, scale_ref):
                for j in range(EDGE):
                    rows = pl.ds(pl.multiple_of(first_row(cell_y, cell_x, j), EDGE), QUAD)
                    blocks_ref[pair, j * QUAD : (j + 1) * QUAD, half * COLS : (half + 1) * COLS] = (
                        field_ref[rows, :].astype(BF16))
            product = jnp.dot(face_mat_ref[...], blocks_ref[pair], preferred_element_type=F32)
            for half, cell_y, cell_x, scale in pair_cells(pair, scale_ref):
                for side in range(2):
                    for j in range(EDGE):
                        at = side * QUAD + j * EDGE
                        rows = pl.ds(side * FACE + ((EDGE - 1) * cell_y + j) * SIDE + (EDGE - 1) * cell_x, EDGE)
                        sums_ref[rows, :] += scale * product[at : at + EDGE, half * COLS : (half + 1) * COLS]
            return 0

        lax.fori_loop(0, PAIRS, step, 0)
        low_out[...] = sums_ref[:FACE, :].astype(BF16)
        high_out[...] = sums_ref[FACE:, :].astype(BF16)


def faces(stage, field, got, bounds, weight, face_mat, scale, emit=False, spread=True):
    settle = got is not None
    args, specs, outs = [field], [VMEM], []
    if settle:
        args += list(got)
        specs += [VMEM] * 2
        outs.append(pltpu.VMEM((NODES, COLS), F32))
    args += [*bounds, weight]
    specs += [SMEM] * 3
    if spread:
        args += [face_mat, scale]
        specs += [VMEM, SMEM]
    if emit:
        outs.append(jax.ShapeDtypeStruct((NODES, COLS), BF16))
    if spread:
        outs += [jax.ShapeDtypeStruct((FACE, COLS), BF16)] * 2
        outs.append(pltpu.VMEM((PAIRS, CELL_NODES, 2 * COLS), BF16))
    return pl.pallas_call(
        functools.partial(faces_kernel, stage, settle, emit, spread),
        name="faces",
        out_shape=tuple(outs),
        in_specs=specs,
        out_specs=(VMEM,) * len(outs),
        scratch_shapes=[pltpu.VMEM((2 * FACE, COLS), F32)] if spread else [],
        input_output_aliases={0: 0} if settle else {},
        compiler_params=BIG,
    )(*args)


def cells_kernel(stage, blocks_ref, field_ref, *refs):
    refs = list(refs)
    prev_ref = refs.pop(0) if 1 < stage <= STEPS else None
    pot_ref, mat_ref, low_ref, high_ref, scale_ref, out_ref = refs
    out_ref[...] = jnp.zeros_like(out_ref)

    def step(pair, _):
        product = jnp.dot(mat_ref[...], blocks_ref[pair], preferred_element_type=F32)
        for half, cell_y, cell_x, scale in pair_cells(pair, scale_ref):
            for j in range(EDGE):
                rows = pl.ds(pl.multiple_of(first_row(cell_y, cell_x, j), EDGE), QUAD)
                out_ref[rows, :] += scale * product[j * QUAD : (j + 1) * QUAD, half * COLS : (half + 1) * COLS]
        return 0

    lax.fori_loop(0, PAIRS, step, 0)
    lead, shift = factors((low_ref, high_ref), stage)
    plane = lax.broadcasted_iota(jnp.int32, (QUAD, COLS), 0) % EDGE
    inside = (plane > 0) & (plane < EDGE - 1)

    def finish(i, _):
        rows = pl.ds(pl.multiple_of(i * QUAD, QUAD), QUAD)
        field = field_ref[rows, :]
        value = out_ref[rows, :] + pot_ref[rows, :] * field
        if stage <= STEPS:
            value = lead * value - shift * field
        if prev_ref is not None:
            value = value - prev_ref[rows, :]
        out_ref[rows, :] = jnp.where(inside, value.astype(BF16).astype(F32), value)
        return 0

    lax.fori_loop(0, NODES // QUAD, finish, 0)


def cells(stage, blocks, field, prev, pot, mat, bounds, scale):
    args = [blocks, field] + ([prev] if 1 < stage <= STEPS else []) + [pot, mat]
    specs = [VMEM] * len(args) + [SMEM] * 3
    return pl.pallas_call(
        functools.partial(cells_kernel, stage),
        name="cells",
        out_shape=pltpu.VMEM((NODES, COLS), F32),
        in_specs=specs,
        out_specs=VMEM,
        compiler_params=BIG,
    )(*args, *bounds, scale)


def return_kernel(field_ref, index_ref, out_ref, hot_ref, rhs_ref):
    j = lax.broadcasted_iota(jnp.int32, (EDGE, COLS), 0)

    def step(plane, _):
        for cell in range(CELLS):
            cell_y, cell_x = cell // SLAB_XY, cell % SLAB_XY
            for k in range(EDGE):
                at = cell * QUAD + k * EDGE
                value = field_ref[pl.ds(first_row(cell_y, cell_x, k) + plane, EDGE, stride=EDGE), :]
                if cell_y > 0 and k == 0:
                    value = jnp.zeros_like(value)
                elif cell_x > 0:
                    value = jnp.where(j == 0, 0.0, value)
                rhs_ref[at : at + EDGE, :] = value
        want = index_ref[pl.ds(plane, 1), :].astype(F32) - (plane * FACE).astype(F32)
        rhs = rhs_ref[...].astype(BF16)
        for part in range(THIRDS):
            row = lax.broadcasted_iota(jnp.int32, (THIRD, CELLS * QUAD), 0).astype(F32) + float(part * THIRD)
            hot_ref[...] = jnp.where(want == row, 1.0, 0.0).astype(BF16)
            got = jnp.dot(hot_ref[...], rhs, preferred_element_type=F32)
            start = pl.multiple_of(plane * FACE + part * THIRD, 16)
            out_ref[pl.ds(start, THIRD), :] = got.astype(BF16)
        return 0

    lax.fori_loop(0, EDGE, step, 0)


def hand_back(field, connectivity):
    index = connectivity.reshape(CELLS, EDGE, QUAD).transpose(1, 0, 2).reshape(EDGE, CELLS * QUAD)
    return pl.pallas_call(
        return_kernel,
        name="hand_back",
        out_shape=jax.ShapeDtypeStruct((NODES, COLS), BF16),
        in_specs=[VMEM] * 2,
        out_specs=VMEM,
        scratch_shapes=[
            pltpu.VMEM((THIRD, CELLS * QUAD), BF16),
            pltpu.VMEM((CELLS * QUAD, COLS), F32),
        ],
        compiler_params=BIG,
    )(field, index)


def in_blocks(x, dim, peers):
    dims = x.shape
    blocks = x.reshape(*dims[:dim], peers, dims[dim] // peers, *dims[dim + 1 :])
    return jnp.moveaxis(blocks, dim, 0)


def summed_on_arrival(x, axis, dim):
    blocks = in_blocks(x, dim, lax.axis_size(axis))
    arrived = lax.all_to_all(blocks, axis, split_axis=0, concat_axis=0, tiled=True)
    return arrived.astype(F32).sum(axis=0)


def swap_faces(low, high):
    count = lax.axis_size("space")
    from_below = lax.ppermute(high, "space", [(i, i + 1) for i in range(count - 1)])
    from_above = lax.ppermute(low, "space", [(i + 1, i) for i in range(count - 1)])
    return from_below, from_above


def local(states, potential, cell_matrix, cell_scale, connectivity, lower_bound, upper_bound):
    bounds = (lower_bound, upper_bound)
    position = lax.axis_index("space")
    count = lax.axis_size("space")
    weight = jnp.stack([
        jnp.where(position > 0, 0.5, 1.0).astype(F32),
        jnp.where(position < count - 1, 0.5, 1.0).astype(F32),
    ])
    field, pot, mat, face_mat = gather(states, potential, connectivity, cell_matrix)
    low, high, blocks = faces(0, field, None, bounds, weight, face_mat, cell_scale)
    prev = None
    for stage in range(1, STEPS + 2):
        got = swap_faces(low, high)
        part = cells(stage, blocks, field, prev, pot, mat, bounds, cell_scale)
        prev = field
        if stage < STEPS:
            field, low, high, blocks = faces(stage, part, got, bounds, weight, face_mat, cell_scale)
        elif stage == STEPS:
            field, current, low, high, blocks = faces(
                stage, part, got, bounds, weight, face_mat, cell_scale, emit=True)
        else:
            _, weighted = faces(stage, part, got, bounds, weight, None, None, emit=True, spread=False)
    node_states = lax.all_to_all(current, "band", split_axis=0, concat_axis=1, tiled=True)
    node_images = lax.all_to_all(weighted, "band", split_axis=0, concat_axis=1, tiled=True)
    partial_matrix = lax.dot_general(
        node_states, node_images, (((0,), (0,)), ((), ())), preferred_element_type=F32)
    row_sums = summed_on_arrival(partial_matrix.astype(BF16), "band", 0)
    totals = summed_on_arrival(row_sums.astype(BF16), "space", 1)
    filtered = hand_back(field, connectivity)
    global_count = FACE * ((EDGE - 1) * count + 1)
    return filtered, totals / global_count


def solution(mesh):
    placed = (P("space", "band"), P("space"), P(), P("space"), P("space", None), P(), P())
    return jax.shard_map(
        local,
        mesh=mesh,
        in_specs=placed,
        out_specs=(P("space", "band"), P("band", "space")),
        check_vma=False,
    )
```

```python
import functools

import jax
import jax.numpy as jnp
from jax import lax
from jax.experimental import pallas as pl
from jax.experimental.pallas import tpu as pltpu
from jax.sharding import PartitionSpec as P

EDGE = 8
SLAB_XY = 5
STEPS = 4
CELLS = SLAB_XY * SLAB_XY
PAIRS = (CELLS + 1) // 2
CELL_NODES = EDGE**3
SIDE = (EDGE - 1) * SLAB_XY + 1
FACE = SIDE * SIDE
NODES = FACE * EDGE
COLS = 128
SLABS = 16
GROUP = 144
GATHER_PARTS = ((0, CELLS),)
QUAD = EDGE * EDGE
THIRDS = 3
THIRD = FACE // THIRDS
F32 = jnp.float32
BF16 = jnp.bfloat16
VMEM = pl.BlockSpec(memory_space=pltpu.VMEM)
SMEM = pl.BlockSpec(memory_space=pltpu.SMEM)
BIG = pltpu.CompilerParams(vmem_limit_bytes=24 * 1024 * 1024)
SMALL = pltpu.CompilerParams(vmem_limit_bytes=8 * 1024 * 1024)


def first_row(cell_y, cell_x, j):
    return (((EDGE - 1) * cell_y + j) * SIDE + (EDGE - 1) * cell_x) * EDGE


def gather_kernel(states_ref, pot_ref, index_ref, matrix_ref, low_ref, high_ref, field_ref, pot_out_ref, mat_ref,
                  face_mat_ref, rhs_ref, hot_ref, column_ref):
    for cell_y in range(SLAB_XY):
        five = index_ref[cell_y * SLAB_XY : (cell_y + 1) * SLAB_XY, :].astype(F32)
        five = jnp.concatenate([five, jnp.zeros((EDGE - SLAB_XY, CELL_NODES), F32)], axis=0)
        column_ref[cell_y * CELL_NODES : (cell_y + 1) * CELL_NODES, :EDGE] = jnp.transpose(five)
    pot = jnp.transpose(pot_ref[...])
    high = pot.astype(BF16)
    rest = pot - high.astype(F32)
    mid = rest.astype(BF16)
    low = (rest - mid.astype(F32)).astype(BF16)
    rhs_ref[:, COLS:] = jnp.concatenate(
        [high, mid, low, jnp.zeros((FACE, COLS - 3 * EDGE), BF16)], axis=1)

    new = lax.broadcasted_iota(jnp.int32, (CELL_NODES, CELL_NODES), 0)
    old = lax.broadcasted_iota(jnp.int32, (CELL_NODES, CELL_NODES), 1)
    order = jnp.where(old == (new % EDGE) * QUAD + new // EDGE, 1.0, 0.0).astype(BF16)
    across = (((1,), (1,)), ((), ()))
    turned = lax.dot_general(matrix_ref[...], order, across, preferred_element_type=F32).astype(BF16)
    face_mat_ref[:QUAD, :] = turned[:QUAD, :]
    face_mat_ref[QUAD:, :] = turned[CELL_NODES - QUAD :, :]
    mat_ref[...] = jnp.dot(order, turned, preferred_element_type=F32).astype(BF16)
    lead, shift = factors((low_ref, high_ref), 2)

    def step(plane, _):
        rhs_ref[:, :COLS] = states_ref[pl.ds(pl.multiple_of(plane * FACE, 16), FACE), :]
        start = (plane * FACE).astype(F32)
        lane = lax.broadcasted_iota(jnp.int32, (EDGE, COLS), 1)
        mine = (lane % EDGE == plane) & (lane < 3 * EDGE)
        for first, last in GATHER_PARTS:
            at = 0
            for cell in range(first, last):
                cell_y, cell_x = cell // SLAB_XY, cell % SLAB_XY
                rows = QUAD if cell_y == SLAB_XY - 1 else QUAD - EDGE
                lanes = lax.broadcasted_iota(jnp.int32, (rows, FACE), 1).astype(F32)
                want = column_ref[pl.ds(pl.multiple_of(cell_y * CELL_NODES + plane * QUAD, 8), rows), cell_x : cell_x + 1] - start
                hot_ref[at : at + rows, :] = jnp.where(want == lanes, 1.0, 0.0).astype(BF16)
                at += rows
            got = jnp.dot(hot_ref[:at, :], rhs_ref[...], preferred_element_type=F32)
            at = 0
            for cell in range(first, last):
                cell_y, cell_x = cell // SLAB_XY, cell % SLAB_XY
                for j in range(EDGE if cell_y == SLAB_XY - 1 else EDGE - 1):
                    rows = pl.ds(first_row(cell_y, cell_x, j) + plane, EDGE, stride=EDGE)
                    field_ref[rows, :] = got[at : at + EDGE, :COLS]
                    value = jnp.sum(jnp.where(mine, got[at : at + EDGE, COLS:], 0.0), axis=1, keepdims=True)
                    pot_out_ref[rows, :] = lead * value - shift
                    at += EDGE
        return 0

    lax.fori_loop(0, EDGE, step, 0)


def gather(states, potential, connectivity, matrix, bounds):
    return pl.pallas_call(
        gather_kernel,
        name="gather_states",
        out_shape=(
            pltpu.VMEM((NODES, COLS), F32),
            pltpu.VMEM((NODES, COLS), F32),
            pltpu.VMEM((CELL_NODES, CELL_NODES), BF16),
            pltpu.VMEM((2 * QUAD, CELL_NODES), BF16),
        ),
        in_specs=[VMEM] * 4 + [SMEM] * 2,
        out_specs=(VMEM,) * 4,
        scratch_shapes=[
            pltpu.VMEM((FACE, 2 * COLS), BF16),
            pltpu.VMEM((CELLS * QUAD, FACE), BF16),
            pltpu.VMEM((SLAB_XY * CELL_NODES, COLS), F32),
        ],
        compiler_params=BIG,
    )(states, potential.reshape(EDGE, FACE), connectivity, matrix, *bounds)


def half_width_of(bounds):
    low, high = bounds
    return jnp.full((1, COLS), (high[0] - low[0]) * 0.5, F32)


def factors(bounds, stage):
    if stage > STEPS:
        return jnp.ones((1, COLS), F32), None
    low, high = bounds
    center = (high[0] + low[0]) * 0.5
    lead = (1.0 if stage == 1 else 2.0) / half_width_of(bounds)
    return lead, lead * center


def pair_cells(pair, scale_ref):
    for half in range(2):
        index = 2 * pair + half
        cell = jnp.minimum(index, CELLS - 1)
        yield half, cell // SLAB_XY, cell % SLAB_XY, jnp.where(index < CELLS, scale_ref[cell], 0.0)


def faces_kernel(stage, settle, emit, spread, *refs):
    refs = list(refs)
    field_ref = refs.pop(0)
    if settle:
        near_in, far_in = refs.pop(0), refs.pop(0)
    bounds = (refs.pop(0), refs.pop(0))
    position_ref = refs.pop(0)
    odd = position_ref[0] % 2
    if spread:
        face_mat_ref, scale_ref = refs.pop(0), refs.pop(0)
    if settle:
        out_ref = refs.pop(0)
    if emit:
        plain_ref = refs.pop(0)
    if spread:
        near_out, far_out, blocks_ref, sums_ref = refs
    if settle:
        lead, _ = factors(bounds, stage)
        ends = (position_ref[0] == 0) | (position_ref[0] == SLABS - 1)
        far_weight = jnp.where(ends, 1.0, 0.5)

        def settle_rows(i, _):
            for face_in, plane, weight in (
                (near_in, (EDGE - 1) * (1 - odd), 0.5),
                (far_in, (EDGE - 1) * odd, far_weight),
            ):
                got = face_in[pl.ds(pl.multiple_of(i * GROUP, 16), GROUP), :].astype(F32)
                for part in range(GROUP // EDGE):
                    rows = pl.ds((i * (GROUP // EDGE) + part) * QUAD + plane, EDGE, stride=EDGE)
                    value = field_ref[rows, :] + lead * got[part * EDGE : (part + 1) * EDGE, :]
                    value = value.astype(BF16).astype(F32)
                    if stage > STEPS:
                        value = value * weight
                    out_ref[rows, :] = value
            return 0

        lax.fori_loop(0, FACE // GROUP, settle_rows, 0)
        field_ref = out_ref
    if emit:

        def emit_rows(i, _):
            rows = pl.ds(pl.multiple_of(i * 128, 128), 128)
            plain_ref[rows, :] = field_ref[rows, :].astype(BF16)
            return 0

        lax.fori_loop(0, NODES // 128, emit_rows, 0)
    if spread:
        sums_ref[...] = jnp.zeros_like(sums_ref)

        def step(pair, _):
            for half, cell_y, cell_x, scale in pair_cells(pair, scale_ref):
                for j in range(EDGE):
                    rows = pl.ds(pl.multiple_of(first_row(cell_y, cell_x, j), EDGE), QUAD)
                    blocks_ref[pair, j * QUAD : (j + 1) * QUAD, half * COLS : (half + 1) * COLS] = (
                        field_ref[rows, :].astype(BF16))
            product = jnp.dot(face_mat_ref[...], blocks_ref[pair], preferred_element_type=F32)
            for half, cell_y, cell_x, scale in pair_cells(pair, scale_ref):
                for side in range(2):
                    for j in range(EDGE):
                        at = side * QUAD + j * EDGE
                        rows = pl.ds(side * FACE + ((EDGE - 1) * cell_y + j) * SIDE + (EDGE - 1) * cell_x, EDGE)
                        sums_ref[rows, :] += scale * product[at : at + EDGE, half * COLS : (half + 1) * COLS]
            return 0

        lax.fori_loop(0, PAIRS, step, 0)
        near_out[...] = sums_ref[pl.ds(pl.multiple_of((1 - odd) * FACE, 16), FACE), :].astype(BF16)
        far_out[...] = sums_ref[pl.ds(pl.multiple_of(odd * FACE, 16), FACE), :].astype(BF16)


def faces(stage, field, got, bounds, position, face_mat, scale, emit=False, spread=True):
    settle = got is not None
    args, specs, outs = [field], [VMEM], []
    if settle:
        args += list(got)
        specs += [VMEM] * 2
        outs.append(pltpu.VMEM((NODES, COLS), F32))
    args += [*bounds, position]
    specs += [SMEM] * 3
    if spread:
        args += [face_mat, scale]
        specs += [VMEM, SMEM]
    if emit:
        outs.append(jax.ShapeDtypeStruct((NODES, COLS), BF16))
    if spread:
        outs += [jax.ShapeDtypeStruct((FACE, COLS), BF16)] * 2
        outs.append(pltpu.VMEM((PAIRS, CELL_NODES, 2 * COLS), BF16))
    return pl.pallas_call(
        functools.partial(faces_kernel, stage, settle, emit, spread),
        name="faces",
        out_shape=tuple(outs),
        in_specs=specs,
        out_specs=(VMEM,) * len(outs),
        scratch_shapes=[pltpu.VMEM((2 * FACE, COLS), F32)] if spread else [],
        input_output_aliases={0: 0} if settle else {},
        compiler_params=SMALL,
    )(*args)


def cells_kernel(stage, blocks_ref, field_ref, *refs):
    refs = list(refs)
    prev_ref = refs.pop(0) if 1 < stage <= STEPS else None
    pot_ref, mat_ref, low_ref, high_ref, scale_ref, out_ref = refs
    bounds = (low_ref, high_ref)
    out_ref[...] = jnp.zeros_like(out_ref)
    lead, _ = factors(bounds, stage)

    def step(pair, _):
        product = jnp.dot(mat_ref[...], blocks_ref[pair], preferred_element_type=F32)
        for half, cell_y, cell_x, scale in pair_cells(pair, scale_ref):
            factor = lead * scale
            for j in range(EDGE):
                rows = pl.ds(pl.multiple_of(first_row(cell_y, cell_x, j), EDGE), QUAD)
                out_ref[rows, :] += factor * product[j * QUAD : (j + 1) * QUAD, half * COLS : (half + 1) * COLS]
        return 0

    lax.fori_loop(0, PAIRS, step, 0)
    plane = lax.broadcasted_iota(jnp.int32, (EDGE, COLS), 0)
    inside = (plane > 0) & (plane < EDGE - 1)
    half_width = half_width_of(bounds) * 0.5
    center = jnp.full((1, COLS), (high_ref[0] + low_ref[0]) * 0.5, F32)

    def finish(i, _):
        for part in range(GROUP // EDGE):
            rows = pl.ds(pl.multiple_of(i * GROUP + part * EDGE, EDGE), EDGE)
            shifted = pot_ref[rows, :]
            if stage == 1:
                shifted = shifted * 0.5
            elif stage > STEPS:
                shifted = shifted * half_width + center
            value = out_ref[rows, :] + shifted * field_ref[rows, :]
            if prev_ref is not None:
                value = value - prev_ref[rows, :]
            out_ref[rows, :] = jnp.where(inside, value.astype(BF16).astype(F32), value)
        return 0

    lax.fori_loop(0, NODES // GROUP, finish, 0)


def cells(stage, blocks, field, prev, pot, mat, bounds, scale):
    args = [blocks, field] + ([prev] if 1 < stage <= STEPS else []) + [pot, mat]
    specs = [VMEM] * len(args) + [SMEM] * 3
    return pl.pallas_call(
        functools.partial(cells_kernel, stage),
        name="cells",
        out_shape=pltpu.VMEM((NODES, COLS), F32),
        in_specs=specs,
        out_specs=VMEM,
        compiler_params=SMALL,
    )(*args, *bounds, scale)


def return_kernel(plain_ref, index_ref, out_ref, hot_ref, rhs_ref, field_ref):
    field_ref[...] = plain_ref[...].astype(F32)
    j = lax.broadcasted_iota(jnp.int32, (EDGE, COLS), 0)

    def step(plane, _):
        for cell in range(CELLS):
            cell_y, cell_x = cell // SLAB_XY, cell % SLAB_XY
            for k in range(EDGE):
                at = cell * QUAD + k * EDGE
                value = field_ref[pl.ds(first_row(cell_y, cell_x, k) + plane, EDGE, stride=EDGE), :]
                if cell_y > 0 and k == 0:
                    value = jnp.zeros_like(value)
                elif cell_x > 0:
                    value = jnp.where(j == 0, 0.0, value)
                rhs_ref[at : at + EDGE, :] = value
        want = index_ref[pl.ds(plane, 1), :].astype(F32) - (plane * FACE).astype(F32)
        rhs = rhs_ref[...].astype(BF16)
        for part in range(THIRDS):
            row = lax.broadcasted_iota(jnp.int32, (THIRD, CELLS * QUAD), 0).astype(F32) + float(part * THIRD)
            hot_ref[...] = jnp.where(want == row, 1.0, 0.0).astype(BF16)
            got = jnp.dot(hot_ref[...], rhs, preferred_element_type=F32)
            start = pl.multiple_of(plane * FACE + part * THIRD, 16)
            out_ref[pl.ds(start, THIRD), :] = got.astype(BF16)
        return 0

    lax.fori_loop(0, EDGE, step, 0)


def hand_back(field, connectivity):
    index = connectivity.reshape(CELLS, EDGE, QUAD).transpose(1, 0, 2).reshape(EDGE, CELLS * QUAD)
    return pl.pallas_call(
        return_kernel,
        name="hand_back",
        out_shape=jax.ShapeDtypeStruct((NODES, COLS), BF16),
        in_specs=[VMEM] * 2,
        out_specs=VMEM,
        scratch_shapes=[
            pltpu.VMEM((THIRD, CELLS * QUAD), BF16),
            pltpu.VMEM((CELLS * QUAD, COLS), F32),
            pltpu.VMEM((NODES, COLS), F32),
        ],
        compiler_params=BIG,
    )(field, index)


def project(states, images):
    count, bands = lax.axis_size("space"), lax.axis_size("band")
    odd = lax.axis_index("space") % 2
    halves = count // 2
    product = lax.dot_general(images, states, (((0,), (0,)), ((), ())), preferred_element_type=F32).astype(BF16)
    width = product.shape[0] // count
    product = product.reshape(halves, 2, width, bands, COLS)
    kept = lax.dynamic_index_in_dim(product, odd, axis=1, keepdims=False)
    sent = lax.dynamic_index_in_dim(product, 1 - odd, axis=1, keepdims=False)
    got = lax.ppermute(sent, "space", [(i, i ^ 1) for i in range(count)])
    both = (kept.astype(F32) + got.astype(F32)).astype(BF16)
    both = both.transpose(0, 2, 1, 3).reshape(halves * bands, width, COLS)
    groups = [[(2 * half + part) * bands + band for half in range(halves) for band in range(bands)] for part in range(2)]
    arrived = lax.all_to_all(both, ("space", "band"), split_axis=0, concat_axis=0, tiled=True, axis_index_groups=groups)
    return arrived.astype(F32).sum(axis=0).T


def swap_faces(near, far):
    count = lax.axis_size("space")
    apart = [(i, i + 1) for i in range(1, count - 1, 2)]
    beside = [(i, i + 1) for i in range(0, count, 2)]
    both_ways = lambda pairs: pairs + [(j, i) for i, j in pairs]
    near, far = lax.optimization_barrier((near, far))
    from_near = lax.ppermute(near, "space", both_ways(beside))
    from_far = lax.ppermute(far, "space", both_ways(apart))
    return from_near, from_far


def local(states, potential, cell_matrix, cell_scale, connectivity, lower_bound, upper_bound):
    bounds = (lower_bound, upper_bound)
    position = lax.axis_index("space").astype(jnp.int32).reshape(1)
    count = lax.axis_size("space")
    field, pot, mat, face_mat = gather(states, potential, connectivity, cell_matrix, bounds)
    near, far, blocks = faces(0, field, None, bounds, position, face_mat, cell_scale)
    prev = None
    for stage in range(1, STEPS + 2):
        got = swap_faces(near, far)
        part = cells(stage, blocks, field, prev, pot, mat, bounds, cell_scale)
        prev = field
        if stage < STEPS:
            field, near, far, blocks = faces(stage, part, got, bounds, position, face_mat, cell_scale)
        elif stage == STEPS:
            field, current, near, far, blocks = faces(
                stage, part, got, bounds, position, face_mat, cell_scale, emit=True)
        else:
            _, weighted = faces(stage, part, got, bounds, position, None, None, emit=True, spread=False)
    node_states = lax.all_to_all(current, "band", split_axis=0, concat_axis=1, tiled=True)
    weighted, current = lax.optimization_barrier((weighted, current))
    filtered = hand_back(current, connectivity)
    node_images = lax.all_to_all(weighted, "band", split_axis=0, concat_axis=1, tiled=True)
    totals = project(node_states, node_images)
    global_count = FACE * ((EDGE - 1) * count + 1)
    return filtered, totals / global_count


def solution(mesh):
    placed = (P("space", "band"), P("space"), P(), P("space"), P("space", None), P(), P())
    return jax.shard_map(
        local,
        mesh=mesh,
        in_specs=placed,
        out_specs=(P("space", "band"), P("band", "space")),
        check_vma=False,
    )
```

```python
import functools

import jax
import jax.numpy as jnp
from jax import lax
from jax.experimental import pallas as pl
from jax.experimental.pallas import tpu as pltpu
from jax.sharding import PartitionSpec as P

EDGE = 8
SLAB_XY = 5
STEPS = 4
CELLS = SLAB_XY * SLAB_XY
PAIRS = (CELLS + 1) // 2
CELL_NODES = EDGE**3
SIDE = (EDGE - 1) * SLAB_XY + 1
FACE = SIDE * SIDE
NODES = FACE * EDGE
COLS = 128
SLABS = 16
GROUP = 144
BANDS = 8
INNER = (EDGE - 2) * FACE
INNER_BLOCK = 976
OUTER = FACE + FACE // 2
OUTER_BLOCK = 256
BLOCK = INNER_BLOCK + 2 * OUTER_BLOCK
GATHER_PARTS = ((0, CELLS),)
QUAD = EDGE * EDGE
THIRDS = 3
THIRD = FACE // THIRDS
F32 = jnp.float32
BF16 = jnp.bfloat16
VMEM = pl.BlockSpec(memory_space=pltpu.VMEM)
SMEM = pl.BlockSpec(memory_space=pltpu.SMEM)
HBM = pl.BlockSpec(memory_space=pltpu.HBM)
BIG = pltpu.CompilerParams(vmem_limit_bytes=24 * 1024 * 1024)
SMALL = pltpu.CompilerParams(vmem_limit_bytes=8 * 1024 * 1024)


def first_row(cell_y, cell_x, j):
    return (((EDGE - 1) * cell_y + j) * SIDE + (EDGE - 1) * cell_x) * EDGE


def gather_kernel(states_hbm, pot_ref, index_hbm, matrix_hbm, low_ref, high_ref, field_ref, pot_out_ref, mat_ref,
                  full_ref, inner_ref, outer_ref, rhs_ref, hot_ref, column_ref, states_ref, index_ref, matrix_ref, sems):
    index_copy = pltpu.make_async_copy(index_hbm, index_ref, sems.at[0])
    matrix_copy = pltpu.make_async_copy(matrix_hbm, matrix_ref, sems.at[1])
    states_copy = pltpu.make_async_copy(states_hbm, states_ref, sems.at[2])
    index_copy.start()
    matrix_copy.start()
    states_copy.start()
    index_copy.wait()
    for cell_y in range(SLAB_XY):
        five = index_ref[cell_y * SLAB_XY : (cell_y + 1) * SLAB_XY, :].astype(F32)
        five = jnp.concatenate([five, jnp.zeros((EDGE - SLAB_XY, CELL_NODES), F32)], axis=0)
        column_ref[cell_y * CELL_NODES : (cell_y + 1) * CELL_NODES, :EDGE] = jnp.transpose(five)
    pot = jnp.transpose(pot_ref[...])
    high = pot.astype(BF16)
    rest = pot - high.astype(F32)
    mid = rest.astype(BF16)
    low = (rest - mid.astype(F32)).astype(BF16)
    rhs_ref[:, COLS:] = jnp.concatenate(
        [high, mid, low, jnp.zeros((FACE, COLS - 3 * EDGE), BF16)], axis=1)

    matrix_copy.wait()
    new = lax.broadcasted_iota(jnp.int32, (CELL_NODES, CELL_NODES), 0)
    old = lax.broadcasted_iota(jnp.int32, (CELL_NODES, CELL_NODES), 1)
    order = jnp.where(old == (new % EDGE) * QUAD + new // EDGE, 1.0, 0.0).astype(BF16)
    across = (((1,), (1,)), ((), ()))
    turned = lax.dot_general(matrix_ref[...], order, across, preferred_element_type=F32).astype(BF16)
    mat_ref[...] = jnp.dot(order, turned, preferred_element_type=F32).astype(BF16)
    for side, first in enumerate((0, CELL_NODES - QUAD)):
        rows = pl.ds(side * QUAD, QUAD)
        face_rows = turned[first : first + QUAD, :].astype(F32)
        z = lax.broadcasted_iota(jnp.int32, (QUAD, CELL_NODES), 1) % EDGE
        full_ref[rows, :] = face_rows.astype(BF16)
        inner_ref[rows, :] = jnp.where((z > 0) & (z < EDGE - 1), face_rows, 0.0).astype(BF16)
        outer_ref[rows, :QUAD] = matrix_ref[first : first + QUAD, :QUAD]
        outer_ref[rows, QUAD:] = matrix_ref[first : first + QUAD, CELL_NODES - QUAD :]
    lead, shift = factors((low_ref, high_ref), 2)
    states_copy.wait()

    def step(plane, _):
        rhs_ref[:, :COLS] = states_ref[pl.ds(pl.multiple_of(plane * FACE, 16), FACE), :]
        start = (plane * FACE).astype(F32)
        lane = lax.broadcasted_iota(jnp.int32, (EDGE, COLS), 1)
        mine = (lane % EDGE == plane) & (lane < 3 * EDGE)
        for first, last in GATHER_PARTS:
            at = 0
            for cell in range(first, last):
                cell_y, cell_x = cell // SLAB_XY, cell % SLAB_XY
                rows = QUAD if cell_y == SLAB_XY - 1 else QUAD - EDGE
                lanes = lax.broadcasted_iota(jnp.int32, (rows, FACE), 1).astype(F32)
                want = column_ref[pl.ds(pl.multiple_of(cell_y * CELL_NODES + plane * QUAD, 8), rows), cell_x : cell_x + 1] - start
                hot_ref[at : at + rows, :] = jnp.where(want == lanes, 1.0, 0.0).astype(BF16)
                at += rows
            got = jnp.dot(hot_ref[:at, :], rhs_ref[...], preferred_element_type=F32)
            at = 0
            for cell in range(first, last):
                cell_y, cell_x = cell // SLAB_XY, cell % SLAB_XY
                for j in range(EDGE if cell_y == SLAB_XY - 1 else EDGE - 1):
                    rows = pl.ds(first_row(cell_y, cell_x, j) + plane, EDGE, stride=EDGE)
                    field_ref[rows, :] = got[at : at + EDGE, :COLS]
                    value = jnp.sum(jnp.where(mine, got[at : at + EDGE, COLS:], 0.0), axis=1, keepdims=True)
                    pot_out_ref[rows, :] = lead * value - shift
                    at += EDGE
        return 0

    lax.fori_loop(0, EDGE, step, 0)


def gather(states, potential, connectivity, matrix, bounds):
    return pl.pallas_call(
        gather_kernel,
        name="gather_states",
        out_shape=(
            pltpu.VMEM((NODES, COLS), F32),
            pltpu.VMEM((NODES, COLS), F32),
            pltpu.VMEM((CELL_NODES, CELL_NODES), BF16),
            pltpu.VMEM((2 * QUAD, CELL_NODES), BF16),
            pltpu.VMEM((2 * QUAD, CELL_NODES), BF16),
            pltpu.VMEM((2 * QUAD, 2 * QUAD), BF16),
        ),
        in_specs=[HBM, VMEM, HBM, HBM] + [SMEM] * 2,
        out_specs=(VMEM,) * 6,
        scratch_shapes=[
            pltpu.VMEM((FACE, 2 * COLS), BF16),
            pltpu.VMEM((CELLS * QUAD, FACE), BF16),
            pltpu.VMEM((SLAB_XY * CELL_NODES, COLS), F32),
            pltpu.VMEM((NODES, COLS), BF16),
            pltpu.VMEM((CELLS, CELL_NODES), jnp.int32),
            pltpu.VMEM((CELL_NODES, CELL_NODES), BF16),
            pltpu.SemaphoreType.DMA((3,)),
        ],
        compiler_params=BIG,
    )(states, potential.reshape(EDGE, FACE), connectivity, matrix, *bounds)


def half_width_of(bounds):
    low, high = bounds
    return jnp.full((1, COLS), (high[0] - low[0]) * 0.5, F32)


def factors(bounds, stage):
    if stage > STEPS:
        return jnp.ones((1, COLS), F32), None
    low, high = bounds
    center = (high[0] + low[0]) * 0.5
    lead = (1.0 if stage == 1 else 2.0) / half_width_of(bounds)
    return lead, lead * center


def pair_cells(pair, scale_ref):
    for half in range(2):
        index = 2 * pair + half
        cell = jnp.minimum(index, CELLS - 1)
        yield half, cell // SLAB_XY, cell % SLAB_XY, jnp.where(index < CELLS, scale_ref[cell], 0.0)


def cell_blocks(field_ref, pair, scale_ref):
    columns = []
    for half, cell_y, cell_x, _ in pair_cells(pair, scale_ref):
        pieces = []
        for j in range(EDGE):
            rows = pl.ds(pl.multiple_of(first_row(cell_y, cell_x, j), EDGE), QUAD)
            pieces.append(field_ref[rows, :].astype(BF16))
        columns.append(jnp.concatenate(pieces, axis=0))
    return jnp.concatenate(columns, axis=1)


def add_faces(sums_ref, product, pair, scale_ref):
    for half, cell_y, cell_x, scale in pair_cells(pair, scale_ref):
        for side in range(2):
            for j in range(EDGE):
                at = side * QUAD + j * EDGE
                rows = pl.ds(side * FACE + ((EDGE - 1) * cell_y + j) * SIDE + (EDGE - 1) * cell_x, EDGE)
                sums_ref[rows, :] += scale * product[at : at + EDGE, half * COLS : (half + 1) * COLS]


def spread_faces(field_ref, matrix_ref, scale_ref, sums_ref):
    sums_ref[...] = jnp.zeros_like(sums_ref)

    def step(pair, _):
        blocks = cell_blocks(field_ref, pair, scale_ref)
        product = jnp.dot(matrix_ref[...], blocks, preferred_element_type=F32)
        add_faces(sums_ref, product, pair, scale_ref)
        return 0

    lax.fori_loop(0, PAIRS, step, 0)


def hand_out(sums_ref, odd, near_out, far_out):
    near_out[...] = sums_ref[pl.ds(pl.multiple_of((1 - odd) * FACE, 16), FACE), :].astype(BF16)
    far_out[...] = sums_ref[pl.ds(pl.multiple_of(odd * FACE, 16), FACE), :].astype(BF16)


def first_faces_kernel(field_ref, full_ref, scale_ref, position_ref, near_out, far_out, sums_ref):
    spread_faces(field_ref, full_ref, scale_ref, sums_ref)
    hand_out(sums_ref, position_ref[0] % 2, near_out, far_out)


def first_faces(field, full, scale, position):
    return pl.pallas_call(
        first_faces_kernel,
        name="first_faces",
        out_shape=(jax.ShapeDtypeStruct((FACE, COLS), BF16),) * 2,
        in_specs=[VMEM] * 2 + [SMEM] * 2,
        out_specs=(VMEM,) * 2,
        scratch_shapes=[pltpu.VMEM((2 * FACE, COLS), F32)],
        compiler_params=SMALL,
    )(field, full, scale, position)


def put_inner(field_ref, store):
    def planes(i, _):
        for z in range(1, EDGE - 1):
            for part in range(3):
                node = i * 48 + part * 16
                halves = [field_ref[pl.ds((node + k) * EDGE + z, EDGE, stride=EDGE), :] for k in (0, EDGE)]
                store((z - 1) * FACE + node, jnp.concatenate(halves, axis=0).astype(BF16))
        return 0

    lax.fori_loop(0, FACE // 48, planes, 0)
    for row in range(INNER, BANDS * INNER_BLOCK, 16):
        store(row, jnp.zeros((16, COLS), BF16))


def put_outer(face_ref, odd, far_weight, store):
    def rows(i, _):
        for part in range(4):
            row = (i * 4 + part) * 16
            far = row < FACE
            near_at = (1 - odd) * FACE + odd * (FACE // 2) + row - FACE
            at = jnp.where(far, odd * FACE + row, jnp.minimum(near_at, 2 * FACE))
            value = face_ref[pl.ds(pl.multiple_of(at, EDGE), 16), :]
            if far_weight is not None:
                value = value * jnp.where(far, far_weight, 1.0)
            index = lax.broadcasted_iota(jnp.int32, (16, COLS), 0) + row
            store(row, jnp.where(index < OUTER, value, 0.0).astype(BF16))
        return 0

    lax.fori_loop(0, BANDS * OUTER_BLOCK // 64, rows, 0)


def faces_kernel(stage, *refs):
    emit, spread = stage >= STEPS, stage <= STEPS
    refs = list(refs)
    field_ref, near_in, far_in, low_ref, high_ref, position_ref = refs[:6]
    refs = refs[6:]
    if spread:
        outer_ref, scale_ref, _ = refs[:3]
        refs = refs[3:]
        out_ref = refs.pop(0)
        if emit:
            plain_ref, edge_ref = refs.pop(0), refs.pop(0)
        sums_ref, near_out, far_out, face_ref = refs
    else:
        _, block_ref, face_ref = refs
    odd = position_ref[0] % 2
    lead, _ = factors((low_ref, high_ref), stage)
    ends = (position_ref[0] == 0) | (position_ref[0] == SLABS - 1)
    far_weight = jnp.where(ends, 1.0, 0.5)

    def settle_rows(i, _):
        for face_in, plane, side in ((near_in, (EDGE - 1) * (1 - odd), 1 - odd), (far_in, (EDGE - 1) * odd, odd)):
            got = face_in[pl.ds(pl.multiple_of(i * GROUP, 16), GROUP), :].astype(F32)
            for part in range(GROUP // EDGE):
                rows = pl.ds((i * (GROUP // EDGE) + part) * QUAD + plane, EDGE, stride=EDGE)
                value = field_ref[rows, :] + lead * got[part * EDGE : (part + 1) * EDGE, :]
                value = value.astype(BF16).astype(F32)
                if spread:
                    out_ref[rows, :] = value
                face_ref[pl.ds(pl.multiple_of(side * FACE + i * GROUP + part * EDGE, EDGE), EDGE), :] = value
        return 0

    lax.fori_loop(0, FACE // GROUP, settle_rows, 0)
    if not spread:

        def put(row, value):
            at = (row // OUTER_BLOCK) * BLOCK + OUTER_BLOCK + INNER_BLOCK + row % OUTER_BLOCK
            block_ref[pl.ds(pl.multiple_of(at, 16), 16), :] = value

        put_outer(face_ref, odd, far_weight, put)
        return
    if spread:

        def step(pair, _):
            columns = []
            for half, cell_y, cell_x, _ in pair_cells(pair, scale_ref):
                pieces = []
                for side in range(2):
                    for j in range(EDGE):
                        rows = pl.ds(side * FACE + ((EDGE - 1) * cell_y + j) * SIDE + (EDGE - 1) * cell_x, EDGE)
                        pieces.append(face_ref[rows, :])
                columns.append(jnp.concatenate(pieces, axis=0).astype(BF16))
            product = jnp.dot(outer_ref[...], jnp.concatenate(columns, axis=1), preferred_element_type=F32)
            add_faces(sums_ref, product, pair, scale_ref)
            return 0

        lax.fori_loop(0, PAIRS, step, 0)
        hand_out(sums_ref, odd, near_out, far_out)
    if emit:

        def emit_rows(i, _):
            rows = pl.ds(pl.multiple_of(i * 2 * GROUP, 2 * GROUP), 2 * GROUP)
            plain_ref[rows, :] = out_ref[rows, :].astype(BF16)
            return 0

        def put_edge(row, value):
            edge_ref[pl.ds(pl.multiple_of(row, 16), 16), :] = value

        lax.fori_loop(0, NODES // (2 * GROUP), emit_rows, 0)
        put_outer(face_ref, odd, None, put_edge)


def faces(stage, part, got, bounds, position, outer=None, scale=None, sums=None, blocks=None):
    emit, spread = stage >= STEPS, stage <= STEPS
    args = [part, *got, *bounds, position]
    specs = [VMEM] * 3 + [SMEM] * 3
    outs = []
    if spread:
        args += [outer, scale, sums]
        specs += [VMEM, SMEM, VMEM]
        outs.append(pltpu.VMEM((NODES, COLS), F32))
        if emit:
            outs.append(jax.ShapeDtypeStruct((NODES, COLS), BF16))
            outs.append(jax.ShapeDtypeStruct((BANDS * OUTER_BLOCK, COLS), BF16))
        aliases = {0: 0, 8: len(outs)}
        outs.append(pltpu.VMEM((2 * FACE, COLS), F32))
        outs += [jax.ShapeDtypeStruct((FACE, COLS), BF16)] * 2
    else:
        args.append(blocks)
        specs.append(VMEM)
        outs.append(pltpu.VMEM((BANDS * BLOCK, COLS), BF16))
        aliases = {6: 0}
    return pl.pallas_call(
        functools.partial(faces_kernel, stage),
        name="faces",
        out_shape=tuple(outs),
        in_specs=specs,
        out_specs=(VMEM,) * len(outs),
        scratch_shapes=[pltpu.VMEM((2 * FACE + 16, COLS), F32)],
        input_output_aliases=aliases,
        compiler_params=SMALL,
    )(*args)


def cells_kernel(stage, field_ref, *refs):
    refs = list(refs)
    in_place = 1 < stage <= STEPS
    if in_place:
        refs.pop(0)
    pot_ref, mat_ref = refs.pop(0), refs.pop(0)
    inner_ref = refs.pop(0) if stage <= STEPS else None
    if stage > STEPS:
        edge_ref = refs.pop(0)
    low_ref, high_ref, scale_ref, out_ref = refs[:4]
    bounds = (low_ref, high_ref)
    if stage > STEPS:
        plain_ref, field_ref, block_ref = field_ref, refs[5], refs[4]
        for band in range(BANDS):
            block_ref[band * BLOCK : band * BLOCK + OUTER_BLOCK, :] = (
                edge_ref[band * OUTER_BLOCK : (band + 1) * OUTER_BLOCK, :])

        def widen(i, _):
            rows = pl.ds(pl.multiple_of(i * 2 * GROUP, 2 * GROUP), 2 * GROUP)
            field_ref[rows, :] = plain_ref[rows, :].astype(F32)
            return 0

        lax.fori_loop(0, NODES // (2 * GROUP), widen, 0)
    lead, _ = factors(bounds, stage)
    if in_place:
        lead = -lead
    else:
        out_ref[...] = jnp.zeros_like(out_ref)

    def step(pair, _):
        product = jnp.dot(mat_ref[...], cell_blocks(field_ref, pair, scale_ref), preferred_element_type=F32)
        for half, cell_y, cell_x, scale in pair_cells(pair, scale_ref):
            factor = lead * scale
            for j in range(EDGE):
                rows = pl.ds(pl.multiple_of(first_row(cell_y, cell_x, j), EDGE), QUAD)
                out_ref[rows, :] += factor * product[j * QUAD : (j + 1) * QUAD, half * COLS : (half + 1) * COLS]
        return 0

    lax.fori_loop(0, PAIRS, step, 0)
    plane = lax.broadcasted_iota(jnp.int32, (EDGE, COLS), 0)
    inside = (plane > 0) & (plane < EDGE - 1)
    half_width = half_width_of(bounds) * 0.5
    center = jnp.full((1, COLS), (high_ref[0] + low_ref[0]) * 0.5, F32)

    def finish(i, _):
        for part in range(GROUP // EDGE):
            rows = pl.ds(pl.multiple_of(i * GROUP + part * EDGE, EDGE), EDGE)
            shifted = pot_ref[rows, :]
            if stage == 1:
                shifted = shifted * 0.5
            elif stage > STEPS:
                shifted = shifted * half_width + center
            value = shifted * field_ref[rows, :]
            value = value - out_ref[rows, :] if in_place else value + out_ref[rows, :]
            out_ref[rows, :] = jnp.where(inside, value.astype(BF16).astype(F32), value)
        return 0

    lax.fori_loop(0, NODES // GROUP, finish, 0)

    def put(row, value):
        if stage == STEPS:
            refs[5][pl.ds(pl.multiple_of(row, 16), 16), :] = value
        else:
            at = (row // INNER_BLOCK) * BLOCK + OUTER_BLOCK + row % INNER_BLOCK
            block_ref[pl.ds(pl.multiple_of(at, 16), 16), :] = value

    if stage >= STEPS:
        put_inner(out_ref, put)
    if stage <= STEPS:
        spread_faces(out_ref, inner_ref, scale_ref, refs[4])


def cells(stage, field, prev, pot, mat, inner, bounds, scale, edge=None):
    args = [field] + ([prev] if 1 < stage <= STEPS else []) + [pot, mat, inner if stage <= STEPS else edge]
    specs = [VMEM] * len(args) + [SMEM] * 3
    outs = [pltpu.VMEM((NODES, COLS), F32)]
    if stage <= STEPS:
        outs.append(pltpu.VMEM((2 * FACE, COLS), F32))
    if stage == STEPS:
        outs.append(jax.ShapeDtypeStruct((BANDS * INNER_BLOCK, COLS), BF16))
    if stage > STEPS:
        outs.append(pltpu.VMEM((BANDS * BLOCK, COLS), BF16))
    return pl.pallas_call(
        functools.partial(cells_kernel, stage),
        name="cells",
        out_shape=tuple(outs),
        in_specs=specs,
        out_specs=(VMEM,) * len(outs),
        scratch_shapes=[] if stage <= STEPS else [pltpu.VMEM((NODES, COLS), F32)],
        input_output_aliases={1: 0} if 1 < stage <= STEPS else {},
        compiler_params=SMALL if stage <= STEPS else BIG,
    )(*args, *bounds, scale)


def return_kernel(plain_ref, index_ref, out_ref, hot_ref, rhs_ref, field_ref):
    field_ref[...] = plain_ref[...].astype(F32)
    j = lax.broadcasted_iota(jnp.int32, (EDGE, COLS), 0)

    def step(plane, _):
        for cell in range(CELLS):
            cell_y, cell_x = cell // SLAB_XY, cell % SLAB_XY
            for k in range(EDGE):
                at = cell * QUAD + k * EDGE
                value = field_ref[pl.ds(first_row(cell_y, cell_x, k) + plane, EDGE, stride=EDGE), :]
                if cell_y > 0 and k == 0:
                    value = jnp.zeros_like(value)
                elif cell_x > 0:
                    value = jnp.where(j == 0, 0.0, value)
                rhs_ref[at : at + EDGE, :] = value
        want = index_ref[pl.ds(plane, 1), :].astype(F32) - (plane * FACE).astype(F32)
        rhs = rhs_ref[...].astype(BF16)
        for part in range(THIRDS):
            row = lax.broadcasted_iota(jnp.int32, (THIRD, CELLS * QUAD), 0).astype(F32) + float(part * THIRD)
            hot_ref[...] = jnp.where(want == row, 1.0, 0.0).astype(BF16)
            got = jnp.dot(hot_ref[...], rhs, preferred_element_type=F32)
            start = pl.multiple_of(plane * FACE + part * THIRD, 16)
            out_ref[pl.ds(start, THIRD), :] = got.astype(BF16)
        return 0

    lax.fori_loop(0, EDGE, step, 0)


def hand_back(field, connectivity):
    index = connectivity.reshape(CELLS, EDGE, QUAD).transpose(1, 0, 2).reshape(EDGE, CELLS * QUAD)
    return pl.pallas_call(
        return_kernel,
        name="hand_back",
        out_shape=jax.ShapeDtypeStruct((NODES, COLS), BF16),
        in_specs=[VMEM] * 2,
        out_specs=VMEM,
        scratch_shapes=[
            pltpu.VMEM((THIRD, CELLS * QUAD), BF16),
            pltpu.VMEM((CELLS * QUAD, COLS), F32),
            pltpu.VMEM((NODES, COLS), F32),
        ],
        compiler_params=BIG,
    )(field, index)


def product_kernel(states_ref, mixed_ref, position_ref, kept_ref, sent_ref, inner_ref, outer_ref):
    odd = position_ref[0] % 2 == 1
    for band in range(BANDS):
        rows = slice(band * COLS, (band + 1) * COLS)
        inner_ref[rows, :] = jnp.transpose(mixed_ref[band, OUTER_BLOCK : OUTER_BLOCK + INNER_BLOCK, :])
        outer_ref[rows, :] = jnp.transpose(mixed_ref[band, OUTER_BLOCK + INNER_BLOCK :, :])

    def step(i, _):
        inner = jnp.concatenate([states_ref[2 * i], states_ref[2 * i + 1]], axis=1)
        outer = jnp.concatenate([mixed_ref[2 * i, :OUTER_BLOCK, :], mixed_ref[2 * i + 1, :OUTER_BLOCK, :]], axis=1)
        product = jnp.dot(inner_ref[...], inner, preferred_element_type=F32)
        product += jnp.dot(outer_ref[...], outer, preferred_element_type=F32)
        half = COLS // 2
        for band in range(BANDS):
            for part in range(2):
                columns = slice(part * COLS, (part + 1) * COLS)
                first = product[band * COLS : band * COLS + half, columns]
                second = product[band * COLS + half : (band + 1) * COLS, columns]
                kept_ref[band, 2 * i + part] = jnp.where(odd, second, first).astype(BF16)
                sent_ref[band, 2 * i + part] = jnp.where(odd, first, second).astype(BF16)
        return 0

    lax.fori_loop(0, BANDS // 2, step, 0)


def project(states, mixed, position):
    count = lax.axis_size("space")
    halves = count // 2
    shape = jax.ShapeDtypeStruct((halves, BANDS, COLS // 2, COLS), BF16)
    kept, sent = pl.pallas_call(
        product_kernel,
        name="products",
        out_shape=(shape, shape),
        in_specs=[VMEM] * 2 + [SMEM],
        out_specs=(VMEM,) * 2,
        scratch_shapes=[
            pltpu.VMEM((BANDS * COLS, INNER_BLOCK), BF16),
            pltpu.VMEM((BANDS * COLS, OUTER_BLOCK), BF16),
        ],
        compiler_params=BIG,
    )(states, mixed, position)
    got = lax.ppermute(sent, "space", [(i, i ^ 1) for i in range(count)])
    both = (kept.astype(F32) + got.astype(F32)).astype(BF16).reshape(halves * BANDS, COLS // 2, COLS)
    groups = [[(2 * half + part) * BANDS + band for half in range(halves) for band in range(BANDS)] for part in range(2)]
    arrived = lax.all_to_all(both, ("space", "band"), split_axis=0, concat_axis=0, tiled=True, axis_index_groups=groups)
    return arrived.astype(F32).sum(axis=0).T


def swap_faces(near, far):
    count = lax.axis_size("space")
    apart = [(i, i + 1) for i in range(1, count - 1, 2)]
    beside = [(i, i + 1) for i in range(0, count, 2)]
    both_ways = lambda pairs: pairs + [(j, i) for i, j in pairs]
    near, far = lax.optimization_barrier((near, far))
    from_near = lax.ppermute(near, "space", both_ways(beside))
    from_far = lax.ppermute(far, "space", both_ways(apart))
    return from_near, from_far


def local(states, potential, cell_matrix, cell_scale, connectivity, lower_bound, upper_bound):
    bounds = (lower_bound, upper_bound)
    position = lax.axis_index("space").astype(jnp.int32).reshape(1)
    count = lax.axis_size("space")
    field, pot, mat, full, inner, outer = gather(states, potential, connectivity, cell_matrix, bounds)
    near, far = first_faces(field, full, cell_scale, position)
    prev = None
    for stage in range(1, STEPS + 1):
        got = swap_faces(near, far)
        part, sums, *early = cells(stage, field, prev, pot, mat, inner, bounds, cell_scale)
        prev = field
        if early:
            got, early = lax.optimization_barrier((got, early))
        field, *plain, _, near, far = faces(stage, part, got, bounds, position, outer, cell_scale, sums)
    node_states = lax.all_to_all(
        early[0].reshape(BANDS, INNER_BLOCK, COLS), "band", split_axis=0, concat_axis=0, tiled=True)
    current, edge = plain
    got = swap_faces(near, far)
    part, blocks = cells(STEPS + 1, current, None, pot, mat, None, bounds, cell_scale, edge)
    blocks, = faces(STEPS + 1, part, got, bounds, position, blocks=blocks)
    blocks, current = lax.optimization_barrier((blocks, current))
    filtered = hand_back(current, connectivity)
    mixed = lax.all_to_all(blocks.reshape(BANDS, BLOCK, COLS), "band", split_axis=0, concat_axis=0, tiled=True)
    totals = project(node_states, mixed, position)
    global_count = FACE * ((EDGE - 1) * count + 1)
    return filtered, totals / global_count


def solution(mesh):
    placed = (P("space", "band"), P("space"), P(), P("space"), P("space", None), P(), P())
    return jax.shard_map(
        local,
        mesh=mesh,
        in_specs=placed,
        out_specs=(P("space", "band"), P("band", "space")),
        check_vma=False,
    )
```

```python
import functools

import jax
import jax.numpy as jnp
from jax import lax
from jax.experimental import pallas as pl
from jax.experimental.pallas import tpu as pltpu
from jax.sharding import PartitionSpec as P

EDGE = 8
SLAB_XY = 5
STEPS = 4
CELLS = SLAB_XY * SLAB_XY
PAIRS = (CELLS + 1) // 2
CELL_NODES = EDGE**3
SIDE = (EDGE - 1) * SLAB_XY + 1
FACE = SIDE * SIDE
NODES = FACE * EDGE
COLS = 128
SLABS = 16
GROUP = 144
BANDS = 8
INNER = (EDGE - 2) * FACE
INNER_BLOCK = 976
OUTER = FACE + FACE // 2
OUTER_BLOCK = 256
BLOCK = INNER_BLOCK + 2 * OUTER_BLOCK
GATHER_PARTS = ((0, CELLS),)
QUAD = EDGE * EDGE
THIRDS = 3
THIRD = FACE // THIRDS
F32 = jnp.float32
BF16 = jnp.bfloat16
VMEM = pl.BlockSpec(memory_space=pltpu.VMEM)
SMEM = pl.BlockSpec(memory_space=pltpu.SMEM)
HBM = pl.BlockSpec(memory_space=pltpu.HBM)
BIG = pltpu.CompilerParams(vmem_limit_bytes=24 * 1024 * 1024)
SMALL = pltpu.CompilerParams(vmem_limit_bytes=8 * 1024 * 1024)


def first_row(cell_y, cell_x, j):
    return (((EDGE - 1) * cell_y + j) * SIDE + (EDGE - 1) * cell_x) * EDGE


def gather_kernel(states_hbm, pot_ref, index_hbm, matrix_hbm, low_ref, high_ref, field_ref, pot_out_ref, mat_ref,
                  full_ref, inner_ref, outer_ref, rhs_ref, hot_ref, column_ref, states_ref, index_ref, matrix_ref, sems):
    index_copy = pltpu.make_async_copy(index_hbm, index_ref, sems.at[0])
    matrix_copy = pltpu.make_async_copy(matrix_hbm, matrix_ref, sems.at[1])
    states_copy = pltpu.make_async_copy(states_hbm, states_ref, sems.at[2])
    index_copy.start()
    matrix_copy.start()
    states_copy.start()
    index_copy.wait()
    for cell_y in range(SLAB_XY):
        five = index_ref[cell_y * SLAB_XY : (cell_y + 1) * SLAB_XY, :].astype(F32)
        five = jnp.concatenate([five, jnp.zeros((EDGE - SLAB_XY, CELL_NODES), F32)], axis=0)
        column_ref[cell_y * CELL_NODES : (cell_y + 1) * CELL_NODES, :EDGE] = jnp.transpose(five)
    pot = jnp.transpose(pot_ref[...])
    high = pot.astype(BF16)
    rest = pot - high.astype(F32)
    mid = rest.astype(BF16)
    low = (rest - mid.astype(F32)).astype(BF16)
    rhs_ref[:, COLS:] = jnp.concatenate(
        [high, mid, low, jnp.zeros((FACE, COLS - 3 * EDGE), BF16)], axis=1)

    matrix_copy.wait()
    new = lax.broadcasted_iota(jnp.int32, (CELL_NODES, CELL_NODES), 0)
    old = lax.broadcasted_iota(jnp.int32, (CELL_NODES, CELL_NODES), 1)
    order = jnp.where(old == (new % EDGE) * QUAD + new // EDGE, 1.0, 0.0).astype(BF16)
    across = (((1,), (1,)), ((), ()))
    turned = lax.dot_general(matrix_ref[...], order, across, preferred_element_type=F32).astype(BF16)
    mat_ref[...] = jnp.dot(order, turned, preferred_element_type=F32).astype(BF16)
    for side, first in enumerate((0, CELL_NODES - QUAD)):
        rows = pl.ds(side * QUAD, QUAD)
        face_rows = turned[first : first + QUAD, :].astype(F32)
        z = lax.broadcasted_iota(jnp.int32, (QUAD, CELL_NODES), 1) % EDGE
        full_ref[rows, :] = face_rows.astype(BF16)
        inner_ref[rows, :] = jnp.where((z > 0) & (z < EDGE - 1), face_rows, 0.0).astype(BF16)
        outer_ref[rows, :QUAD] = matrix_ref[first : first + QUAD, :QUAD]
        outer_ref[rows, QUAD:] = matrix_ref[first : first + QUAD, CELL_NODES - QUAD :]
    lead, shift = factors((low_ref, high_ref), 2)
    states_copy.wait()

    def step(plane, _):
        rhs_ref[:, :COLS] = states_ref[pl.ds(pl.multiple_of(plane * FACE, 16), FACE), :]
        start = (plane * FACE).astype(F32)
        lane = lax.broadcasted_iota(jnp.int32, (EDGE, COLS), 1)
        mine = (lane % EDGE == plane) & (lane < 3 * EDGE)
        for first, last in GATHER_PARTS:
            at = 0
            for cell in range(first, last):
                cell_y, cell_x = cell // SLAB_XY, cell % SLAB_XY
                rows = QUAD if cell_y == SLAB_XY - 1 else QUAD - EDGE
                lanes = lax.broadcasted_iota(jnp.int32, (rows, FACE), 1).astype(F32)
                want = column_ref[pl.ds(pl.multiple_of(cell_y * CELL_NODES + plane * QUAD, 8), rows), cell_x : cell_x + 1] - start
                hot_ref[at : at + rows, :] = jnp.where(want == lanes, 1.0, 0.0).astype(BF16)
                at += rows
            got = jnp.dot(hot_ref[:at, :], rhs_ref[...], preferred_element_type=F32)
            at = 0
            for cell in range(first, last):
                cell_y, cell_x = cell // SLAB_XY, cell % SLAB_XY
                for j in range(EDGE if cell_y == SLAB_XY - 1 else EDGE - 1):
                    rows = pl.ds(first_row(cell_y, cell_x, j) + plane, EDGE, stride=EDGE)
                    field_ref[rows, :] = got[at : at + EDGE, :COLS]
                    value = jnp.sum(jnp.where(mine, got[at : at + EDGE, COLS:], 0.0), axis=1, keepdims=True)
                    pot_out_ref[rows, :] = lead * value - shift
                    at += EDGE
        return 0

    lax.fori_loop(0, EDGE, step, 0)


def in_hbm(x):
    return pltpu.with_memory_space_constraint(x, pltpu.HBM)


def gather(states, potential, connectivity, matrix, bounds):
    return pl.pallas_call(
        gather_kernel,
        name="gather_states",
        out_shape=(
            pltpu.VMEM((NODES, COLS), F32),
            pltpu.VMEM((NODES, COLS), F32),
            pltpu.VMEM((CELL_NODES, CELL_NODES), BF16),
            pltpu.VMEM((2 * QUAD, CELL_NODES), BF16),
            pltpu.VMEM((2 * QUAD, CELL_NODES), BF16),
            pltpu.VMEM((2 * QUAD, 2 * QUAD), BF16),
        ),
        in_specs=[HBM, VMEM, HBM, HBM] + [SMEM] * 2,
        out_specs=(VMEM,) * 6,
        scratch_shapes=[
            pltpu.VMEM((FACE, 2 * COLS), BF16),
            pltpu.VMEM((CELLS * QUAD, FACE), BF16),
            pltpu.VMEM((SLAB_XY * CELL_NODES, COLS), F32),
            pltpu.VMEM((NODES, COLS), BF16),
            pltpu.VMEM((CELLS, CELL_NODES), jnp.int32),
            pltpu.VMEM((CELL_NODES, CELL_NODES), BF16),
            pltpu.SemaphoreType.DMA((3,)),
        ],
        compiler_params=BIG,
    )(in_hbm(states), potential.reshape(EDGE, FACE), in_hbm(connectivity), in_hbm(matrix), *bounds)


def half_width_of(bounds):
    low, high = bounds
    return jnp.full((1, COLS), (high[0] - low[0]) * 0.5, F32)


def factors(bounds, stage):
    if stage > STEPS:
        return jnp.ones((1, COLS), F32), None
    low, high = bounds
    center = (high[0] + low[0]) * 0.5
    lead = (1.0 if stage == 1 else 2.0) / half_width_of(bounds)
    return lead, lead * center


def pair_cells(pair, scale_ref):
    for half in range(2):
        index = 2 * pair + half
        cell = jnp.minimum(index, CELLS - 1)
        yield half, cell // SLAB_XY, cell % SLAB_XY, jnp.where(index < CELLS, scale_ref[cell], 0.0)


def for_pairs(work, group):
    def step(i, _):
        work(*[group * i + k for k in range(group)])
        return 0

    lax.fori_loop(0, PAIRS // group, step, 0)
    if PAIRS % group:
        work(*[jnp.int32(pair) for pair in range(PAIRS - PAIRS % group, PAIRS)])


def cell_blocks(field_ref, pair, scale_ref):
    columns = []
    for half, cell_y, cell_x, _ in pair_cells(pair, scale_ref):
        pieces = []
        for j in range(EDGE):
            rows = pl.ds(pl.multiple_of(first_row(cell_y, cell_x, j), EDGE), QUAD)
            pieces.append(field_ref[rows, :].astype(BF16))
        columns.append(jnp.concatenate(pieces, axis=0))
    return jnp.concatenate(columns, axis=1)


def add_faces(sums_ref, product, pair, scale_ref):
    for half, cell_y, cell_x, scale in pair_cells(pair, scale_ref):
        for side in range(2):
            for j in range(EDGE):
                at = side * QUAD + j * EDGE
                rows = pl.ds(side * FACE + ((EDGE - 1) * cell_y + j) * SIDE + (EDGE - 1) * cell_x, EDGE)
                sums_ref[rows, :] += scale * product[at : at + EDGE, half * COLS : (half + 1) * COLS]


def spread_faces(field_ref, matrix_ref, scale_ref, sums_ref):
    sums_ref[...] = jnp.zeros_like(sums_ref)

    def spread(*pairs):
        blocks = [cell_blocks(field_ref, pair, scale_ref) for pair in pairs]
        products = [jnp.dot(matrix_ref[...], block, preferred_element_type=F32) for block in blocks]
        for pair, product in zip(pairs, products):
            add_faces(sums_ref, product, pair, scale_ref)

    for_pairs(spread, 3)


def hand_out(sums_ref, odd, near_out, far_out):
    near_out[...] = sums_ref[pl.ds(pl.multiple_of((1 - odd) * FACE, 16), FACE), :].astype(BF16)
    far_out[...] = sums_ref[pl.ds(pl.multiple_of(odd * FACE, 16), FACE), :].astype(BF16)


def first_faces_kernel(field_ref, full_ref, scale_ref, position_ref, near_out, far_out, sums_ref):
    spread_faces(field_ref, full_ref, scale_ref, sums_ref)
    hand_out(sums_ref, position_ref[0] % 2, near_out, far_out)


def first_faces(field, full, scale, position):
    return pl.pallas_call(
        first_faces_kernel,
        name="first_faces",
        out_shape=(jax.ShapeDtypeStruct((FACE, COLS), BF16),) * 2,
        in_specs=[VMEM] * 2 + [SMEM] * 2,
        out_specs=(VMEM,) * 2,
        scratch_shapes=[pltpu.VMEM((2 * FACE, COLS), F32)],
        compiler_params=SMALL,
    )(field, full, scale, position)


def put_inner(field_ref, store):
    def planes(i, _):
        for z in range(1, EDGE - 1):
            for part in range(3):
                node = i * 48 + part * 16
                halves = [field_ref[pl.ds((node + k) * EDGE + z, EDGE, stride=EDGE), :] for k in (0, EDGE)]
                store((z - 1) * FACE + node, jnp.concatenate(halves, axis=0).astype(BF16))
        return 0

    lax.fori_loop(0, FACE // 48, planes, 0)
    for row in range(INNER, BANDS * INNER_BLOCK, 16):
        store(row, jnp.zeros((16, COLS), BF16))


def put_outer(face_ref, odd, far_weight, store):
    def rows(i, _):
        for part in range(4):
            row = (i * 4 + part) * 16
            far = row < FACE
            near_at = (1 - odd) * FACE + odd * (FACE // 2) + row - FACE
            at = jnp.where(far, odd * FACE + row, jnp.minimum(near_at, 2 * FACE - 16))
            value = face_ref[pl.ds(pl.multiple_of(at, EDGE), 16), :]
            if far_weight is not None:
                value = value * jnp.where(far, far_weight, 1.0)
            index = lax.broadcasted_iota(jnp.int32, (16, COLS), 0) + row
            store(row, jnp.where(index < OUTER, value, 0.0).astype(BF16))
        return 0

    lax.fori_loop(0, BANDS * OUTER_BLOCK // 64, rows, 0)


def faces_kernel(stage, *refs):
    late, spread = stage >= STEPS, stage <= STEPS
    refs = list(refs)
    field_ref, near_in, far_in, low_ref, high_ref, position_ref = refs[:6]
    refs = refs[6:]
    if spread:
        outer_ref, scale_ref, _ = refs[:3]
        refs = refs[3:]
        if late:
            face_ref, edge_ref, sums_ref, near_out, far_out = refs
        else:
            out_ref, sums_ref, near_out, far_out, face_ref = refs
    else:
        _, block_ref, face_ref, edge_ref, sems = refs
    odd = position_ref[0] % 2
    lead, _ = factors((low_ref, high_ref), stage)

    def settle_rows(i, _):
        for face_in, plane, side in ((near_in, (EDGE - 1) * (1 - odd), 1 - odd), (far_in, (EDGE - 1) * odd, odd)):
            got = face_in[pl.ds(pl.multiple_of(i * GROUP, 16), GROUP), :].astype(F32)
            for part in range(GROUP // EDGE):
                here = pl.ds(pl.multiple_of(side * FACE + i * GROUP + part * EDGE, EDGE), EDGE)
                rows = here if late else pl.ds((i * (GROUP // EDGE) + part) * QUAD + plane, EDGE, stride=EDGE)
                value = field_ref[rows, :] + lead * got[part * EDGE : (part + 1) * EDGE, :]
                value = value.astype(BF16).astype(F32)
                if not late:
                    out_ref[rows, :] = value
                face_ref[here, :] = value
        return 0

    lax.fori_loop(0, FACE // GROUP, settle_rows, 0)
    if spread:

        def face_blocks(pair):
            columns = []
            for half, cell_y, cell_x, _ in pair_cells(pair, scale_ref):
                pieces = []
                for side in range(2):
                    for j in range(EDGE):
                        rows = pl.ds(side * FACE + ((EDGE - 1) * cell_y + j) * SIDE + (EDGE - 1) * cell_x, EDGE)
                        pieces.append(face_ref[rows, :])
                columns.append(jnp.concatenate(pieces, axis=0).astype(BF16))
            return jnp.concatenate(columns, axis=1)

        def spread_outer(*pairs):
            blocks = [face_blocks(pair) for pair in pairs]
            products = [jnp.dot(outer_ref[...], block, preferred_element_type=F32) for block in blocks]
            for pair, product in zip(pairs, products):
                add_faces(sums_ref, product, pair, scale_ref)

        for_pairs(spread_outer, 3)
        hand_out(sums_ref, odd, near_out, far_out)
    if late:
        ends = (position_ref[0] == 0) | (position_ref[0] == SLABS - 1)
        far_weight = jnp.where(ends, 1.0, 0.5)

        def put_edge(row, value):
            edge_ref[pl.ds(pl.multiple_of(row, 16), 16), :] = value

        put_outer(face_ref, odd, None if spread else far_weight, put_edge)
    if not spread:
        copies = [
            pltpu.make_async_copy(
                edge_ref.at[pl.ds(band * OUTER_BLOCK, OUTER_BLOCK), :],
                block_ref.at[pl.ds(band * BLOCK + OUTER_BLOCK + INNER_BLOCK, OUTER_BLOCK), :],
                sems.at[band],
            )
            for band in range(BANDS)
        ]
        for copy in copies:
            copy.start()
        for copy in copies:
            copy.wait()


def faces(stage, part, got, bounds, position, outer=None, scale=None, sums=None, blocks=None):
    args = [part, *got, *bounds, position]
    specs = [VMEM] * 3 + [SMEM] * 3
    faces_shape = (2 * FACE, COLS)
    scratch = []
    if stage < STEPS:
        outs = [pltpu.VMEM((NODES, COLS), F32), pltpu.VMEM(faces_shape, F32)]
        aliases = {0: 0, 8: 1}
        scratch = [pltpu.VMEM(faces_shape, F32)]
    elif stage == STEPS:
        outs = [
            jax.ShapeDtypeStruct(faces_shape, F32),
            jax.ShapeDtypeStruct((BANDS * OUTER_BLOCK, COLS), BF16),
            jax.ShapeDtypeStruct(faces_shape, F32),
        ]
        aliases = {8: 2}
    else:
        args.append(in_hbm(blocks))
        outs = [pltpu.HBM((BANDS * BLOCK, COLS), BF16)]
        aliases = {6: 0}
        scratch = [
            pltpu.VMEM(faces_shape, F32),
            pltpu.VMEM((BANDS * OUTER_BLOCK, COLS), BF16),
            pltpu.SemaphoreType.DMA((BANDS,)),
        ]
    if stage <= STEPS:
        args += [outer, scale, sums]
        specs += [VMEM, SMEM, VMEM]
        outs += [jax.ShapeDtypeStruct((FACE, COLS), BF16)] * 2
    else:
        specs.append(HBM)
    return pl.pallas_call(
        functools.partial(faces_kernel, stage),
        name="faces",
        out_shape=tuple(outs),
        in_specs=specs,
        out_specs=((VMEM,) * len(outs)) if stage <= STEPS else (HBM,),
        scratch_shapes=scratch,
        input_output_aliases=aliases,
        compiler_params=SMALL if stage < STEPS else BIG,
    )(*args)


def rebuild(inner_ref, settled_ref, field_ref):
    def nodes(i, _):
        for part in range(3):
            node = i * 48 + part * 16
            for z in range(EDGE):
                for k in (0, EDGE):
                    if z in (0, EDGE - 1):
                        at = pl.ds(pl.multiple_of((z // (EDGE - 1)) * FACE + node + k, EDGE), EDGE)
                        value = settled_ref[at, :]
                    elif k == 0:
                        both = inner_ref[pl.ds(pl.multiple_of((z - 1) * FACE + node, 16), 16), :].astype(F32)
                        value = both[:EDGE]
                    else:
                        value = both[EDGE:]
                    field_ref[pl.ds((node + k) * EDGE + z, EDGE, stride=EDGE), :] = value
        return 0

    lax.fori_loop(0, FACE // 48, nodes, 0)


def cells_kernel(stage, *refs):
    refs = list(refs)
    last = stage > STEPS
    if last:
        (early_ref, settled_ref, edge_ref, pot_ref, mat_ref, low_ref, high_ref, scale_ref,
         rim_ref, plain_ref, block_ref, field_ref, out_ref) = refs
        for band in range(BANDS):
            block_ref[band * BLOCK : band * BLOCK + OUTER_BLOCK, :] = (
                edge_ref[band * OUTER_BLOCK : (band + 1) * OUTER_BLOCK, :])
        rebuild(early_ref, settled_ref, field_ref)
    else:
        field_ref = refs.pop(0)
        if stage > 1:
            refs.pop(0)
        pot_ref, mat_ref, inner_ref, low_ref, high_ref, scale_ref, out_ref, sums_ref, *more = refs
        if more:
            early_ref, rim_ref = more
    in_place = 1 < stage <= STEPS
    bounds = (low_ref, high_ref)
    lead, _ = factors(bounds, stage)
    if in_place:
        lead = -lead
    else:
        out_ref[...] = jnp.zeros_like(out_ref)

    def multiply(*pairs):
        blocks = [cell_blocks(field_ref, pair, scale_ref) for pair in pairs]
        products = [jnp.dot(mat_ref[...], block, preferred_element_type=F32) for block in blocks]
        for pair, product in zip(pairs, products):
            for half, cell_y, cell_x, scale in pair_cells(pair, scale_ref):
                factor = lead * scale
                for j in range(EDGE):
                    rows = pl.ds(pl.multiple_of(first_row(cell_y, cell_x, j), EDGE), QUAD)
                    out_ref[rows, :] += factor * product[j * QUAD : (j + 1) * QUAD, half * COLS : (half + 1) * COLS]

    for_pairs(multiply, 4)
    plane = lax.broadcasted_iota(jnp.int32, (EDGE, COLS), 0)
    inside = (plane > 0) & (plane < EDGE - 1)
    half_width = half_width_of(bounds) * 0.5
    center = jnp.full((1, COLS), (high_ref[0] + low_ref[0]) * 0.5, F32)

    def finish(i, _):
        for part in range(GROUP // EDGE):
            rows = pl.ds(pl.multiple_of(i * GROUP + part * EDGE, EDGE), EDGE)
            shifted = pot_ref[rows, :]
            if stage == 1:
                shifted = shifted * 0.5
            elif last:
                shifted = shifted * half_width + center
            value = shifted * field_ref[rows, :]
            value = value - out_ref[rows, :] if in_place else value + out_ref[rows, :]
            out_ref[rows, :] = jnp.where(inside, value.astype(BF16).astype(F32), value)
        return 0

    lax.fori_loop(0, NODES // GROUP, finish, 0)

    def put(row, value):
        if last:
            at = (row // INNER_BLOCK) * BLOCK + OUTER_BLOCK + row % INNER_BLOCK
            block_ref[pl.ds(pl.multiple_of(at, 16), 16), :] = value
        else:
            early_ref[pl.ds(pl.multiple_of(row, 16), 16), :] = value

    def put_rim(i, _):
        for side in range(2):
            for part in range(GROUP // EDGE):
                node = i * GROUP + part * EDGE
                rows = pl.ds(node * EDGE + side * (EDGE - 1), EDGE, stride=EDGE)
                rim_ref[pl.ds(pl.multiple_of(side * FACE + node, EDGE), EDGE), :] = out_ref[rows, :]
        return 0

    if stage >= STEPS:
        put_inner(out_ref, put)
        lax.fori_loop(0, FACE // GROUP, put_rim, 0)
    if last:

        def emit_rows(i, _):
            rows = pl.ds(pl.multiple_of(i * 2 * GROUP, 2 * GROUP), 2 * GROUP)
            plain_ref[rows, :] = field_ref[rows, :].astype(BF16)
            return 0

        lax.fori_loop(0, NODES // (2 * GROUP), emit_rows, 0)
    else:
        spread_faces(out_ref, inner_ref, scale_ref, sums_ref)


def cells(stage, field, prev, pot, mat, inner, bounds, scale):
    args = [field] + ([prev] if stage > 1 else []) + [pot, mat, inner]
    faces_shape = (2 * FACE, COLS)
    outs = [pltpu.VMEM((NODES, COLS), F32)]
    if stage < STEPS:
        outs.append(pltpu.VMEM(faces_shape, F32))
    else:
        outs += [
            pltpu.HBM(faces_shape, F32),
            pltpu.HBM((BANDS * INNER_BLOCK, COLS), BF16),
            pltpu.HBM(faces_shape, F32),
        ]
    return pl.pallas_call(
        functools.partial(cells_kernel, stage),
        name="cells",
        out_shape=tuple(outs),
        in_specs=[VMEM] * len(args) + [SMEM] * 3,
        out_specs=(VMEM,) * len(outs),
        input_output_aliases={1: 0} if stage > 1 else {},
        compiler_params=SMALL if stage < STEPS else BIG,
    )(*args, *bounds, scale)


def last_cells(early, settled, edge, pot, mat, bounds, scale):
    return pl.pallas_call(
        functools.partial(cells_kernel, STEPS + 1),
        name="last_cells",
        out_shape=(
            pltpu.VMEM((2 * FACE, COLS), F32),
            jax.ShapeDtypeStruct((NODES, COLS), BF16),
            jax.ShapeDtypeStruct((BANDS * BLOCK, COLS), BF16),
        ),
        in_specs=[VMEM] * 5 + [SMEM] * 3,
        out_specs=(VMEM,) * 3,
        scratch_shapes=[pltpu.VMEM((NODES, COLS), F32)] * 2,
        compiler_params=pltpu.CompilerParams(vmem_limit_bytes=32 * 1024 * 1024),
    )(early, settled, edge, pot, mat, *bounds, scale)


def return_kernel(plain_ref, index_ref, out_ref, hot_ref, rhs_ref, field_ref):
    field_ref[...] = plain_ref[...].astype(F32)
    j = lax.broadcasted_iota(jnp.int32, (EDGE, COLS), 0)

    def step(plane, _):
        for cell in range(CELLS):
            cell_y, cell_x = cell // SLAB_XY, cell % SLAB_XY
            for k in range(EDGE):
                at = cell * QUAD + k * EDGE
                value = field_ref[pl.ds(first_row(cell_y, cell_x, k) + plane, EDGE, stride=EDGE), :]
                if cell_y > 0 and k == 0:
                    value = jnp.zeros_like(value)
                elif cell_x > 0:
                    value = jnp.where(j == 0, 0.0, value)
                rhs_ref[at : at + EDGE, :] = value
        want = index_ref[pl.ds(plane, 1), :].astype(F32) - (plane * FACE).astype(F32)
        rhs = rhs_ref[...].astype(BF16)
        for part in range(THIRDS):
            row = lax.broadcasted_iota(jnp.int32, (THIRD, CELLS * QUAD), 0).astype(F32) + float(part * THIRD)
            hot_ref[...] = jnp.where(want == row, 1.0, 0.0).astype(BF16)
            got = jnp.dot(hot_ref[...], rhs, preferred_element_type=F32)
            start = pl.multiple_of(plane * FACE + part * THIRD, 16)
            out_ref[pl.ds(start, THIRD), :] = got.astype(BF16)
        return 0

    lax.fori_loop(0, EDGE, step, 0)


def hand_back(field, connectivity):
    index = connectivity.reshape(CELLS, EDGE, QUAD).transpose(1, 0, 2).reshape(EDGE, CELLS * QUAD)
    return pl.pallas_call(
        return_kernel,
        name="hand_back",
        out_shape=jax.ShapeDtypeStruct((NODES, COLS), BF16),
        in_specs=[VMEM] * 2,
        out_specs=VMEM,
        scratch_shapes=[
            pltpu.VMEM((THIRD, CELLS * QUAD), BF16),
            pltpu.VMEM((CELLS * QUAD, COLS), F32),
            pltpu.VMEM((NODES, COLS), F32),
        ],
        compiler_params=BIG,
    )(field, index)


def product_kernel(factor, states_ref, mixed_ref, position_ref, kept_ref, sent_ref, inner_ref, outer_ref):
    odd = position_ref[0] % 2 == 1
    for band in range(BANDS):
        rows = slice(band * COLS, (band + 1) * COLS)
        inner_ref[rows, :] = jnp.transpose(mixed_ref[band, OUTER_BLOCK : OUTER_BLOCK + INNER_BLOCK, :])
        outer_ref[rows, :] = jnp.transpose(mixed_ref[band, OUTER_BLOCK + INNER_BLOCK :, :])

    def step(i, _):
        inner = jnp.concatenate([states_ref[2 * i], states_ref[2 * i + 1]], axis=1)
        outer = jnp.concatenate([mixed_ref[2 * i, :OUTER_BLOCK, :], mixed_ref[2 * i + 1, :OUTER_BLOCK, :]], axis=1)
        product = jnp.dot(inner_ref[...], inner, preferred_element_type=F32)
        product = (product + jnp.dot(outer_ref[...], outer, preferred_element_type=F32)) * factor
        half = COLS // 2
        for band in range(BANDS):
            for part in range(2):
                columns = slice(part * COLS, (part + 1) * COLS)
                first = product[band * COLS : band * COLS + half, columns]
                second = product[band * COLS + half : (band + 1) * COLS, columns]
                kept_ref[band, 2 * i + part] = jnp.where(odd, second, first).astype(BF16)
                sent_ref[band, 2 * i + part] = jnp.where(odd, first, second).astype(BF16)
        return 0

    lax.fori_loop(0, BANDS // 2, step, 0)


def project(states, mixed, position):
    count = lax.axis_size("space")
    halves = count // 2
    factor = 1.0 / (FACE * ((EDGE - 1) * count + 1))
    shape = jax.ShapeDtypeStruct((halves, BANDS, COLS // 2, COLS), BF16)
    kept, sent = pl.pallas_call(
        functools.partial(product_kernel, factor),
        name="products",
        out_shape=(shape, shape),
        in_specs=[VMEM] * 2 + [SMEM],
        out_specs=(VMEM,) * 2,
        scratch_shapes=[
            pltpu.VMEM((BANDS * COLS, INNER_BLOCK), BF16),
            pltpu.VMEM((BANDS * COLS, OUTER_BLOCK), BF16),
        ],
        compiler_params=BIG,
    )(states, mixed, position)
    got = lax.ppermute(sent, "space", [(i, i ^ 1) for i in range(count)])
    both = (kept.astype(F32) + got.astype(F32)).astype(BF16).reshape(halves * BANDS, COLS // 2, COLS)
    groups = [[(2 * half + part) * BANDS + band for half in range(halves) for band in range(BANDS)] for part in range(2)]
    arrived = lax.all_to_all(both, ("space", "band"), split_axis=0, concat_axis=0, tiled=True, axis_index_groups=groups)
    return arrived.astype(F32).sum(axis=0).T


def swap_faces(near, far):
    count = lax.axis_size("space")
    apart = [(i, i + 1) for i in range(1, count - 1, 2)]
    beside = [(i, i + 1) for i in range(0, count, 2)]
    both_ways = lambda pairs: pairs + [(j, i) for i, j in pairs]
    near, far = lax.optimization_barrier((near, far))
    from_near = lax.ppermute(near, "space", both_ways(beside))
    from_far = lax.ppermute(far, "space", both_ways(apart))
    return from_near, from_far


def local(states, potential, cell_matrix, cell_scale, connectivity, lower_bound, upper_bound):
    bounds = (lower_bound, upper_bound)
    position = lax.axis_index("space").astype(jnp.int32).reshape(1)
    count = lax.axis_size("space")
    field, pot, mat, full, inner, outer = gather(states, potential, connectivity, cell_matrix, bounds)
    near, far = first_faces(field, full, cell_scale, position)
    prev = None
    for stage in range(1, STEPS):
        got = swap_faces(near, far)
        part, sums = cells(stage, field, prev, pot, mat, inner, bounds, cell_scale)
        prev = field
        field, _, near, far = faces(stage, part, got, bounds, position, outer, cell_scale, sums)
    got = swap_faces(near, far)
    _, sums, early, rim = cells(STEPS, field, prev, pot, mat, inner, bounds, cell_scale)
    got, early = lax.optimization_barrier((got, early))
    node_states = lax.all_to_all(
        early.reshape(BANDS, INNER_BLOCK, COLS), "band", split_axis=0, concat_axis=0, tiled=True)
    settled, edge, _, near, far = faces(STEPS, rim, got, bounds, position, outer, cell_scale, sums)
    got = swap_faces(near, far)
    rim, current, blocks = last_cells(early, settled, edge, pot, mat, bounds, cell_scale)
    blocks, = faces(STEPS + 1, rim, got, bounds, position, blocks=blocks)
    blocks, current = lax.optimization_barrier((blocks, current))
    filtered = hand_back(current, connectivity)
    mixed = lax.all_to_all(blocks.reshape(BANDS, BLOCK, COLS), "band", split_axis=0, concat_axis=0, tiled=True)
    totals = project(node_states, mixed, position)
    return filtered, totals


def solution(mesh):
    placed = (P("space", "band"), P("space"), P(), P("space"), P("space", None), P(), P())
    return jax.shard_map(
        local,
        mesh=mesh,
        in_specs=placed,
        out_specs=(P("space", "band"), P("band", "space")),
        check_vma=False,
    )
```

```python
import functools

import jax
import jax.numpy as jnp
from jax import lax
from jax.experimental import pallas as pl
from jax.experimental.pallas import tpu as pltpu
from jax.sharding import PartitionSpec as P


EDGE = 8
SLAB_XY = 5
STEPS = 4
CELLS = SLAB_XY * SLAB_XY
PAIRS = (CELLS + 1) // 2
CELL_NODES = EDGE**3
SIDE = (EDGE - 1) * SLAB_XY + 1
FACE = SIDE * SIDE
NODES = FACE * EDGE
COLS = 128
SLABS = 16
GROUP = 144
BANDS = 8
INNER = (EDGE - 2) * FACE
INNER_BLOCK = 976
OUTER = FACE + FACE // 2
OUTER_BLOCK = 256
BLOCK = INNER_BLOCK + 2 * OUTER_BLOCK
GATHER_PARTS = ((0, CELLS),)
QUAD = EDGE * EDGE
THIRDS = 3
THIRD = FACE // THIRDS
F32 = jnp.float32
BF16 = jnp.bfloat16
VMEM = pl.BlockSpec(memory_space=pltpu.VMEM)
SMEM = pl.BlockSpec(memory_space=pltpu.SMEM)
HBM = pl.BlockSpec(memory_space=pltpu.HBM)
BIG = pltpu.CompilerParams(vmem_limit_bytes=24 * 1024 * 1024)
SMALL = pltpu.CompilerParams(vmem_limit_bytes=8 * 1024 * 1024)


def first_row(cell_y, cell_x, j):
    return (((EDGE - 1) * cell_y + j) * SIDE + (EDGE - 1) * cell_x) * EDGE


def gather_kernel(states_hbm, pot_ref, index_hbm, matrix_hbm, low_ref, high_ref, field_ref, pot_out_ref, mat_ref,
                  full_ref, inner_ref, outer_ref, rhs_ref, hot_ref, column_ref, states_ref, index_ref, matrix_ref, sems):
    index_copy = pltpu.make_async_copy(index_hbm, index_ref, sems.at[0])
    matrix_copy = pltpu.make_async_copy(matrix_hbm, matrix_ref, sems.at[1])
    states_copy = pltpu.make_async_copy(states_hbm, states_ref, sems.at[2])
    index_copy.start()
    matrix_copy.start()
    states_copy.start()
    index_copy.wait()
    for cell_y in range(SLAB_XY):
        five = index_ref[cell_y * SLAB_XY : (cell_y + 1) * SLAB_XY, :].astype(F32)
        five = jnp.concatenate([five, jnp.zeros((EDGE - SLAB_XY, CELL_NODES), F32)], axis=0)
        column_ref[cell_y * CELL_NODES : (cell_y + 1) * CELL_NODES, :EDGE] = jnp.transpose(five)
    pot = jnp.transpose(pot_ref[...])
    high = pot.astype(BF16)
    rest = pot - high.astype(F32)
    mid = rest.astype(BF16)
    low = (rest - mid.astype(F32)).astype(BF16)
    rhs_ref[:, COLS:] = jnp.concatenate(
        [high, mid, low, jnp.zeros((FACE, COLS - 3 * EDGE), BF16)], axis=1)

    matrix_copy.wait()
    new = lax.broadcasted_iota(jnp.int32, (CELL_NODES, CELL_NODES), 0)
    old = lax.broadcasted_iota(jnp.int32, (CELL_NODES, CELL_NODES), 1)
    order = jnp.where(old == (new % EDGE) * QUAD + new // EDGE, 1.0, 0.0).astype(BF16)
    across = (((1,), (1,)), ((), ()))
    turned = lax.dot_general(matrix_ref[...], order, across, preferred_element_type=F32).astype(BF16)
    mat_ref[...] = jnp.dot(order, turned, preferred_element_type=F32).astype(BF16)
    for side, first in enumerate((0, CELL_NODES - QUAD)):
        rows = pl.ds(side * QUAD, QUAD)
        face_rows = turned[first : first + QUAD, :].astype(F32)
        z = lax.broadcasted_iota(jnp.int32, (QUAD, CELL_NODES), 1) % EDGE
        full_ref[rows, :] = face_rows.astype(BF16)
        inner_ref[rows, :] = jnp.where((z > 0) & (z < EDGE - 1), face_rows, 0.0).astype(BF16)
        outer_ref[rows, :QUAD] = matrix_ref[first : first + QUAD, :QUAD]
        outer_ref[rows, QUAD:] = matrix_ref[first : first + QUAD, CELL_NODES - QUAD :]
    lead, shift = factors((low_ref, high_ref), 2)
    states_copy.wait()

    def step(plane, _):
        rhs_ref[:, :COLS] = states_ref[pl.ds(pl.multiple_of(plane * FACE, 16), FACE), :]
        start = (plane * FACE).astype(F32)
        lane = lax.broadcasted_iota(jnp.int32, (EDGE, COLS), 1)
        mine = (lane % EDGE == plane) & (lane < 3 * EDGE)
        for first, last in GATHER_PARTS:
            at = 0
            for cell in range(first, last):
                cell_y, cell_x = cell // SLAB_XY, cell % SLAB_XY
                rows = QUAD if cell_y == SLAB_XY - 1 else QUAD - EDGE
                lanes = lax.broadcasted_iota(jnp.int32, (rows, FACE), 1).astype(F32)
                want = column_ref[pl.ds(pl.multiple_of(cell_y * CELL_NODES + plane * QUAD, 8), rows), cell_x : cell_x + 1] - start
                hot_ref[at : at + rows, :] = jnp.where(want == lanes, 1.0, 0.0).astype(BF16)
                at += rows
            got = jnp.dot(hot_ref[:at, :], rhs_ref[...], preferred_element_type=F32)
            at = 0
            for cell in range(first, last):
                cell_y, cell_x = cell // SLAB_XY, cell % SLAB_XY
                for j in range(EDGE if cell_y == SLAB_XY - 1 else EDGE - 1):
                    rows = pl.ds(first_row(cell_y, cell_x, j) + plane, EDGE, stride=EDGE)
                    field_ref[rows, :] = got[at : at + EDGE, :COLS]
                    value = jnp.sum(jnp.where(mine, got[at : at + EDGE, COLS:], 0.0), axis=1, keepdims=True)
                    pot_out_ref[rows, :] = lead * value - shift
                    at += EDGE
        return 0

    lax.fori_loop(0, EDGE, step, 0)


def in_hbm(x):
    return pltpu.with_memory_space_constraint(x, pltpu.HBM)


def gather(states, potential, connectivity, matrix, bounds):
    return pl.pallas_call(
        gather_kernel,
        name="gather_states",
        out_shape=(
            pltpu.VMEM((NODES, COLS), F32),
            pltpu.VMEM((NODES, COLS), F32),
            pltpu.VMEM((CELL_NODES, CELL_NODES), BF16),
            pltpu.VMEM((2 * QUAD, CELL_NODES), BF16),
            pltpu.VMEM((2 * QUAD, CELL_NODES), BF16),
            pltpu.VMEM((2 * QUAD, 2 * QUAD), BF16),
        ),
        in_specs=[HBM, VMEM, HBM, HBM] + [SMEM] * 2,
        out_specs=(VMEM,) * 6,
        scratch_shapes=[
            pltpu.VMEM((FACE, 2 * COLS), BF16),
            pltpu.VMEM((CELLS * QUAD, FACE), BF16),
            pltpu.VMEM((SLAB_XY * CELL_NODES, COLS), F32),
            pltpu.VMEM((NODES, COLS), BF16),
            pltpu.VMEM((CELLS, CELL_NODES), jnp.int32),
            pltpu.VMEM((CELL_NODES, CELL_NODES), BF16),
            pltpu.SemaphoreType.DMA((3,)),
        ],
        compiler_params=BIG,
    )(in_hbm(states), potential.reshape(EDGE, FACE), in_hbm(connectivity), in_hbm(matrix), *bounds)


def half_width_of(bounds):
    low, high = bounds
    return jnp.full((1, COLS), (high[0] - low[0]) * 0.5, F32)


def factors(bounds, stage):
    if stage > STEPS:
        return jnp.ones((1, COLS), F32), None
    low, high = bounds
    center = (high[0] + low[0]) * 0.5
    lead = (1.0 if stage == 1 else 2.0) / half_width_of(bounds)
    return lead, lead * center


def pair_cells(pair, scale_ref):
    for half in range(2):
        index = 2 * pair + half
        cell = jnp.minimum(index, CELLS - 1)
        yield half, cell // SLAB_XY, cell % SLAB_XY, jnp.where(index < CELLS, scale_ref[cell], 0.0)


def for_pairs(work, group):
    def step(i, _):
        work(*[group * i + k for k in range(group)])
        return 0

    lax.fori_loop(0, PAIRS // group, step, 0)
    if PAIRS % group:
        work(*[jnp.int32(pair) for pair in range(PAIRS - PAIRS % group, PAIRS)])


def cell_blocks(field_ref, pair, scale_ref):
    columns = []
    for half, cell_y, cell_x, _ in pair_cells(pair, scale_ref):
        pieces = []
        for j in range(EDGE):
            rows = pl.ds(pl.multiple_of(first_row(cell_y, cell_x, j), EDGE), QUAD)
            pieces.append(field_ref[rows, :].astype(BF16))
        columns.append(jnp.concatenate(pieces, axis=0))
    return jnp.concatenate(columns, axis=1)


def add_faces(sums_ref, product, pair, scale_ref):
    for half, cell_y, cell_x, scale in pair_cells(pair, scale_ref):
        for side in range(2):
            for j in range(EDGE):
                at = side * QUAD + j * EDGE
                rows = pl.ds(side * FACE + ((EDGE - 1) * cell_y + j) * SIDE + (EDGE - 1) * cell_x, EDGE)
                sums_ref[rows, :] += scale * product[at : at + EDGE, half * COLS : (half + 1) * COLS]


def spread_faces(field_ref, matrix_ref, scale_ref, sums_ref):
    sums_ref[...] = jnp.zeros_like(sums_ref)

    def spread(*pairs):
        blocks = [cell_blocks(field_ref, pair, scale_ref) for pair in pairs]
        products = [jnp.dot(matrix_ref[...], block, preferred_element_type=F32) for block in blocks]
        for pair, product in zip(pairs, products):
            add_faces(sums_ref, product, pair, scale_ref)

    for_pairs(spread, 3)


def hand_out(sums_ref, odd, near_out, far_out):
    near_out[...] = sums_ref[pl.ds(pl.multiple_of((1 - odd) * FACE, 16), FACE), :].astype(BF16)
    far_out[...] = sums_ref[pl.ds(pl.multiple_of(odd * FACE, 16), FACE), :].astype(BF16)


def first_faces_kernel(field_ref, full_ref, scale_ref, position_ref, near_out, far_out, sums_ref):
    spread_faces(field_ref, full_ref, scale_ref, sums_ref)
    hand_out(sums_ref, position_ref[0] % 2, near_out, far_out)


def first_faces(field, full, scale, position):
    return pl.pallas_call(
        first_faces_kernel,
        name="first_faces",
        out_shape=(jax.ShapeDtypeStruct((FACE, COLS), BF16),) * 2,
        in_specs=[VMEM] * 2 + [SMEM] * 2,
        out_specs=(VMEM,) * 2,
        scratch_shapes=[pltpu.VMEM((2 * FACE, COLS), F32)],
        compiler_params=SMALL,
    )(field, full, scale, position)


def put_inner(field_ref, store):
    def planes(i, _):
        for z in range(1, EDGE - 1):
            for part in range(3):
                node = i * 48 + part * 16
                halves = [field_ref[pl.ds((node + k) * EDGE + z, EDGE, stride=EDGE), :] for k in (0, EDGE)]
                store((z - 1) * FACE + node, jnp.concatenate(halves, axis=0).astype(BF16))
        return 0

    lax.fori_loop(0, FACE // 48, planes, 0)
    for row in range(INNER, BANDS * INNER_BLOCK, 16):
        store(row, jnp.zeros((16, COLS), BF16))


def put_outer(face_ref, odd, far_weight, store):
    def rows(i, _):
        for part in range(4):
            row = (i * 4 + part) * 16
            far = row < FACE
            near_at = (1 - odd) * FACE + odd * (FACE // 2) + row - FACE
            at = jnp.where(far, odd * FACE + row, jnp.minimum(near_at, 2 * FACE - 16))
            value = face_ref[pl.ds(pl.multiple_of(at, EDGE), 16), :]
            if far_weight is not None:
                value = value * jnp.where(far, far_weight, 1.0)
            index = lax.broadcasted_iota(jnp.int32, (16, COLS), 0) + row
            store(row, jnp.where(index < OUTER, value, 0.0).astype(BF16))
        return 0

    lax.fori_loop(0, BANDS * OUTER_BLOCK // 64, rows, 0)


def faces_kernel(stage, *refs):
    late, spread = stage >= STEPS, stage <= STEPS
    refs = list(refs)
    rim_ref, near_in, far_in, low_ref, high_ref, position_ref = refs[:6]
    refs = refs[6:]
    if spread:
        outer_ref, scale_ref, _ = refs[:3]
        refs = refs[3:]
        face_ref = refs.pop(0)
        if late:
            edge_ref = refs.pop(0)
        sums_ref, near_out, far_out = refs
    else:
        _, block_ref, face_ref, edge_ref, sems = refs
    odd = position_ref[0] % 2
    lead, _ = factors((low_ref, high_ref), stage)

    def settle_rows(i, _):
        for face_in, side in ((near_in, 1 - odd), (far_in, odd)):
            got = face_in[pl.ds(pl.multiple_of(i * GROUP, 16), GROUP), :].astype(F32)
            for part in range(GROUP // EDGE):
                rows = pl.ds(pl.multiple_of(side * FACE + i * GROUP + part * EDGE, EDGE), EDGE)
                value = rim_ref[rows, :] + lead * got[part * EDGE : (part + 1) * EDGE, :]
                face_ref[rows, :] = value.astype(BF16).astype(F32)
        return 0

    lax.fori_loop(0, FACE // GROUP, settle_rows, 0)
    if spread:

        def face_blocks(pair):
            columns = []
            for half, cell_y, cell_x, _ in pair_cells(pair, scale_ref):
                pieces = []
                for side in range(2):
                    for j in range(EDGE):
                        rows = pl.ds(side * FACE + ((EDGE - 1) * cell_y + j) * SIDE + (EDGE - 1) * cell_x, EDGE)
                        pieces.append(face_ref[rows, :])
                columns.append(jnp.concatenate(pieces, axis=0).astype(BF16))
            return jnp.concatenate(columns, axis=1)

        def spread_outer(*pairs):
            blocks = [face_blocks(pair) for pair in pairs]
            products = [jnp.dot(outer_ref[...], block, preferred_element_type=F32) for block in blocks]
            for pair, product in zip(pairs, products):
                add_faces(sums_ref, product, pair, scale_ref)

        for_pairs(spread_outer, 3)
        hand_out(sums_ref, odd, near_out, far_out)
    if late:
        ends = (position_ref[0] == 0) | (position_ref[0] == SLABS - 1)
        far_weight = jnp.where(ends, 1.0, 0.5)

        def put_edge(row, value):
            edge_ref[pl.ds(pl.multiple_of(row, 16), 16), :] = value

        put_outer(face_ref, odd, None if spread else far_weight, put_edge)
    if not spread:
        copies = [
            pltpu.make_async_copy(
                edge_ref.at[pl.ds(band * OUTER_BLOCK, OUTER_BLOCK), :],
                block_ref.at[pl.ds(band * BLOCK + OUTER_BLOCK + INNER_BLOCK, OUTER_BLOCK), :],
                sems.at[band],
            )
            for band in range(BANDS)
        ]
        for copy in copies:
            copy.start()
        for copy in copies:
            copy.wait()


def faces(stage, rim, got, bounds, position, outer=None, scale=None, sums=None, blocks=None):
    args = [rim, *got, *bounds, position]
    specs = [VMEM] * 3 + [SMEM] * 3
    faces_shape = (2 * FACE, COLS)
    scratch = []
    if stage < STEPS:
        outs = [pltpu.VMEM(faces_shape, F32), pltpu.VMEM(faces_shape, F32)]
        aliases = {0: 0, 8: 1}
    elif stage == STEPS:
        outs = [
            jax.ShapeDtypeStruct(faces_shape, F32),
            jax.ShapeDtypeStruct((BANDS * OUTER_BLOCK, COLS), BF16),
            jax.ShapeDtypeStruct(faces_shape, F32),
        ]
        aliases = {8: 2}
    else:
        args.append(in_hbm(blocks))
        outs = [pltpu.HBM((BANDS * BLOCK, COLS), BF16)]
        aliases = {6: 0}
        scratch = [
            pltpu.VMEM(faces_shape, F32),
            pltpu.VMEM((BANDS * OUTER_BLOCK, COLS), BF16),
            pltpu.SemaphoreType.DMA((BANDS,)),
        ]
    if stage <= STEPS:
        args += [outer, scale, sums]
        specs += [VMEM, SMEM, VMEM]
        outs += [jax.ShapeDtypeStruct((FACE, COLS), BF16)] * 2
    else:
        specs.append(HBM)
    return pl.pallas_call(
        functools.partial(faces_kernel, stage),
        name="faces",
        out_shape=tuple(outs),
        in_specs=specs,
        out_specs=((VMEM,) * len(outs)) if stage <= STEPS else (HBM,),
        scratch_shapes=scratch,
        input_output_aliases=aliases,
        compiler_params=SMALL if stage < STEPS else BIG,
    )(*args)


def rebuild(inner_ref, settled_ref, field_ref):
    def nodes(i, _):
        for part in range(3):
            node = i * 48 + part * 16
            for z in range(EDGE):
                for k in (0, EDGE):
                    if z in (0, EDGE - 1):
                        at = pl.ds(pl.multiple_of((z // (EDGE - 1)) * FACE + node + k, EDGE), EDGE)
                        value = settled_ref[at, :]
                    elif k == 0:
                        both = inner_ref[pl.ds(pl.multiple_of((z - 1) * FACE + node, 16), 16), :].astype(F32)
                        value = both[:EDGE]
                    else:
                        value = both[EDGE:]
                    field_ref[pl.ds((node + k) * EDGE + z, EDGE, stride=EDGE), :] = value
        return 0

    lax.fori_loop(0, FACE // 48, nodes, 0)


def cells_kernel(stage, *refs):
    refs = list(refs)
    last = stage > STEPS
    if last:
        (early_ref, settled_ref, edge_ref, pot_ref, mat_ref, low_ref, high_ref, scale_ref,
         rim_ref, plain_ref, block_ref, field_ref, out_ref) = refs
        for band in range(BANDS):
            block_ref[band * BLOCK : band * BLOCK + OUTER_BLOCK, :] = (
                edge_ref[band * OUTER_BLOCK : (band + 1) * OUTER_BLOCK, :])
        rebuild(early_ref, settled_ref, field_ref)
    else:
        if stage > 1:
            settled_ref = refs[2]
            refs = refs[3:]
        pot_ref, mat_ref, inner_ref, low_ref, high_ref, scale_ref, out_ref, sums_ref, rim_ref, *more = (
            refs if stage > 1 else refs[1:])
        if stage == STEPS:
            early_ref = more.pop(0)
        field_ref = more[0] if stage > 1 else refs[0]
        if stage > 1:

            def put_settled(i, _):
                for side in range(2):
                    for part in range(GROUP // EDGE):
                        node = i * GROUP + part * EDGE
                        rows = pl.ds(node * EDGE + side * (EDGE - 1), EDGE, stride=EDGE)
                        field_ref[rows, :] = settled_ref[pl.ds(pl.multiple_of(side * FACE + node, EDGE), EDGE), :]
                return 0

            lax.fori_loop(0, FACE // GROUP, put_settled, 0)
    in_place = 1 < stage <= STEPS
    bounds = (low_ref, high_ref)
    lead, _ = factors(bounds, stage)
    if in_place:
        lead = -lead
    else:
        out_ref[...] = jnp.zeros_like(out_ref)

    def multiply(*pairs):
        blocks = [cell_blocks(field_ref, pair, scale_ref) for pair in pairs]
        products = [jnp.dot(mat_ref[...], block, preferred_element_type=F32) for block in blocks]
        for pair, product in zip(pairs, products):
            for half, cell_y, cell_x, scale in pair_cells(pair, scale_ref):
                factor = lead * scale
                for j in range(EDGE):
                    rows = pl.ds(pl.multiple_of(first_row(cell_y, cell_x, j), EDGE), QUAD)
                    out_ref[rows, :] += factor * product[j * QUAD : (j + 1) * QUAD, half * COLS : (half + 1) * COLS]

    for_pairs(multiply, 4)
    plane = lax.broadcasted_iota(jnp.int32, (EDGE, COLS), 0)
    inside = (plane > 0) & (plane < EDGE - 1)
    half_width = half_width_of(bounds) * 0.5
    center = jnp.full((1, COLS), (high_ref[0] + low_ref[0]) * 0.5, F32)

    def finish(i, _):
        for part in range(GROUP // EDGE):
            rows = pl.ds(pl.multiple_of(i * GROUP + part * EDGE, EDGE), EDGE)
            shifted = pot_ref[rows, :]
            if stage == 1:
                shifted = shifted * 0.5
            elif last:
                shifted = shifted * half_width + center
            value = shifted * field_ref[rows, :]
            value = value - out_ref[rows, :] if in_place else value + out_ref[rows, :]
            out_ref[rows, :] = jnp.where(inside, value.astype(BF16).astype(F32), value)
        return 0

    lax.fori_loop(0, NODES // GROUP, finish, 0)

    def put(row, value):
        if last:
            at = (row // INNER_BLOCK) * BLOCK + OUTER_BLOCK + row % INNER_BLOCK
            block_ref[pl.ds(pl.multiple_of(at, 16), 16), :] = value
        else:
            early_ref[pl.ds(pl.multiple_of(row, 16), 16), :] = value

    def put_rim(i, _):
        for side in range(2):
            for part in range(GROUP // EDGE):
                node = i * GROUP + part * EDGE
                rows = pl.ds(node * EDGE + side * (EDGE - 1), EDGE, stride=EDGE)
                rim_ref[pl.ds(pl.multiple_of(side * FACE + node, EDGE), EDGE), :] = out_ref[rows, :]
        return 0

    if stage >= STEPS:
        put_inner(out_ref, put)
    lax.fori_loop(0, FACE // GROUP, put_rim, 0)
    if last:

        def emit_rows(i, _):
            rows = pl.ds(pl.multiple_of(i * 2 * GROUP, 2 * GROUP), 2 * GROUP)
            plain_ref[rows, :] = field_ref[rows, :].astype(BF16)
            return 0

        lax.fori_loop(0, NODES // (2 * GROUP), emit_rows, 0)
    else:
        spread_faces(out_ref, inner_ref, scale_ref, sums_ref)


def cells(stage, field, prev, settled, pot, mat, inner, bounds, scale):
    args = [field] + ([prev, settled] if stage > 1 else []) + [pot, mat, inner]
    faces_shape = (2 * FACE, COLS)
    kind = pltpu.VMEM if stage < STEPS else pltpu.HBM
    outs = [pltpu.VMEM((NODES, COLS), F32), kind(faces_shape, F32), kind(faces_shape, F32)]
    if stage == STEPS:
        outs.append(pltpu.HBM((BANDS * INNER_BLOCK, COLS), BF16))
    aliases = {}
    if stage > 1:
        aliases = {1: 0, 0: len(outs)}
        outs.append(pltpu.VMEM((NODES, COLS), F32))
    return pl.pallas_call(
        functools.partial(cells_kernel, stage),
        name="cells",
        out_shape=tuple(outs),
        in_specs=[VMEM] * len(args) + [SMEM] * 3,
        out_specs=(VMEM,) * len(outs),
        input_output_aliases=aliases,
        compiler_params=SMALL if stage < STEPS else BIG,
    )(*args, *bounds, scale)


def last_cells(early, settled, edge, pot, mat, bounds, scale):
    return pl.pallas_call(
        functools.partial(cells_kernel, STEPS + 1),
        name="last_cells",
        out_shape=(
            pltpu.VMEM((2 * FACE, COLS), F32),
            jax.ShapeDtypeStruct((NODES, COLS), BF16),
            jax.ShapeDtypeStruct((BANDS * BLOCK, COLS), BF16),
        ),
        in_specs=[VMEM] * 5 + [SMEM] * 3,
        out_specs=(VMEM,) * 3,
        scratch_shapes=[pltpu.VMEM((NODES, COLS), F32)] * 2,
        compiler_params=pltpu.CompilerParams(vmem_limit_bytes=32 * 1024 * 1024),
    )(early, settled, edge, pot, mat, *bounds, scale)


def return_kernel(plain_ref, index_ref, out_ref, hot_ref, rhs_ref, field_ref):
    field_ref[...] = plain_ref[...].astype(F32)
    j = lax.broadcasted_iota(jnp.int32, (EDGE, COLS), 0)

    def step(plane, _):
        for cell in range(CELLS):
            cell_y, cell_x = cell // SLAB_XY, cell % SLAB_XY
            for k in range(EDGE):
                at = cell * QUAD + k * EDGE
                value = field_ref[pl.ds(first_row(cell_y, cell_x, k) + plane, EDGE, stride=EDGE), :]
                if cell_y > 0 and k == 0:
                    value = jnp.zeros_like(value)
                elif cell_x > 0:
                    value = jnp.where(j == 0, 0.0, value)
                rhs_ref[at : at + EDGE, :] = value
        want = index_ref[pl.ds(plane, 1), :].astype(F32) - (plane * FACE).astype(F32)
        rhs = rhs_ref[...].astype(BF16)
        for part in range(THIRDS):
            row = lax.broadcasted_iota(jnp.int32, (THIRD, CELLS * QUAD), 0).astype(F32) + float(part * THIRD)
            hot_ref[...] = jnp.where(want == row, 1.0, 0.0).astype(BF16)
            got = jnp.dot(hot_ref[...], rhs, preferred_element_type=F32)
            start = pl.multiple_of(plane * FACE + part * THIRD, 16)
            out_ref[pl.ds(start, THIRD), :] = got.astype(BF16)
        return 0

    lax.fori_loop(0, EDGE, step, 0)


def hand_back(field, connectivity):
    index = connectivity.reshape(CELLS, EDGE, QUAD).transpose(1, 0, 2).reshape(EDGE, CELLS * QUAD)
    return pl.pallas_call(
        return_kernel,
        name="hand_back",
        out_shape=jax.ShapeDtypeStruct((NODES, COLS), BF16),
        in_specs=[VMEM] * 2,
        out_specs=VMEM,
        scratch_shapes=[
            pltpu.VMEM((THIRD, CELLS * QUAD), BF16),
            pltpu.VMEM((CELLS * QUAD, COLS), F32),
            pltpu.VMEM((NODES, COLS), F32),
        ],
        compiler_params=BIG,
    )(field, index)


def product_kernel(factor, states_ref, mixed_ref, position_ref, kept_ref, sent_ref, inner_ref, outer_ref):
    odd = position_ref[0] % 2 == 1
    for band in range(BANDS):
        rows = slice(band * COLS, (band + 1) * COLS)
        inner_ref[rows, :] = jnp.transpose(mixed_ref[band, OUTER_BLOCK : OUTER_BLOCK + INNER_BLOCK, :])
        outer_ref[rows, :] = jnp.transpose(mixed_ref[band, OUTER_BLOCK + INNER_BLOCK :, :])

    def step(i, _):
        inner = jnp.concatenate([states_ref[2 * i], states_ref[2 * i + 1]], axis=1)
        outer = jnp.concatenate([mixed_ref[2 * i, :OUTER_BLOCK, :], mixed_ref[2 * i + 1, :OUTER_BLOCK, :]], axis=1)
        product = jnp.dot(inner_ref[...], inner, preferred_element_type=F32)
        product = (product + jnp.dot(outer_ref[...], outer, preferred_element_type=F32)) * factor
        half = COLS // 2
        for band in range(BANDS):
            for part in range(2):
                columns = slice(part * COLS, (part + 1) * COLS)
                first = product[band * COLS : band * COLS + half, columns]
                second = product[band * COLS + half : (band + 1) * COLS, columns]
                kept_ref[band, 2 * i + part] = jnp.where(odd, second, first).astype(BF16)
                sent_ref[band, 2 * i + part] = jnp.where(odd, first, second).astype(BF16)
        return 0

    lax.fori_loop(0, BANDS // 2, step, 0)


def project(states, mixed, position):
    count = lax.axis_size("space")
    halves = count // 2
    factor = 1.0 / (FACE * ((EDGE - 1) * count + 1))
    shape = jax.ShapeDtypeStruct((halves, BANDS, COLS // 2, COLS), BF16)
    kept, sent = pl.pallas_call(
        functools.partial(product_kernel, factor),
        name="products",
        out_shape=(shape, shape),
        in_specs=[VMEM] * 2 + [SMEM],
        out_specs=(VMEM,) * 2,
        scratch_shapes=[
            pltpu.VMEM((BANDS * COLS, INNER_BLOCK), BF16),
            pltpu.VMEM((BANDS * COLS, OUTER_BLOCK), BF16),
        ],
        compiler_params=BIG,
    )(states, mixed, position)
    got = lax.ppermute(sent, "space", [(i, i ^ 1) for i in range(count)])
    both = (kept.astype(F32) + got.astype(F32)).astype(BF16).reshape(halves * BANDS, COLS // 2, COLS)
    groups = [[(2 * half + part) * BANDS + band for half in range(halves) for band in range(BANDS)] for part in range(2)]
    arrived = lax.all_to_all(both, ("space", "band"), split_axis=0, concat_axis=0, tiled=True, axis_index_groups=groups)
    return arrived.astype(F32).sum(axis=0).T


def swap_faces(near, far):
    count = lax.axis_size("space")
    apart = [(i, i + 1) for i in range(1, count - 1, 2)]
    beside = [(i, i + 1) for i in range(0, count, 2)]
    both_ways = lambda pairs: pairs + [(j, i) for i, j in pairs]
    near, far = lax.optimization_barrier((near, far))
    from_far = lax.ppermute(far, "space", both_ways(apart))
    from_near = lax.ppermute(near, "space", both_ways(beside))
    return from_near, from_far


def local(states, potential, cell_matrix, cell_scale, connectivity, lower_bound, upper_bound):
    bounds = (lower_bound, upper_bound)
    position = lax.axis_index("space").astype(jnp.int32).reshape(1)
    field, pot, mat, full, inner, outer = gather(states, potential, connectivity, cell_matrix, bounds)
    near, far = first_faces(field, full, cell_scale, position)
    prev = settled = None
    for stage in range(1, STEPS):
        got = swap_faces(near, far)
        part, sums, rim, *patched = cells(stage, field, prev, settled, pot, mat, inner, bounds, cell_scale)
        prev, field = (patched or [field])[0], part
        settled, _, near, far = faces(stage, rim, got, bounds, position, outer, cell_scale, sums)
    got = swap_faces(near, far)
    _, sums, rim, early, _ = cells(STEPS, field, prev, settled, pot, mat, inner, bounds, cell_scale)
    got, early = lax.optimization_barrier((got, early))
    node_states = lax.all_to_all(
        early.reshape(BANDS, INNER_BLOCK, COLS), "band", split_axis=0, concat_axis=0, tiled=True)
    settled, edge, _, near, far = faces(STEPS, rim, got, bounds, position, outer, cell_scale, sums)
    got = swap_faces(near, far)
    rim, current, blocks = last_cells(early, settled, edge, pot, mat, bounds, cell_scale)
    blocks, = faces(STEPS + 1, rim, got, bounds, position, blocks=blocks)
    blocks, current = lax.optimization_barrier((blocks, current))
    filtered = hand_back(current, connectivity)
    mixed = lax.all_to_all(blocks.reshape(BANDS, BLOCK, COLS), "band", split_axis=0, concat_axis=0, tiled=True)
    totals = project(node_states, mixed, position)
    return filtered, totals


def solution(mesh):
    placed = (P("space", "band"), P("space"), P(), P("space"), P("space", None), P(), P())
    return jax.shard_map(
        local,
        mesh=mesh,
        in_specs=placed,
        out_specs=(P("space", "band"), P("band", "space")),
        check_vma=False,
    )
```

```python
import functools

import jax
import jax.numpy as jnp
from jax import lax
from jax.experimental import pallas as pl
from jax.experimental.pallas import tpu as pltpu
from jax.sharding import PartitionSpec as P


EDGE = 8
SLAB_XY = 5
STEPS = 4
CELLS = SLAB_XY * SLAB_XY
PAIRS = (CELLS + 1) // 2
CELL_NODES = EDGE**3
SIDE = (EDGE - 1) * SLAB_XY + 1
FACE = SIDE * SIDE
NODES = FACE * EDGE
COLS = 128
SLABS = 16
GROUP = 144
BANDS = 8
INNER = (EDGE - 2) * FACE
INNER_BLOCK = 976
OUTER = FACE + FACE // 2
OUTER_BLOCK = 256
BLOCK = INNER_BLOCK + 2 * OUTER_BLOCK
GATHER_PARTS = ((0, CELLS),)
QUAD = EDGE * EDGE
THIRDS = 3
THIRD = FACE // THIRDS
F32 = jnp.float32
BF16 = jnp.bfloat16
VMEM = pl.BlockSpec(memory_space=pltpu.VMEM)
SMEM = pl.BlockSpec(memory_space=pltpu.SMEM)
HBM = pl.BlockSpec(memory_space=pltpu.HBM)
BIG = pltpu.CompilerParams(vmem_limit_bytes=24 * 1024 * 1024)
SMALL = pltpu.CompilerParams(vmem_limit_bytes=8 * 1024 * 1024)


def first_row(cell_y, cell_x, j):
    return (((EDGE - 1) * cell_y + j) * SIDE + (EDGE - 1) * cell_x) * EDGE


def gather_kernel(states_hbm, pot_ref, index_hbm, matrix_hbm, low_ref, high_ref, field_ref, pot_out_ref, mat_ref,
                  full_ref, inner_ref, outer_ref, rhs_ref, hot_ref, column_ref, states_ref, index_ref, matrix_ref, sems):
    index_copy = pltpu.make_async_copy(index_hbm, index_ref, sems.at[0])
    matrix_copy = pltpu.make_async_copy(matrix_hbm, matrix_ref, sems.at[1])
    states_copy = pltpu.make_async_copy(states_hbm, states_ref, sems.at[2])
    index_copy.start()
    matrix_copy.start()
    states_copy.start()
    index_copy.wait()
    for cell_y in range(SLAB_XY):
        five = index_ref[cell_y * SLAB_XY : (cell_y + 1) * SLAB_XY, :].astype(F32)
        five = jnp.concatenate([five, jnp.zeros((EDGE - SLAB_XY, CELL_NODES), F32)], axis=0)
        column_ref[cell_y * CELL_NODES : (cell_y + 1) * CELL_NODES, :EDGE] = jnp.transpose(five)
    pot = jnp.transpose(pot_ref[...])
    high = pot.astype(BF16)
    rest = pot - high.astype(F32)
    mid = rest.astype(BF16)
    low = (rest - mid.astype(F32)).astype(BF16)
    rhs_ref[:, COLS:] = jnp.concatenate(
        [high, mid, low, jnp.zeros((FACE, COLS - 3 * EDGE), BF16)], axis=1)

    matrix_copy.wait()
    new = lax.broadcasted_iota(jnp.int32, (CELL_NODES, CELL_NODES), 0)
    old = lax.broadcasted_iota(jnp.int32, (CELL_NODES, CELL_NODES), 1)
    order = jnp.where(old == (new % EDGE) * QUAD + new // EDGE, 1.0, 0.0).astype(BF16)
    across = (((1,), (1,)), ((), ()))
    turned = lax.dot_general(matrix_ref[...], order, across, preferred_element_type=F32).astype(BF16)
    mat_ref[...] = jnp.dot(order, turned, preferred_element_type=F32).astype(BF16)
    for side, first in enumerate((0, CELL_NODES - QUAD)):
        rows = pl.ds(side * QUAD, QUAD)
        face_rows = turned[first : first + QUAD, :].astype(F32)
        z = lax.broadcasted_iota(jnp.int32, (QUAD, CELL_NODES), 1) % EDGE
        full_ref[rows, :] = face_rows.astype(BF16)
        inner_ref[rows, :] = jnp.where((z > 0) & (z < EDGE - 1), face_rows, 0.0).astype(BF16)
        outer_ref[rows, :QUAD] = matrix_ref[first : first + QUAD, :QUAD]
        outer_ref[rows, QUAD:] = matrix_ref[first : first + QUAD, CELL_NODES - QUAD :]
    lead, shift = factors((low_ref, high_ref), 2)
    states_copy.wait()

    def step(plane, _):
        rhs_ref[:, :COLS] = states_ref[pl.ds(pl.multiple_of(plane * FACE, 16), FACE), :]
        start = (plane * FACE).astype(F32)
        lane = lax.broadcasted_iota(jnp.int32, (EDGE, COLS), 1)
        mine = (lane % EDGE == plane) & (lane < 3 * EDGE)
        for first, last in GATHER_PARTS:
            at = 0
            for cell in range(first, last):
                cell_y, cell_x = cell // SLAB_XY, cell % SLAB_XY
                rows = QUAD if cell_y == SLAB_XY - 1 else QUAD - EDGE
                lanes = lax.broadcasted_iota(jnp.int32, (rows, FACE), 1).astype(F32)
                want = column_ref[pl.ds(pl.multiple_of(cell_y * CELL_NODES + plane * QUAD, 8), rows), cell_x : cell_x + 1] - start
                hot_ref[at : at + rows, :] = jnp.where(want == lanes, 1.0, 0.0).astype(BF16)
                at += rows
            got = jnp.dot(hot_ref[:at, :], rhs_ref[...], preferred_element_type=F32)
            at = 0
            for cell in range(first, last):
                cell_y, cell_x = cell // SLAB_XY, cell % SLAB_XY
                for j in range(EDGE if cell_y == SLAB_XY - 1 else EDGE - 1):
                    rows = pl.ds(first_row(cell_y, cell_x, j) + plane, EDGE, stride=EDGE)
                    field_ref[rows, :] = got[at : at + EDGE, :COLS]
                    value = jnp.sum(jnp.where(mine, got[at : at + EDGE, COLS:], 0.0), axis=1, keepdims=True)
                    pot_out_ref[rows, :] = lead * value - shift
                    at += EDGE
        return 0

    lax.fori_loop(0, EDGE, step, 0)


def in_hbm(x):
    return pltpu.with_memory_space_constraint(x, pltpu.HBM)


def gather(states, potential, connectivity, matrix, bounds):
    return pl.pallas_call(
        gather_kernel,
        name="gather_states",
        out_shape=(
            pltpu.VMEM((NODES, COLS), F32),
            pltpu.VMEM((NODES, COLS), F32),
            pltpu.VMEM((CELL_NODES, CELL_NODES), BF16),
            pltpu.VMEM((2 * QUAD, CELL_NODES), BF16),
            pltpu.VMEM((2 * QUAD, CELL_NODES), BF16),
            pltpu.VMEM((2 * QUAD, 2 * QUAD), BF16),
        ),
        in_specs=[HBM, VMEM, HBM, HBM] + [SMEM] * 2,
        out_specs=(VMEM,) * 6,
        scratch_shapes=[
            pltpu.VMEM((FACE, 2 * COLS), BF16),
            pltpu.VMEM((CELLS * QUAD, FACE), BF16),
            pltpu.VMEM((SLAB_XY * CELL_NODES, COLS), F32),
            pltpu.VMEM((NODES, COLS), BF16),
            pltpu.VMEM((CELLS, CELL_NODES), jnp.int32),
            pltpu.VMEM((CELL_NODES, CELL_NODES), BF16),
            pltpu.SemaphoreType.DMA((3,)),
        ],
        compiler_params=BIG,
    )(in_hbm(states), potential.reshape(EDGE, FACE), in_hbm(connectivity), in_hbm(matrix), *bounds)


def half_width_of(bounds):
    low, high = bounds
    return jnp.full((1, COLS), (high[0] - low[0]) * 0.5, F32)


def factors(bounds, stage):
    if stage > STEPS:
        return jnp.ones((1, COLS), F32), None
    low, high = bounds
    center = (high[0] + low[0]) * 0.5
    lead = (1.0 if stage == 1 else 2.0) / half_width_of(bounds)
    return lead, lead * center


def pair_cells(pair, scale_ref):
    for half in range(2):
        index = 2 * pair + half
        cell = jnp.minimum(index, CELLS - 1)
        yield half, cell // SLAB_XY, cell % SLAB_XY, jnp.where(index < CELLS, scale_ref[cell], 0.0)


def for_pairs(work, group):
    def step(i, _):
        work(*[group * i + k for k in range(group)])
        return 0

    lax.fori_loop(0, PAIRS // group, step, 0)
    if PAIRS % group:
        work(*[jnp.int32(pair) for pair in range(PAIRS - PAIRS % group, PAIRS)])


def cell_blocks(field_ref, pair, scale_ref):
    columns = []
    for half, cell_y, cell_x, _ in pair_cells(pair, scale_ref):
        pieces = []
        for j in range(EDGE):
            rows = pl.ds(pl.multiple_of(first_row(cell_y, cell_x, j), EDGE), QUAD)
            pieces.append(field_ref[rows, :].astype(BF16))
        columns.append(jnp.concatenate(pieces, axis=0))
    return jnp.concatenate(columns, axis=1)


def add_faces(sums_ref, product, pair, scale_ref):
    for half, cell_y, cell_x, scale in pair_cells(pair, scale_ref):
        fresh = []
        for side in range(2):
            for j in range(EDGE):
                at = side * QUAD + j * EDGE
                rows = pl.ds(side * FACE + ((EDGE - 1) * cell_y + j) * SIDE + (EDGE - 1) * cell_x, EDGE)
                value = scale * product[at : at + EDGE, half * COLS : (half + 1) * COLS]
                fresh.append((rows, sums_ref[rows, :] + value))
        for rows, value in fresh:
            sums_ref[rows, :] = value


def spread_faces(field_ref, matrix_ref, scale_ref, sums_ref):
    sums_ref[...] = jnp.zeros_like(sums_ref)

    def spread(*pairs):
        blocks = [cell_blocks(field_ref, pair, scale_ref) for pair in pairs]
        products = [jnp.dot(matrix_ref[...], block, preferred_element_type=F32) for block in blocks]
        for pair, product in zip(pairs, products):
            add_faces(sums_ref, product, pair, scale_ref)

    for_pairs(spread, 3)


def hand_out(sums_ref, odd, near_out, far_out):
    near_out[...] = sums_ref[pl.ds(pl.multiple_of((1 - odd) * FACE, 16), FACE), :].astype(BF16)
    far_out[...] = sums_ref[pl.ds(pl.multiple_of(odd * FACE, 16), FACE), :].astype(BF16)


def first_faces_kernel(field_ref, full_ref, scale_ref, position_ref, near_out, far_out, sums_ref):
    spread_faces(field_ref, full_ref, scale_ref, sums_ref)
    hand_out(sums_ref, position_ref[0] % 2, near_out, far_out)


def first_faces(field, full, scale, position):
    return pl.pallas_call(
        first_faces_kernel,
        name="first_faces",
        out_shape=(jax.ShapeDtypeStruct((FACE, COLS), BF16),) * 2,
        in_specs=[VMEM] * 2 + [SMEM] * 2,
        out_specs=(VMEM,) * 2,
        scratch_shapes=[pltpu.VMEM((2 * FACE, COLS), F32)],
        compiler_params=SMALL,
    )(field, full, scale, position)


def put_inner(field_ref, store):
    def planes(i, _):
        for z in range(1, EDGE - 1):
            for part in range(3):
                node = i * 48 + part * 16
                halves = [field_ref[pl.ds((node + k) * EDGE + z, EDGE, stride=EDGE), :] for k in (0, EDGE)]
                store((z - 1) * FACE + node, jnp.concatenate(halves, axis=0).astype(BF16))
        return 0

    lax.fori_loop(0, FACE // 48, planes, 0)
    for row in range(INNER, BANDS * INNER_BLOCK, 16):
        store(row, jnp.zeros((16, COLS), BF16))


def put_outer(face_ref, odd, far_weight, store):
    def rows(i, _):
        for part in range(4):
            row = (i * 4 + part) * 16
            far = row < FACE
            near_at = (1 - odd) * FACE + odd * (FACE // 2) + row - FACE
            at = jnp.where(far, odd * FACE + row, jnp.minimum(near_at, 2 * FACE - 16))
            value = face_ref[pl.ds(pl.multiple_of(at, EDGE), 16), :]
            if far_weight is not None:
                value = value * jnp.where(far, far_weight, 1.0)
            index = lax.broadcasted_iota(jnp.int32, (16, COLS), 0) + row
            store(row, jnp.where(index < OUTER, value, 0.0).astype(BF16))
        return 0

    lax.fori_loop(0, BANDS * OUTER_BLOCK // 64, rows, 0)


def faces_kernel(stage, *refs):
    late, spread = stage >= STEPS, stage <= STEPS
    refs = list(refs)
    rim_ref, near_in, far_in, low_ref, high_ref, position_ref = refs[:6]
    refs = refs[6:]
    if spread:
        outer_ref, scale_ref, _ = refs[:3]
        refs = refs[3:]
        face_ref = refs.pop(0)
        if late:
            edge_ref = refs.pop(0)
        sums_ref, near_out, far_out = refs
    else:
        _, block_ref, face_ref, edge_ref, sems = refs
    odd = position_ref[0] % 2
    lead, _ = factors((low_ref, high_ref), stage)

    def settle_rows(i, _):
        here = pl.ds(pl.multiple_of(i * GROUP, 16), GROUP)
        settled = []
        for face_in, side in ((near_in, 1 - odd), (far_in, odd)):
            rows = pl.ds(pl.multiple_of(side * FACE + i * GROUP, 16), GROUP)
            settled.append((rows, (rim_ref[rows, :] + lead * face_in[here, :].astype(F32)).astype(BF16).astype(F32)))
        for rows, value in settled:
            face_ref[rows, :] = value
        return 0

    lax.fori_loop(0, FACE // GROUP, settle_rows, 0)
    if spread:

        def face_blocks(pair):
            columns = []
            for half, cell_y, cell_x, _ in pair_cells(pair, scale_ref):
                pieces = []
                for side in range(2):
                    for j in range(EDGE):
                        rows = pl.ds(side * FACE + ((EDGE - 1) * cell_y + j) * SIDE + (EDGE - 1) * cell_x, EDGE)
                        pieces.append(face_ref[rows, :])
                columns.append(jnp.concatenate(pieces, axis=0).astype(BF16))
            return jnp.concatenate(columns, axis=1)

        def spread_outer(*pairs):
            blocks = [face_blocks(pair) for pair in pairs]
            products = [jnp.dot(outer_ref[...], block, preferred_element_type=F32) for block in blocks]
            for pair, product in zip(pairs, products):
                add_faces(sums_ref, product, pair, scale_ref)

        for_pairs(spread_outer, 3)
        hand_out(sums_ref, odd, near_out, far_out)
    if late:
        ends = (position_ref[0] == 0) | (position_ref[0] == SLABS - 1)
        far_weight = jnp.where(ends, 1.0, 0.5)

        def put_edge(row, value):
            edge_ref[pl.ds(pl.multiple_of(row, 16), 16), :] = value

        put_outer(face_ref, odd, None if spread else far_weight, put_edge)
    if not spread:
        copies = [
            pltpu.make_async_copy(
                edge_ref.at[pl.ds(band * OUTER_BLOCK, OUTER_BLOCK), :],
                block_ref.at[pl.ds(band * BLOCK + OUTER_BLOCK + INNER_BLOCK, OUTER_BLOCK), :],
                sems.at[band],
            )
            for band in range(BANDS)
        ]
        for copy in copies:
            copy.start()
        for copy in copies:
            copy.wait()


def faces(stage, rim, got, bounds, position, outer=None, scale=None, sums=None, blocks=None):
    args = [rim, *got, *bounds, position]
    specs = [VMEM] * 3 + [SMEM] * 3
    faces_shape = (2 * FACE, COLS)
    scratch = []
    if stage < STEPS:
        outs = [pltpu.VMEM(faces_shape, F32), pltpu.VMEM(faces_shape, F32)]
        aliases = {0: 0, 8: 1}
    elif stage == STEPS:
        outs = [
            jax.ShapeDtypeStruct(faces_shape, F32),
            jax.ShapeDtypeStruct((BANDS * OUTER_BLOCK, COLS), BF16),
            jax.ShapeDtypeStruct(faces_shape, F32),
        ]
        aliases = {8: 2}
    else:
        args.append(in_hbm(blocks))
        outs = [pltpu.HBM((BANDS * BLOCK, COLS), BF16)]
        aliases = {6: 0}
        scratch = [
            pltpu.VMEM(faces_shape, F32),
            pltpu.VMEM((BANDS * OUTER_BLOCK, COLS), BF16),
            pltpu.SemaphoreType.DMA((BANDS,)),
        ]
    if stage <= STEPS:
        args += [outer, scale, sums]
        specs += [VMEM, SMEM, VMEM]
        outs += [jax.ShapeDtypeStruct((FACE, COLS), BF16)] * 2
    else:
        specs.append(HBM)
    return pl.pallas_call(
        functools.partial(faces_kernel, stage),
        name="faces",
        out_shape=tuple(outs),
        in_specs=specs,
        out_specs=((VMEM,) * len(outs)) if stage <= STEPS else (HBM,),
        scratch_shapes=scratch,
        input_output_aliases=aliases,
        compiler_params=SMALL if stage < STEPS else BIG,
    )(*args)


def rebuild(inner_ref, settled_ref, field_ref):
    def nodes(i, _):
        for part in range(3):
            node = i * 48 + part * 16
            for z in range(EDGE):
                for k in (0, EDGE):
                    if z in (0, EDGE - 1):
                        at = pl.ds(pl.multiple_of((z // (EDGE - 1)) * FACE + node + k, EDGE), EDGE)
                        value = settled_ref[at, :]
                    elif k == 0:
                        both = inner_ref[pl.ds(pl.multiple_of((z - 1) * FACE + node, 16), 16), :].astype(F32)
                        value = both[:EDGE]
                    else:
                        value = both[EDGE:]
                    field_ref[pl.ds((node + k) * EDGE + z, EDGE, stride=EDGE), :] = value
        return 0

    lax.fori_loop(0, FACE // 48, nodes, 0)


def cells_kernel(stage, *refs):
    refs = list(refs)
    last = stage > STEPS
    if last:
        (early_ref, settled_ref, edge_ref, pot_ref, mat_ref, low_ref, high_ref, scale_ref,
         rim_ref, plain_ref, block_ref, field_ref, out_ref) = refs
        for band in range(BANDS):
            block_ref[band * BLOCK : band * BLOCK + OUTER_BLOCK, :] = (
                edge_ref[band * OUTER_BLOCK : (band + 1) * OUTER_BLOCK, :])
        rebuild(early_ref, settled_ref, field_ref)
    else:
        if stage > 1:
            settled_ref = refs[2]
            refs = refs[3:]
        pot_ref, mat_ref, inner_ref, low_ref, high_ref, scale_ref, out_ref, sums_ref, rim_ref, *more = (
            refs if stage > 1 else refs[1:])
        if stage == STEPS:
            early_ref = more.pop(0)
        field_ref = more[0] if stage > 1 else refs[0]
        if stage > 1:

            def put_settled(i, _):
                for side in range(2):
                    for part in range(GROUP // EDGE):
                        node = i * GROUP + part * EDGE
                        rows = pl.ds(node * EDGE + side * (EDGE - 1), EDGE, stride=EDGE)
                        field_ref[rows, :] = settled_ref[pl.ds(pl.multiple_of(side * FACE + node, EDGE), EDGE), :]
                return 0

            lax.fori_loop(0, FACE // GROUP, put_settled, 0)
    in_place = 1 < stage <= STEPS
    bounds = (low_ref, high_ref)
    lead, _ = factors(bounds, stage)
    if in_place:
        lead = -lead
    else:
        out_ref[...] = jnp.zeros_like(out_ref)

    def multiply(*pairs):
        blocks = [cell_blocks(field_ref, pair, scale_ref) for pair in pairs]
        products = [jnp.dot(mat_ref[...], block, preferred_element_type=F32) for block in blocks]
        for pair, product in zip(pairs, products):
            for half, cell_y, cell_x, scale in pair_cells(pair, scale_ref):
                factor = lead * scale
                for j in range(EDGE):
                    rows = pl.ds(pl.multiple_of(first_row(cell_y, cell_x, j), EDGE), QUAD)
                    out_ref[rows, :] += factor * product[j * QUAD : (j + 1) * QUAD, half * COLS : (half + 1) * COLS]

    for_pairs(multiply, 4)
    plane = lax.broadcasted_iota(jnp.int32, (EDGE, COLS), 0)
    inside = (plane > 0) & (plane < EDGE - 1)
    half_width = half_width_of(bounds) * 0.5
    center = jnp.full((1, COLS), (high_ref[0] + low_ref[0]) * 0.5, F32)

    def finish(i, _):
        for part in range(GROUP // EDGE):
            rows = pl.ds(pl.multiple_of(i * GROUP + part * EDGE, EDGE), EDGE)
            shifted = pot_ref[rows, :]
            if stage == 1:
                shifted = shifted * 0.5
            elif last:
                shifted = shifted * half_width + center
            value = shifted * field_ref[rows, :]
            value = value - out_ref[rows, :] if in_place else value + out_ref[rows, :]
            out_ref[rows, :] = jnp.where(inside, value.astype(BF16).astype(F32), value)
        return 0

    lax.fori_loop(0, NODES // GROUP, finish, 0)

    def put(row, value):
        if last:
            at = (row // INNER_BLOCK) * BLOCK + OUTER_BLOCK + row % INNER_BLOCK
            block_ref[pl.ds(pl.multiple_of(at, 16), 16), :] = value
        else:
            early_ref[pl.ds(pl.multiple_of(row, 16), 16), :] = value

    def put_rim(i, _):
        for side in range(2):
            for part in range(GROUP // EDGE):
                node = i * GROUP + part * EDGE
                rows = pl.ds(node * EDGE + side * (EDGE - 1), EDGE, stride=EDGE)
                rim_ref[pl.ds(pl.multiple_of(side * FACE + node, EDGE), EDGE), :] = out_ref[rows, :]
        return 0

    if stage >= STEPS:
        put_inner(out_ref, put)
    lax.fori_loop(0, FACE // GROUP, put_rim, 0)
    if last:

        def emit_rows(i, _):
            rows = pl.ds(pl.multiple_of(i * 2 * GROUP, 2 * GROUP), 2 * GROUP)
            plain_ref[rows, :] = field_ref[rows, :].astype(BF16)
            return 0

        lax.fori_loop(0, NODES // (2 * GROUP), emit_rows, 0)
    else:
        spread_faces(out_ref, inner_ref, scale_ref, sums_ref)


def cells(stage, field, prev, settled, pot, mat, inner, bounds, scale):
    args = [field] + ([prev, settled] if stage > 1 else []) + [pot, mat, inner]
    faces_shape = (2 * FACE, COLS)
    kind = pltpu.VMEM if stage < STEPS else pltpu.HBM
    outs = [pltpu.VMEM((NODES, COLS), F32), kind(faces_shape, F32), kind(faces_shape, F32)]
    if stage == STEPS:
        outs.append(pltpu.HBM((BANDS * INNER_BLOCK, COLS), BF16))
    aliases = {}
    if stage > 1:
        aliases = {1: 0, 0: len(outs)}
        outs.append(pltpu.VMEM((NODES, COLS), F32))
    return pl.pallas_call(
        functools.partial(cells_kernel, stage),
        name="cells",
        out_shape=tuple(outs),
        in_specs=[VMEM] * len(args) + [SMEM] * 3,
        out_specs=(VMEM,) * len(outs),
        input_output_aliases=aliases,
        compiler_params=SMALL if stage < STEPS else BIG,
    )(*args, *bounds, scale)


def last_cells(early, settled, edge, pot, mat, bounds, scale):
    return pl.pallas_call(
        functools.partial(cells_kernel, STEPS + 1),
        name="last_cells",
        out_shape=(
            pltpu.VMEM((2 * FACE, COLS), F32),
            jax.ShapeDtypeStruct((NODES, COLS), BF16),
            jax.ShapeDtypeStruct((BANDS * BLOCK, COLS), BF16),
        ),
        in_specs=[VMEM] * 5 + [SMEM] * 3,
        out_specs=(VMEM,) * 3,
        scratch_shapes=[pltpu.VMEM((NODES, COLS), F32)] * 2,
        compiler_params=pltpu.CompilerParams(vmem_limit_bytes=32 * 1024 * 1024),
    )(early, settled, edge, pot, mat, *bounds, scale)


def return_kernel(plain_ref, index_ref, out_ref, hot_ref, rhs_ref, field_ref):
    field_ref[...] = plain_ref[...].astype(F32)
    j = lax.broadcasted_iota(jnp.int32, (EDGE, COLS), 0)

    def step(plane, _):
        for cell in range(CELLS):
            cell_y, cell_x = cell // SLAB_XY, cell % SLAB_XY
            for k in range(EDGE):
                at = cell * QUAD + k * EDGE
                value = field_ref[pl.ds(first_row(cell_y, cell_x, k) + plane, EDGE, stride=EDGE), :]
                if cell_y > 0 and k == 0:
                    value = jnp.zeros_like(value)
                elif cell_x > 0:
                    value = jnp.where(j == 0, 0.0, value)
                rhs_ref[at : at + EDGE, :] = value
        want = index_ref[pl.ds(plane, 1), :].astype(F32) - (plane * FACE).astype(F32)
        rhs = rhs_ref[...].astype(BF16)
        for part in range(THIRDS):
            row = lax.broadcasted_iota(jnp.int32, (THIRD, CELLS * QUAD), 0).astype(F32) + float(part * THIRD)
            hot_ref[...] = jnp.where(want == row, 1.0, 0.0).astype(BF16)
            got = jnp.dot(hot_ref[...], rhs, preferred_element_type=F32)
            start = pl.multiple_of(plane * FACE + part * THIRD, 16)
            out_ref[pl.ds(start, THIRD), :] = got.astype(BF16)
        return 0

    lax.fori_loop(0, EDGE, step, 0)


def hand_back(field, connectivity):
    index = connectivity.reshape(CELLS, EDGE, QUAD).transpose(1, 0, 2).reshape(EDGE, CELLS * QUAD)
    return pl.pallas_call(
        return_kernel,
        name="hand_back",
        out_shape=jax.ShapeDtypeStruct((NODES, COLS), BF16),
        in_specs=[VMEM] * 2,
        out_specs=VMEM,
        scratch_shapes=[
            pltpu.VMEM((THIRD, CELLS * QUAD), BF16),
            pltpu.VMEM((CELLS * QUAD, COLS), F32),
            pltpu.VMEM((NODES, COLS), F32),
        ],
        compiler_params=BIG,
    )(field, index)


def product_kernel(factor, states_ref, mixed_ref, position_ref, kept_ref, sent_ref, inner_ref, outer_ref):
    odd = position_ref[0] % 2 == 1
    for band in range(BANDS):
        rows = slice(band * COLS, (band + 1) * COLS)
        inner_ref[rows, :] = jnp.transpose(mixed_ref[band, OUTER_BLOCK : OUTER_BLOCK + INNER_BLOCK, :])
        outer_ref[rows, :] = jnp.transpose(mixed_ref[band, OUTER_BLOCK + INNER_BLOCK :, :])

    def step(i, _):
        inner = jnp.concatenate([states_ref[2 * i], states_ref[2 * i + 1]], axis=1)
        outer = jnp.concatenate([mixed_ref[2 * i, :OUTER_BLOCK, :], mixed_ref[2 * i + 1, :OUTER_BLOCK, :]], axis=1)
        product = jnp.dot(inner_ref[...], inner, preferred_element_type=F32)
        product = (product + jnp.dot(outer_ref[...], outer, preferred_element_type=F32)) * factor
        half = COLS // 2
        for band in range(BANDS):
            for part in range(2):
                columns = slice(part * COLS, (part + 1) * COLS)
                first = product[band * COLS : band * COLS + half, columns]
                second = product[band * COLS + half : (band + 1) * COLS, columns]
                kept_ref[band, 2 * i + part] = jnp.where(odd, second, first).astype(BF16)
                sent_ref[band, 2 * i + part] = jnp.where(odd, first, second).astype(BF16)
        return 0

    lax.fori_loop(0, BANDS // 2, step, 0)


def project(states, mixed, position):
    count = lax.axis_size("space")
    halves = count // 2
    factor = 1.0 / (FACE * ((EDGE - 1) * count + 1))
    shape = jax.ShapeDtypeStruct((halves, BANDS, COLS // 2, COLS), BF16)
    kept, sent = pl.pallas_call(
        functools.partial(product_kernel, factor),
        name="products",
        out_shape=(shape, shape),
        in_specs=[VMEM] * 2 + [SMEM],
        out_specs=(VMEM,) * 2,
        scratch_shapes=[
            pltpu.VMEM((BANDS * COLS, INNER_BLOCK), BF16),
            pltpu.VMEM((BANDS * COLS, OUTER_BLOCK), BF16),
        ],
        compiler_params=BIG,
    )(states, mixed, position)
    got = lax.ppermute(sent, "space", [(i, i ^ 1) for i in range(count)])
    both = (kept.astype(F32) + got.astype(F32)).astype(BF16).reshape(halves * BANDS, COLS // 2, COLS)
    groups = [[(2 * half + part) * BANDS + band for half in range(halves) for band in range(BANDS)] for part in range(2)]
    arrived = lax.all_to_all(both, ("space", "band"), split_axis=0, concat_axis=0, tiled=True, axis_index_groups=groups)
    return arrived.astype(F32).sum(axis=0).T


def swap_faces(near, far):
    count = lax.axis_size("space")
    apart = [(i, i + 1) for i in range(1, count - 1, 2)]
    beside = [(i, i + 1) for i in range(0, count, 2)]
    both_ways = lambda pairs: pairs + [(j, i) for i, j in pairs]
    near, far = lax.optimization_barrier((near, far))
    from_far = lax.ppermute(far, "space", both_ways(apart))
    from_near = lax.ppermute(near, "space", both_ways(beside))
    return from_near, from_far


def local(states, potential, cell_matrix, cell_scale, connectivity, lower_bound, upper_bound):
    bounds = (lower_bound, upper_bound)
    position = lax.axis_index("space").astype(jnp.int32).reshape(1)
    field, pot, mat, full, inner, outer = gather(states, potential, connectivity, cell_matrix, bounds)
    near, far = first_faces(field, full, cell_scale, position)
    prev = settled = None
    for stage in range(1, STEPS):
        got = swap_faces(near, far)
        part, sums, rim, *patched = cells(stage, field, prev, settled, pot, mat, inner, bounds, cell_scale)
        prev, field = (patched or [field])[0], part
        settled, _, near, far = faces(stage, rim, got, bounds, position, outer, cell_scale, sums)
    got = swap_faces(near, far)
    _, sums, rim, early, _ = cells(STEPS, field, prev, settled, pot, mat, inner, bounds, cell_scale)
    got, early = lax.optimization_barrier((got, early))
    node_states = lax.all_to_all(
        early.reshape(BANDS, INNER_BLOCK, COLS), "band", split_axis=0, concat_axis=0, tiled=True)
    settled, edge, _, near, far = faces(STEPS, rim, got, bounds, position, outer, cell_scale, sums)
    got = swap_faces(near, far)
    rim, current, blocks = last_cells(early, settled, edge, pot, mat, bounds, cell_scale)
    blocks, = faces(STEPS + 1, rim, got, bounds, position, blocks=blocks)
    blocks, current = lax.optimization_barrier((blocks, current))
    filtered = hand_back(current, connectivity)
    mixed = lax.all_to_all(blocks.reshape(BANDS, BLOCK, COLS), "band", split_axis=0, concat_axis=0, tiled=True)
    totals = project(node_states, mixed, position)
    return filtered, totals


def solution(mesh):
    placed = (P("space", "band"), P("space"), P(), P("space"), P("space", None), P(), P())
    return jax.shard_map(
        local,
        mesh=mesh,
        in_specs=placed,
        out_specs=(P("space", "band"), P("band", "space")),
        check_vma=False,
    )
```

```python
import functools

import jax
import jax.numpy as jnp
from jax import lax
from jax.experimental import pallas as pl
from jax.experimental.pallas import tpu as pltpu
from jax.sharding import PartitionSpec as P


EDGE = 8
SLAB_XY = 5
STEPS = 4
CELLS = SLAB_XY * SLAB_XY
PAIRS = (CELLS + 1) // 2
CELL_NODES = EDGE**3
SIDE = (EDGE - 1) * SLAB_XY + 1
FACE = SIDE * SIDE
NODES = FACE * EDGE
COLS = 128
SLABS = 16
GROUP = 144
BANDS = 8
INNER = (EDGE - 2) * FACE
INNER_BLOCK = 976
OUTER = FACE + FACE // 2
OUTER_BLOCK = 256
BLOCK = INNER_BLOCK + 2 * OUTER_BLOCK
GATHER_PARTS = ((0, CELLS),)
QUAD = EDGE * EDGE
THIRDS = 3
THIRD = FACE // THIRDS
F32 = jnp.float32
BF16 = jnp.bfloat16
VMEM = pl.BlockSpec(memory_space=pltpu.VMEM)
SMEM = pl.BlockSpec(memory_space=pltpu.SMEM)
HBM = pl.BlockSpec(memory_space=pltpu.HBM)
BIG = pltpu.CompilerParams(vmem_limit_bytes=24 * 1024 * 1024)
SMALL = pltpu.CompilerParams(vmem_limit_bytes=8 * 1024 * 1024)


def first_row(cell_y, cell_x, j):
    return (((EDGE - 1) * cell_y + j) * SIDE + (EDGE - 1) * cell_x) * EDGE


def gather_kernel(states_hbm, pot_ref, index_hbm, matrix_hbm, low_ref, high_ref, field_ref, pot_out_ref, mat_ref,
                  full_ref, inner_ref, outer_ref, rhs_ref, hot_ref, column_ref, states_ref, index_ref, matrix_ref, sems):
    index_copy = pltpu.make_async_copy(index_hbm, index_ref, sems.at[0])
    matrix_copy = pltpu.make_async_copy(matrix_hbm, matrix_ref, sems.at[1])
    states_copy = pltpu.make_async_copy(states_hbm, states_ref, sems.at[2])
    index_copy.start()
    matrix_copy.start()
    states_copy.start()
    index_copy.wait()
    for cell_y in range(SLAB_XY):
        five = index_ref[cell_y * SLAB_XY : (cell_y + 1) * SLAB_XY, :].astype(F32)
        five = jnp.concatenate([five, jnp.zeros((EDGE - SLAB_XY, CELL_NODES), F32)], axis=0)
        column_ref[cell_y * CELL_NODES : (cell_y + 1) * CELL_NODES, :EDGE] = jnp.transpose(five)
    pot = jnp.transpose(pot_ref[...])
    high = pot.astype(BF16)
    rest = pot - high.astype(F32)
    mid = rest.astype(BF16)
    low = (rest - mid.astype(F32)).astype(BF16)
    rhs_ref[:, COLS:] = jnp.concatenate(
        [high, mid, low, jnp.zeros((FACE, COLS - 3 * EDGE), BF16)], axis=1)

    matrix_copy.wait()
    new = lax.broadcasted_iota(jnp.int32, (CELL_NODES, CELL_NODES), 0)
    old = lax.broadcasted_iota(jnp.int32, (CELL_NODES, CELL_NODES), 1)
    order = jnp.where(old == (new % EDGE) * QUAD + new // EDGE, 1.0, 0.0).astype(BF16)
    across = (((1,), (1,)), ((), ()))
    turned = lax.dot_general(matrix_ref[...], order, across, preferred_element_type=F32).astype(BF16)
    mat_ref[...] = jnp.dot(order, turned, preferred_element_type=F32).astype(BF16)
    for side, first in enumerate((0, CELL_NODES - QUAD)):
        rows = pl.ds(side * QUAD, QUAD)
        face_rows = turned[first : first + QUAD, :].astype(F32)
        z = lax.broadcasted_iota(jnp.int32, (QUAD, CELL_NODES), 1) % EDGE
        full_ref[rows, :] = face_rows.astype(BF16)
        inner_ref[rows, :] = jnp.where((z > 0) & (z < EDGE - 1), face_rows, 0.0).astype(BF16)
        outer_ref[rows, :QUAD] = matrix_ref[first : first + QUAD, :QUAD]
        outer_ref[rows, QUAD:] = matrix_ref[first : first + QUAD, CELL_NODES - QUAD :]
    lead, shift = factors((low_ref, high_ref), 2)
    states_copy.wait()

    def step(plane, _):
        rhs_ref[:, :COLS] = states_ref[pl.ds(pl.multiple_of(plane * FACE, 16), FACE), :]
        start = (plane * FACE).astype(F32)
        lane = lax.broadcasted_iota(jnp.int32, (EDGE, COLS), 1)
        mine = (lane % EDGE == plane) & (lane < 3 * EDGE)
        for first, last in GATHER_PARTS:
            at = 0
            for cell in range(first, last):
                cell_y, cell_x = cell // SLAB_XY, cell % SLAB_XY
                rows = QUAD if cell_y == SLAB_XY - 1 else QUAD - EDGE
                lanes = lax.broadcasted_iota(jnp.int32, (rows, FACE), 1).astype(F32)
                want = column_ref[pl.ds(pl.multiple_of(cell_y * CELL_NODES + plane * QUAD, 8), rows), cell_x : cell_x + 1] - start
                hot_ref[at : at + rows, :] = jnp.where(want == lanes, 1.0, 0.0).astype(BF16)
                at += rows
            got = jnp.dot(hot_ref[:at, :], rhs_ref[...], preferred_element_type=F32)
            at = 0
            for cell in range(first, last):
                cell_y, cell_x = cell // SLAB_XY, cell % SLAB_XY
                for j in range(EDGE if cell_y == SLAB_XY - 1 else EDGE - 1):
                    rows = pl.ds(first_row(cell_y, cell_x, j) + plane, EDGE, stride=EDGE)
                    field_ref[rows, :] = got[at : at + EDGE, :COLS]
                    value = jnp.sum(jnp.where(mine, got[at : at + EDGE, COLS:], 0.0), axis=1, keepdims=True)
                    pot_out_ref[rows, :] = lead * value - shift
                    at += EDGE
        return 0

    lax.fori_loop(0, EDGE, step, 0)


def in_hbm(x):
    return pltpu.with_memory_space_constraint(x, pltpu.HBM)


def gather(states, potential, connectivity, matrix, bounds):
    return pl.pallas_call(
        gather_kernel,
        name="gather_states",
        out_shape=(
            pltpu.VMEM((NODES, COLS), F32),
            pltpu.VMEM((NODES, COLS), F32),
            pltpu.VMEM((CELL_NODES, CELL_NODES), BF16),
            pltpu.VMEM((2 * QUAD, CELL_NODES), BF16),
            pltpu.VMEM((2 * QUAD, CELL_NODES), BF16),
            pltpu.VMEM((2 * QUAD, 2 * QUAD), BF16),
        ),
        in_specs=[HBM, VMEM, HBM, HBM] + [SMEM] * 2,
        out_specs=(VMEM,) * 6,
        scratch_shapes=[
            pltpu.VMEM((FACE, 2 * COLS), BF16),
            pltpu.VMEM((CELLS * QUAD, FACE), BF16),
            pltpu.VMEM((SLAB_XY * CELL_NODES, COLS), F32),
            pltpu.VMEM((NODES, COLS), BF16),
            pltpu.VMEM((CELLS, CELL_NODES), jnp.int32),
            pltpu.VMEM((CELL_NODES, CELL_NODES), BF16),
            pltpu.SemaphoreType.DMA((3,)),
        ],
        compiler_params=BIG,
    )(in_hbm(states), potential.reshape(EDGE, FACE), in_hbm(connectivity), in_hbm(matrix), *bounds)


def half_width_of(bounds):
    low, high = bounds
    return jnp.full((1, COLS), (high[0] - low[0]) * 0.5, F32)


def factors(bounds, stage):
    if stage > STEPS:
        return jnp.ones((1, COLS), F32), None
    low, high = bounds
    center = (high[0] + low[0]) * 0.5
    lead = (1.0 if stage == 1 else 2.0) / half_width_of(bounds)
    return lead, lead * center


def pair_cells(pair, scale_ref):
    for half in range(2):
        index = 2 * pair + half
        cell = jnp.minimum(index, CELLS - 1)
        yield half, cell // SLAB_XY, cell % SLAB_XY, jnp.where(index < CELLS, scale_ref[cell], 0.0)


def for_pairs(work, group):
    def step(i, _):
        work(*[group * i + k for k in range(group)])
        return 0

    lax.fori_loop(0, PAIRS // group, step, 0)
    if PAIRS % group:
        work(*[jnp.int32(pair) for pair in range(PAIRS - PAIRS % group, PAIRS)])


def cell_blocks(field_ref, pair, scale_ref):
    columns = []
    for half, cell_y, cell_x, _ in pair_cells(pair, scale_ref):
        pieces = []
        for j in range(EDGE):
            rows = pl.ds(pl.multiple_of(first_row(cell_y, cell_x, j), EDGE), QUAD)
            pieces.append(field_ref[rows, :].astype(BF16))
        columns.append(jnp.concatenate(pieces, axis=0))
    return jnp.concatenate(columns, axis=1)


def add_faces(sums_ref, product, pair, scale_ref):
    for half, cell_y, cell_x, scale in pair_cells(pair, scale_ref):
        fresh = []
        for side in range(2):
            for j in range(EDGE):
                at = side * QUAD + j * EDGE
                rows = pl.ds(side * FACE + ((EDGE - 1) * cell_y + j) * SIDE + (EDGE - 1) * cell_x, EDGE)
                value = scale * product[at : at + EDGE, half * COLS : (half + 1) * COLS]
                fresh.append((rows, sums_ref[rows, :] + value))
        for rows, value in fresh:
            sums_ref[rows, :] = value


def spread_faces(field_ref, matrix_ref, scale_ref, sums_ref):
    sums_ref[...] = jnp.zeros_like(sums_ref)

    def spread(*pairs):
        blocks = [cell_blocks(field_ref, pair, scale_ref) for pair in pairs]
        products = [jnp.dot(matrix_ref[...], block, preferred_element_type=F32) for block in blocks]
        for pair, product in zip(pairs, products):
            add_faces(sums_ref, product, pair, scale_ref)

    for_pairs(spread, 3)


def hand_out(sums_ref, odd, near_out, far_out):
    near_out[...] = sums_ref[pl.ds(pl.multiple_of((1 - odd) * FACE, 16), FACE), :].astype(BF16)
    far_out[...] = sums_ref[pl.ds(pl.multiple_of(odd * FACE, 16), FACE), :].astype(BF16)


def first_faces_kernel(field_ref, full_ref, scale_ref, position_ref, near_out, far_out, sums_ref):
    spread_faces(field_ref, full_ref, scale_ref, sums_ref)
    hand_out(sums_ref, position_ref[0] % 2, near_out, far_out)


def first_faces(field, full, scale, position):
    return pl.pallas_call(
        first_faces_kernel,
        name="first_faces",
        out_shape=(jax.ShapeDtypeStruct((FACE, COLS), BF16),) * 2,
        in_specs=[VMEM] * 2 + [SMEM] * 2,
        out_specs=(VMEM,) * 2,
        scratch_shapes=[pltpu.VMEM((2 * FACE, COLS), F32)],
        compiler_params=SMALL,
    )(field, full, scale, position)


def put_inner(field_ref, store):
    def planes(i, _):
        for z in range(1, EDGE - 1):
            for part in range(3):
                node = i * 48 + part * 16
                halves = [field_ref[pl.ds((node + k) * EDGE + z, EDGE, stride=EDGE), :] for k in (0, EDGE)]
                store((z - 1) * FACE + node, jnp.concatenate(halves, axis=0).astype(BF16))
        return 0

    lax.fori_loop(0, FACE // 48, planes, 0)
    for row in range(INNER, BANDS * INNER_BLOCK, 16):
        store(row, jnp.zeros((16, COLS), BF16))


def put_outer(face_ref, odd, far_weight, store):
    def rows(i, _):
        ready = []
        for part in range(8):
            row = (i * 8 + part) * 16
            far = row < FACE
            near_at = (1 - odd) * FACE + odd * (FACE // 2) + row - FACE
            at = jnp.where(far, odd * FACE + row, jnp.minimum(near_at, 2 * FACE - 16))
            value = face_ref[pl.ds(pl.multiple_of(at, EDGE), 16), :]
            if far_weight is not None:
                value = value * jnp.where(far, far_weight, 1.0)
            index = lax.broadcasted_iota(jnp.int32, (16, COLS), 0) + row
            ready.append((row, jnp.where(index < OUTER, value, 0.0).astype(BF16)))
        for row, value in ready:
            store(row, value)
        return 0

    lax.fori_loop(0, BANDS * OUTER_BLOCK // 128, rows, 0)


def faces_kernel(stage, *refs):
    late, spread = stage >= STEPS, stage <= STEPS
    refs = list(refs)
    rim_ref, near_in, far_in, low_ref, high_ref, position_ref = refs[:6]
    refs = refs[6:]
    if spread:
        outer_ref, scale_ref, _ = refs[:3]
        refs = refs[3:]
        face_ref = refs.pop(0)
        if late:
            edge_ref = refs.pop(0)
        sums_ref, near_out, far_out = refs
    else:
        _, block_ref, face_ref, edge_ref, sems = refs
    odd = position_ref[0] % 2
    lead, _ = factors((low_ref, high_ref), stage)

    def settle_rows(i, _):
        here = pl.ds(pl.multiple_of(i * GROUP, 16), GROUP)
        settled = []
        for face_in, side in ((near_in, 1 - odd), (far_in, odd)):
            rows = pl.ds(pl.multiple_of(side * FACE + i * GROUP, 16), GROUP)
            settled.append((rows, (rim_ref[rows, :] + lead * face_in[here, :].astype(F32)).astype(BF16).astype(F32)))
        for rows, value in settled:
            face_ref[rows, :] = value
        return 0

    lax.fori_loop(0, FACE // GROUP, settle_rows, 0)
    if spread:

        def face_blocks(pair):
            columns = []
            for half, cell_y, cell_x, _ in pair_cells(pair, scale_ref):
                pieces = []
                for side in range(2):
                    for j in range(EDGE):
                        rows = pl.ds(side * FACE + ((EDGE - 1) * cell_y + j) * SIDE + (EDGE - 1) * cell_x, EDGE)
                        pieces.append(face_ref[rows, :])
                columns.append(jnp.concatenate(pieces, axis=0).astype(BF16))
            return jnp.concatenate(columns, axis=1)

        def spread_outer(*pairs):
            blocks = [face_blocks(pair) for pair in pairs]
            products = [jnp.dot(outer_ref[...], block, preferred_element_type=F32) for block in blocks]
            for pair, product in zip(pairs, products):
                add_faces(sums_ref, product, pair, scale_ref)

        for_pairs(spread_outer, 3)
        hand_out(sums_ref, odd, near_out, far_out)
    if late:
        ends = (position_ref[0] == 0) | (position_ref[0] == SLABS - 1)
        far_weight = jnp.where(ends, 1.0, 0.5)

        def put_edge(row, value):
            edge_ref[pl.ds(pl.multiple_of(row, 16), 16), :] = value

        put_outer(face_ref, odd, None if spread else far_weight, put_edge)
    if not spread:
        copies = [
            pltpu.make_async_copy(
                edge_ref.at[pl.ds(band * OUTER_BLOCK, OUTER_BLOCK), :],
                block_ref.at[pl.ds(band * BLOCK + OUTER_BLOCK + INNER_BLOCK, OUTER_BLOCK), :],
                sems.at[band],
            )
            for band in range(BANDS)
        ]
        for copy in copies:
            copy.start()
        for copy in copies:
            copy.wait()


def faces(stage, rim, got, bounds, position, outer=None, scale=None, sums=None, blocks=None):
    args = [rim, *got, *bounds, position]
    specs = [VMEM] * 3 + [SMEM] * 3
    faces_shape = (2 * FACE, COLS)
    scratch = []
    if stage < STEPS:
        outs = [pltpu.VMEM(faces_shape, F32), pltpu.VMEM(faces_shape, F32)]
        aliases = {0: 0, 8: 1}
    elif stage == STEPS:
        outs = [
            jax.ShapeDtypeStruct(faces_shape, F32),
            jax.ShapeDtypeStruct((BANDS * OUTER_BLOCK, COLS), BF16),
            jax.ShapeDtypeStruct(faces_shape, F32),
        ]
        aliases = {8: 2}
    else:
        args.append(in_hbm(blocks))
        outs = [pltpu.HBM((BANDS * BLOCK, COLS), BF16)]
        aliases = {6: 0}
        scratch = [
            pltpu.VMEM(faces_shape, F32),
            pltpu.VMEM((BANDS * OUTER_BLOCK, COLS), BF16),
            pltpu.SemaphoreType.DMA((BANDS,)),
        ]
    if stage <= STEPS:
        args += [outer, scale, sums]
        specs += [VMEM, SMEM, VMEM]
        outs += [jax.ShapeDtypeStruct((FACE, COLS), BF16)] * 2
    else:
        specs.append(HBM)
    return pl.pallas_call(
        functools.partial(faces_kernel, stage),
        name="faces",
        out_shape=tuple(outs),
        in_specs=specs,
        out_specs=((VMEM,) * len(outs)) if stage <= STEPS else (HBM,),
        scratch_shapes=scratch,
        input_output_aliases=aliases,
        compiler_params=SMALL if stage < STEPS else BIG,
    )(*args)


def rebuild(inner_ref, settled_ref, field_ref):
    def nodes(i, _):
        for part in range(3):
            node = i * 48 + part * 16
            for z in range(EDGE):
                for k in (0, EDGE):
                    if z in (0, EDGE - 1):
                        at = pl.ds(pl.multiple_of((z // (EDGE - 1)) * FACE + node + k, EDGE), EDGE)
                        value = settled_ref[at, :]
                    elif k == 0:
                        both = inner_ref[pl.ds(pl.multiple_of((z - 1) * FACE + node, 16), 16), :].astype(F32)
                        value = both[:EDGE]
                    else:
                        value = both[EDGE:]
                    field_ref[pl.ds((node + k) * EDGE + z, EDGE, stride=EDGE), :] = value
        return 0

    lax.fori_loop(0, FACE // 48, nodes, 0)


def cells_kernel(stage, *refs):
    refs = list(refs)
    last = stage > STEPS
    if last:
        (early_ref, settled_ref, edge_ref, pot_ref, mat_ref, low_ref, high_ref, scale_ref,
         rim_ref, plain_ref, block_ref, field_ref, out_ref) = refs
        for band in range(BANDS):
            block_ref[band * BLOCK : band * BLOCK + OUTER_BLOCK, :] = (
                edge_ref[band * OUTER_BLOCK : (band + 1) * OUTER_BLOCK, :])
        rebuild(early_ref, settled_ref, field_ref)
    else:
        if stage > 1:
            settled_ref = refs[2]
            refs = refs[3:]
        pot_ref, mat_ref, inner_ref, low_ref, high_ref, scale_ref, out_ref, sums_ref, rim_ref, *more = (
            refs if stage > 1 else refs[1:])
        if stage == STEPS:
            early_ref = more.pop(0)
        field_ref = more[0] if stage > 1 else refs[0]
        if stage > 1:

            def put_settled(i, _):
                for side in range(2):
                    for part in range(GROUP // EDGE):
                        node = i * GROUP + part * EDGE
                        rows = pl.ds(node * EDGE + side * (EDGE - 1), EDGE, stride=EDGE)
                        field_ref[rows, :] = settled_ref[pl.ds(pl.multiple_of(side * FACE + node, EDGE), EDGE), :]
                return 0

            lax.fori_loop(0, FACE // GROUP, put_settled, 0)
    in_place = 1 < stage <= STEPS
    bounds = (low_ref, high_ref)
    lead, _ = factors(bounds, stage)
    if in_place:
        lead = -lead
    else:
        out_ref[...] = jnp.zeros_like(out_ref)

    def multiply(*pairs):
        blocks = [cell_blocks(field_ref, pair, scale_ref) for pair in pairs]
        products = [jnp.dot(mat_ref[...], block, preferred_element_type=F32) for block in blocks]
        for pair, product in zip(pairs, products):
            for half, cell_y, cell_x, scale in pair_cells(pair, scale_ref):
                factor = lead * scale
                for j in range(EDGE):
                    rows = pl.ds(pl.multiple_of(first_row(cell_y, cell_x, j), EDGE), QUAD)
                    out_ref[rows, :] += factor * product[j * QUAD : (j + 1) * QUAD, half * COLS : (half + 1) * COLS]

    for_pairs(multiply, 4)
    plane = lax.broadcasted_iota(jnp.int32, (EDGE, COLS), 0)
    inside = (plane > 0) & (plane < EDGE - 1)
    half_width = half_width_of(bounds) * 0.5
    center = jnp.full((1, COLS), (high_ref[0] + low_ref[0]) * 0.5, F32)

    def finish(i, _):
        for part in range(GROUP // EDGE):
            rows = pl.ds(pl.multiple_of(i * GROUP + part * EDGE, EDGE), EDGE)
            shifted = pot_ref[rows, :]
            if stage == 1:
                shifted = shifted * 0.5
            elif last:
                shifted = shifted * half_width + center
            value = shifted * field_ref[rows, :]
            value = value - out_ref[rows, :] if in_place else value + out_ref[rows, :]
            out_ref[rows, :] = jnp.where(inside, value.astype(BF16).astype(F32), value)
        return 0

    lax.fori_loop(0, NODES // GROUP, finish, 0)

    def put(row, value):
        if last:
            at = (row // INNER_BLOCK) * BLOCK + OUTER_BLOCK + row % INNER_BLOCK
            block_ref[pl.ds(pl.multiple_of(at, 16), 16), :] = value
        else:
            early_ref[pl.ds(pl.multiple_of(row, 16), 16), :] = value

    def put_rim(i, _):
        for side in range(2):
            for part in range(GROUP // EDGE):
                node = i * GROUP + part * EDGE
                rows = pl.ds(node * EDGE + side * (EDGE - 1), EDGE, stride=EDGE)
                rim_ref[pl.ds(pl.multiple_of(side * FACE + node, EDGE), EDGE), :] = out_ref[rows, :]
        return 0

    if stage >= STEPS:
        put_inner(out_ref, put)
    lax.fori_loop(0, FACE // GROUP, put_rim, 0)
    if last:

        def emit_rows(i, _):
            rows = pl.ds(pl.multiple_of(i * 2 * GROUP, 2 * GROUP), 2 * GROUP)
            plain_ref[rows, :] = field_ref[rows, :].astype(BF16)
            return 0

        lax.fori_loop(0, NODES // (2 * GROUP), emit_rows, 0)
    else:
        spread_faces(out_ref, inner_ref, scale_ref, sums_ref)


def cells(stage, field, prev, settled, pot, mat, inner, bounds, scale):
    args = [field] + ([prev, settled] if stage > 1 else []) + [pot, mat, inner]
    faces_shape = (2 * FACE, COLS)
    kind = pltpu.VMEM if stage < STEPS else pltpu.HBM
    outs = [pltpu.VMEM((NODES, COLS), F32), kind(faces_shape, F32), kind(faces_shape, F32)]
    if stage == STEPS:
        outs.append(pltpu.HBM((BANDS * INNER_BLOCK, COLS), BF16))
    aliases = {}
    if stage > 1:
        aliases = {1: 0, 0: len(outs)}
        outs.append(pltpu.VMEM((NODES, COLS), F32))
    return pl.pallas_call(
        functools.partial(cells_kernel, stage),
        name="cells",
        out_shape=tuple(outs),
        in_specs=[VMEM] * len(args) + [SMEM] * 3,
        out_specs=(VMEM,) * len(outs),
        input_output_aliases=aliases,
        compiler_params=SMALL if stage < STEPS else BIG,
    )(*args, *bounds, scale)


def last_cells(early, settled, edge, pot, mat, bounds, scale):
    return pl.pallas_call(
        functools.partial(cells_kernel, STEPS + 1),
        name="last_cells",
        out_shape=(
            pltpu.VMEM((2 * FACE, COLS), F32),
            jax.ShapeDtypeStruct((NODES, COLS), BF16),
            jax.ShapeDtypeStruct((BANDS * BLOCK, COLS), BF16),
        ),
        in_specs=[VMEM] * 5 + [SMEM] * 3,
        out_specs=(VMEM,) * 3,
        scratch_shapes=[pltpu.VMEM((NODES, COLS), F32)] * 2,
        compiler_params=pltpu.CompilerParams(vmem_limit_bytes=32 * 1024 * 1024),
    )(early, settled, edge, pot, mat, *bounds, scale)


def return_kernel(plain_ref, index_ref, out_ref, hot_ref, rhs_ref, field_ref):
    field_ref[...] = plain_ref[...].astype(F32)
    j = lax.broadcasted_iota(jnp.int32, (EDGE, COLS), 0)

    def step(plane, _):
        for cell in range(CELLS):
            cell_y, cell_x = cell // SLAB_XY, cell % SLAB_XY
            for k in range(EDGE):
                at = cell * QUAD + k * EDGE
                value = field_ref[pl.ds(first_row(cell_y, cell_x, k) + plane, EDGE, stride=EDGE), :]
                if cell_y > 0 and k == 0:
                    value = jnp.zeros_like(value)
                elif cell_x > 0:
                    value = jnp.where(j == 0, 0.0, value)
                rhs_ref[at : at + EDGE, :] = value
        want = index_ref[pl.ds(plane, 1), :].astype(F32) - (plane * FACE).astype(F32)
        rhs = rhs_ref[...].astype(BF16)
        for part in range(THIRDS):
            row = lax.broadcasted_iota(jnp.int32, (THIRD, CELLS * QUAD), 0).astype(F32) + float(part * THIRD)
            hot_ref[...] = jnp.where(want == row, 1.0, 0.0).astype(BF16)
            got = jnp.dot(hot_ref[...], rhs, preferred_element_type=F32)
            start = pl.multiple_of(plane * FACE + part * THIRD, 16)
            out_ref[pl.ds(start, THIRD), :] = got.astype(BF16)
        return 0

    lax.fori_loop(0, EDGE, step, 0)


def hand_back(field, connectivity):
    index = connectivity.reshape(CELLS, EDGE, QUAD).transpose(1, 0, 2).reshape(EDGE, CELLS * QUAD)
    return pl.pallas_call(
        return_kernel,
        name="hand_back",
        out_shape=jax.ShapeDtypeStruct((NODES, COLS), BF16),
        in_specs=[VMEM] * 2,
        out_specs=VMEM,
        scratch_shapes=[
            pltpu.VMEM((THIRD, CELLS * QUAD), BF16),
            pltpu.VMEM((CELLS * QUAD, COLS), F32),
            pltpu.VMEM((NODES, COLS), F32),
        ],
        compiler_params=BIG,
    )(field, index)


def product_kernel(factor, states_ref, mixed_ref, position_ref, kept_ref, sent_ref, inner_ref, outer_ref):
    odd = position_ref[0] % 2 == 1
    for band in range(BANDS):
        rows = slice(band * COLS, (band + 1) * COLS)
        inner_ref[rows, :] = jnp.transpose(mixed_ref[band, OUTER_BLOCK : OUTER_BLOCK + INNER_BLOCK, :])
        outer_ref[rows, :] = jnp.transpose(mixed_ref[band, OUTER_BLOCK + INNER_BLOCK :, :])

    def step(i, _):
        inner = jnp.concatenate([states_ref[2 * i], states_ref[2 * i + 1]], axis=1)
        outer = jnp.concatenate([mixed_ref[2 * i, :OUTER_BLOCK, :], mixed_ref[2 * i + 1, :OUTER_BLOCK, :]], axis=1)
        product = jnp.dot(inner_ref[...], inner, preferred_element_type=F32)
        product = (product + jnp.dot(outer_ref[...], outer, preferred_element_type=F32)) * factor
        half = COLS // 2
        for band in range(BANDS):
            for part in range(2):
                columns = slice(part * COLS, (part + 1) * COLS)
                first = product[band * COLS : band * COLS + half, columns]
                second = product[band * COLS + half : (band + 1) * COLS, columns]
                kept_ref[band, 2 * i + part] = jnp.where(odd, second, first).astype(BF16)
                sent_ref[band, 2 * i + part] = jnp.where(odd, first, second).astype(BF16)
        return 0

    lax.fori_loop(0, BANDS // 2, step, 0)


def total_kernel(parts_ref, total_ref):
    for row in range(0, COLS // 2, 16):
        sums = [jnp.zeros((16, COLS), F32)] * 4
        for part in range(parts_ref.shape[0]):
            sums[part % 4] = sums[part % 4] + parts_ref[part, row : row + 16, :].astype(F32)
        total_ref[row : row + 16, :] = (sums[0] + sums[1]) + (sums[2] + sums[3])


def project(states, mixed, position):
    count = lax.axis_size("space")
    halves = count // 2
    factor = 1.0 / (FACE * ((EDGE - 1) * count + 1))
    shape = jax.ShapeDtypeStruct((halves, BANDS, COLS // 2, COLS), BF16)
    kept, sent = pl.pallas_call(
        functools.partial(product_kernel, factor),
        name="products",
        out_shape=(shape, shape),
        in_specs=[VMEM] * 2 + [SMEM],
        out_specs=(VMEM,) * 2,
        scratch_shapes=[
            pltpu.VMEM((BANDS * COLS, INNER_BLOCK), BF16),
            pltpu.VMEM((BANDS * COLS, OUTER_BLOCK), BF16),
        ],
        compiler_params=BIG,
    )(states, mixed, position)
    got = lax.ppermute(sent, "space", [(i, i ^ 1) for i in range(count)])
    both = (kept.astype(F32) + got.astype(F32)).astype(BF16).reshape(halves * BANDS, COLS // 2, COLS)
    groups = [[(2 * half + part) * BANDS + band for half in range(halves) for band in range(BANDS)] for part in range(2)]
    arrived = lax.all_to_all(both, ("space", "band"), split_axis=0, concat_axis=0, tiled=True, axis_index_groups=groups)
    return pl.pallas_call(
        total_kernel,
        name="total",
        out_shape=jax.ShapeDtypeStruct((COLS // 2, COLS), F32),
        in_specs=[VMEM],
        out_specs=VMEM,
        compiler_params=SMALL,
    )(arrived).T


def swap_faces(near, far):
    count = lax.axis_size("space")
    apart = [(i, i + 1) for i in range(1, count - 1, 2)]
    beside = [(i, i + 1) for i in range(0, count, 2)]
    both_ways = lambda pairs: pairs + [(j, i) for i, j in pairs]
    near, far = lax.optimization_barrier((near, far))
    from_far = lax.ppermute(far, "space", both_ways(apart))
    from_near = lax.ppermute(near, "space", both_ways(beside))
    return from_near, from_far


def local(states, potential, cell_matrix, cell_scale, connectivity, lower_bound, upper_bound):
    bounds = (lower_bound, upper_bound)
    position = lax.axis_index("space").astype(jnp.int32).reshape(1)
    field, pot, mat, full, inner, outer = gather(states, potential, connectivity, cell_matrix, bounds)
    near, far = first_faces(field, full, cell_scale, position)
    prev = settled = None
    for stage in range(1, STEPS):
        got = swap_faces(near, far)
        part, sums, rim, *patched = cells(stage, field, prev, settled, pot, mat, inner, bounds, cell_scale)
        prev, field = (patched or [field])[0], part
        settled, _, near, far = faces(stage, rim, got, bounds, position, outer, cell_scale, sums)
    got = swap_faces(near, far)
    _, sums, rim, early, _ = cells(STEPS, field, prev, settled, pot, mat, inner, bounds, cell_scale)
    got, early = lax.optimization_barrier((got, early))
    node_states = lax.all_to_all(
        early.reshape(BANDS, INNER_BLOCK, COLS), "band", split_axis=0, concat_axis=0, tiled=True)
    settled, edge, _, near, far = faces(STEPS, rim, got, bounds, position, outer, cell_scale, sums)
    got = swap_faces(near, far)
    rim, current, blocks = last_cells(early, settled, edge, pot, mat, bounds, cell_scale)
    blocks, = faces(STEPS + 1, rim, got, bounds, position, blocks=blocks)
    blocks, current = lax.optimization_barrier((blocks, current))
    filtered = hand_back(current, connectivity)
    mixed = lax.all_to_all(blocks.reshape(BANDS, BLOCK, COLS), "band", split_axis=0, concat_axis=0, tiled=True)
    totals = project(node_states, mixed, position)
    return filtered, totals


def solution(mesh):
    placed = (P("space", "band"), P("space"), P(), P("space"), P("space", None), P(), P())
    return jax.shard_map(
        local,
        mesh=mesh,
        in_specs=placed,
        out_specs=(P("space", "band"), P("band", "space")),
        check_vma=False,
    )
```
